32 devices in a mesh: dp: 8 (over y, x, core), seq: 4 (over z).
Axes of the slice: x: 2, y: 2, z: 4, core: 2. Of those that a mesh axis runs over, the one named last changes fastest.
Arguments:
- layer_input: bfloat16 [8, 1024, 1024], P('dp', 'seq'), may hold values from -6 to 6
- attn_gain: bfloat16 [1024], P('seq'), may hold values from 0.5 to 1.5
- attn_shift: bfloat16 [1024], P('seq'), may hold values from -0.59765625 to 0.59765625
- mlp_gain: bfloat16 [1024], P('seq'), may hold values from 0.5 to 1.5
- mlp_shift: bfloat16 [1024], P('seq'), may hold values from -0.59765625 to 0.59765625
- qkv_weight: bfloat16 [1024, 3072], P('seq'), may hold values from -0.1875 to 0.1875
- qkv_bias: bfloat16 [3072], P('seq'), may hold values from -0.29882812 to 0.29882812
- dense_weight: bfloat16 [1024, 1024], P('seq'), may hold values from -2 to 2
- dense_bias: bfloat16 [1024], P('seq'), may hold values from -0.59765625 to 0.59765625
- up_weight: bfloat16 [1024, 4096], P('seq'), may hold values from -0.1875 to 0.1875
- up_bias: bfloat16 [4096], P('seq'), may hold values from -0.59765625 to 0.59765625
- down_weight: bfloat16 [4096, 1024], P('seq'), may hold values from -0.125 to 0.125
- down_bias: bfloat16 [1024], P('seq'), may hold values from -0.59765625 to 0.59765625
- out_grad: bfloat16 [8, 1024, 1024], P('dp', 'seq'), may hold values from -6 to 6
Outputs:
- layer_output: bfloat16 [8, 1024, 1024], P('dp', 'seq')
- input_grad: bfloat16 [8, 1024, 1024], P('dp', 'seq')
- attn_gain_grad: float32 [1024], P('seq')
- attn_shift_grad: float32 [1024], P('seq')
- mlp_gain_grad: float32 [1024], P('seq')
- mlp_shift_grad: float32 [1024], P('seq')
- qkv_weight_grad: float32 [1024, 3072], P('seq')
- qkv_bias_grad: float32 [3072], P('seq')
- dense_weight_grad: float32 [1024, 1024], P('seq')
- dense_bias_grad: float32 [1024], P('seq')
- up_weight_grad: float32 [1024, 4096], P('seq')
- up_bias_grad: float32 [4096], P('seq')
- down_weight_grad: float32 [4096, 1024], P('seq')
- down_bias_grad: float32 [1024], P('seq')
The draws below stay inside these ranges and needn't reach their ends.
All inputs are finite; a program needn't handle non-finite values.
Results may differ from the reference program's by a relative error of at most 0.0076.
The reference program's roundings to bfloat16 on the way count: a program that leaves them out, or rounds other values in their place, can miss the bound.
Values may be sent and summed in bfloat16 or wider, within the bound.
A program may use at most 256 MiB of HBM per device.

```python
import jax
import jax.numpy as jnp
from jax import lax

D = 1024
HEADS = 16
HEAD_DIM = 64
FF = 4096
ROT_DIM = 16
SEQ_LEN = 1024
SEQS = 8


def spiked(array, rng, source, target, parts, factor):
    def block_of(dim):
        return (jnp.arange(array.shape[dim]) // (array.shape[dim] // parts)).reshape((-1,) + (1,) * (array.ndim - 1 - dim))

    first = jax.random.permutation(rng, parts)[block_of(target)]
    second = (block_of(target) + parts // 2) % parts
    return jnp.where((block_of(source) == first) | (block_of(source) == second), factor * array, array)


def level_of(stream_key, shape, split, least, top_value):
    def one(axis_at, shards_of):
        heights = jax.random.uniform(jax.random.fold_in(jax.random.fold_in(stream_key, 6), axis_at), (shards_of,), jnp.float32, least / len(split), top_value / len(split))
        return jnp.repeat(jnp.exp(heights), shape[axis_at] // shards_of).reshape((-1,) + (1,) * (len(shape) - axis_at - 1))

    factor_of = one(*split[0])
    for cut in split[1:]:
        factor_of = factor_of * one(*cut)
    return factor_of


def noise(rng, shape, deviation, reach, shards=(), kind=jnp.bfloat16):
    entries = deviation * jax.random.normal(rng, shape, jnp.float32)
    if shards:
        entries = entries * level_of(rng, shape, shards, -0.22, 0.18)
    return jnp.clip(entries, -reach, reach).astype(kind)


def noise_with(key, dims, scale, limit, cuts, heavy, kind=jnp.bfloat16):
    drawn = scale * jax.random.normal(key, dims, jnp.float32)
    if cuts:
        drawn = drawn * level_of(key, dims, cuts, -0.22, 0.18)
    return jnp.clip(spiked(drawn, jax.random.fold_in(key, 3), *heavy), -limit, limit).astype(kind)


def setup_inputs(seed: int = 0) -> dict:
    streams_of = jax.random.split(jax.random.key(seed), 15)
    layer_input = noise(streams_of[0], (SEQS, SEQ_LEN, D), 1.0, 6.0, ((0, 8), (1, 4)))
    attn_gain = jnp.clip(1.0 + 0.1 * jax.random.normal(streams_of[1], (D,), jnp.float32), 0.5, 1.5).astype(jnp.bfloat16)
    attn_shift = noise(streams_of[2], (D,), 0.1, 0.59765625, ((0, 4),))
    mlp_gain = jnp.clip(1.0 + 0.1 * jax.random.normal(streams_of[3], (D,), jnp.float32), 0.5, 1.5).astype(jnp.bfloat16)
    mlp_shift = noise(streams_of[4], (D,), 0.1, 0.59765625, ((0, 4),))
    qkv_weight = noise(streams_of[5], (D, 3 * D), D ** -0.5, 0.1875, ((0, 4),))
    qkv_bias = noise(streams_of[6], (3 * D,), 0.05, 0.29882812, ((0, 4),))
    dense_weight = noise(streams_of[7], (D, D), (max(D // 128, 1)) ** -0.5, 2.0, ((0, 4),))
    dense_bias = noise(streams_of[8], (D,), 0.1, 0.59765625, ((0, 4),))
    up_weight = noise(streams_of[9], (D, FF), D ** -0.5, 0.1875, ((0, 4),))
    up_bias = noise(streams_of[10], (FF,), 0.1, 0.59765625, ((0, 4),))
    down_weight = noise(streams_of[11], (FF, D), (FF // 2) ** -0.5, 0.125, ((0, 4),))
    down_bias = noise(streams_of[12], (D,), 0.1, 0.59765625, ((0, 4),))
    out_grad = noise_with(streams_of[13], (SEQS, SEQ_LEN, D), 1.0, 6.0, ((0, 8), (1, 4)), (0, 2, 8, 2.0))
    return dict(layer_input=layer_input, attn_gain=attn_gain, attn_shift=attn_shift, mlp_gain=mlp_gain, mlp_shift=mlp_shift, qkv_weight=qkv_weight, qkv_bias=qkv_bias, dense_weight=dense_weight, dense_bias=dense_bias, up_weight=up_weight, up_bias=up_bias, down_weight=down_weight, down_bias=down_bias, out_grad=out_grad)


@jax.custom_vjp
def low(v):
    return lax.optimization_barrier(v.astype(jnp.bfloat16)).astype(jnp.float32)

@jax.custom_vjp
def low_back(v):
    return v

def low_keep(v):
    return (low(v), None)

def low_pass(kept, grad):
    return (grad,)

def back_keep(v):
    return (v, None)

def back_low(kept, grad):
    return (low(grad),)
low.defvjp(low_keep, low_pass)
low_back.defvjp(back_keep, back_low)
epsilon = 1e-05
highest = lax.Precision.HIGHEST

def layer_norm(token_rows, gain, shift):
    average = lax.optimization_barrier(jnp.mean(token_rows, axis=-1, keepdims=True))
    centered = token_rows - average
    variance = lax.optimization_barrier(jnp.mean(centered * centered, axis=-1, keepdims=True))
    return centered * lax.rsqrt(variance + epsilon) * gain + shift

def rotate(packed, positions, sign):
    half = ROT_DIM // 2
    freqs = 10000.0 ** (-jnp.arange(half, dtype=jnp.float32) * 2.0 / ROT_DIM)
    angles = positions.astype(jnp.float32)[:, None] * freqs[None, :]
    cosine = jnp.cos(angles)[:, None, None, :]
    sine = jnp.sin(angles)[:, None, None, :] * sign
    first = packed[..., :half]
    second = packed[..., half:ROT_DIM]
    turned = jnp.concatenate([first * cosine - second * sine, second * cosine + first * sine, packed[..., ROT_DIM:]], axis=-1)
    select = (jnp.arange(3) < 2)[:, None]
    return jnp.where(select, turned, packed)

def forward(seq_input, params):
    gain_one, shift_one, gain_two, shift_two, w_qkv, b_qkv, w_dense, b_dense, w_up, b_up, w_down, b_down = params
    length = seq_input.shape[0]
    norm_one = low(layer_norm(seq_input, gain_one, shift_one))
    norm_two = low(layer_norm(seq_input, gain_two, shift_two))
    packed = low_back(jnp.dot(norm_one, w_qkv, precision=highest) + b_qkv)
    packed = packed.reshape(length, HEADS, 3, HEAD_DIM)
    packed = low_back(low(rotate(packed, jnp.arange(length, dtype=jnp.int32), 1.0)))
    query = packed[:, :, 0]
    keys = packed[:, :, 1]
    values = packed[:, :, 2]
    scores = jnp.einsum('qhd,khd->hqk', query, keys, precision=highest) * HEAD_DIM ** (-0.5)
    scores = low_back(scores)
    causal = jnp.arange(length)[:, None] >= jnp.arange(length)[None, :]
    scores = jnp.where(causal[None], scores, -1e+30)
    probs = jax.nn.softmax(scores, axis=-1)
    context = jnp.einsum('hqk,khd->qhd', low(probs), values, precision=highest)
    context = low_back(low(context)).reshape(length, HEADS * HEAD_DIM)
    attn_out = jnp.dot(context, w_dense, precision=highest) + b_dense
    hidden = low_back(jnp.dot(norm_two, w_up, precision=highest) + b_up)
    active = low(jax.nn.gelu(hidden, approximate=False))
    mlp_out = jnp.dot(active, w_down, precision=highest) + b_down
    return seq_input + attn_out + mlp_out

def reference(layer_input, attn_gain, attn_shift, mlp_gain, mlp_shift, qkv_weight, qkv_bias, dense_weight, dense_bias, up_weight, up_bias, down_weight, down_bias, out_grad):
    params = tuple((param.astype(jnp.float32) for param in (attn_gain, attn_shift, mlp_gain, mlp_shift, qkv_weight, qkv_bias, dense_weight, dense_bias, up_weight, up_bias, down_weight, down_bias)))

    def per_sequence(totals, pair):
        seq_input, seq_grad = pair
        result, pullback = jax.vjp(forward, seq_input.astype(jnp.float32), params)
        seq_input_grad, param_grads = pullback(seq_grad.astype(jnp.float32))
        totals = jax.tree.map(lambda left, right: left + right, totals, param_grads)
        return (totals, (result.astype(jnp.bfloat16), seq_input_grad.astype(jnp.bfloat16)))
    zeros = tuple((jnp.zeros_like(param) for param in params))
    totals, (outputs, input_grads) = lax.scan(per_sequence, zeros, (layer_input, out_grad))
    return (outputs, input_grads, totals[0], totals[1], totals[2], totals[3], totals[4], totals[5], totals[6], totals[7], totals[8], totals[9], totals[10], totals[11])
```

```python
import functools
import math

import jax
import jax.numpy as jnp
from jax import lax
from jax.experimental import pallas as pl
from jax.experimental.pallas import tpu as pltpu
from jax.sharding import PartitionSpec as P

HEADS = 16
HEAD_DIM = 64
ROT_DIM = 16
PLANE = 8
CHIPS = 4
epsilon = 1e-05
mask_fill = -1e30
MESH = pl.DeviceIdType.MESH
BF = jnp.bfloat16
F32 = jnp.float32


def rows_at(ref, start, count):
    return ref.at[pl.ds(pl.multiple_of(start, count), count)]


def block_at(ref, row, rows, col, cols):
    return ref.at[
        pl.ds(pl.multiple_of(row, rows), rows), pl.ds(pl.multiple_of(col, cols), cols)
    ]


class Place:
    def __init__(self, n, data):
        self.n, self.data = n, data
        self.d = lax.axis_index("dp")
        self.z = lax.axis_index("seq")
        self.base = self.d // PLANE * PLANE
        self.r = lax.rem(self.d, PLANE)
        self.ch = self.r // 2
        self.c = lax.rem(self.r, 2)
        self.piece = self.c * CHIPS + self.ch

    def seq_peer(self, k):
        other = lax.rem(self.z + k, self.n)
        return other, (self.d, other)

    def chip_peer(self, k):
        other = lax.rem(self.ch + k, CHIPS)
        return other, (self.base + other * 2 + self.c, self.z)

    def partner(self):
        return (self.base + self.ch * 2 + 1 - self.c, self.z)

    def dp_peer(self, k):
        other = lax.rem(self.d + k, self.data)
        return other, (other, self.z)

    def barrier(self):
        sem = pltpu.get_barrier_semaphore()
        for k in range(1, self.n):
            pl.semaphore_signal(sem, inc=1, device_id=self.seq_peer(k)[1], device_id_type=MESH)
        for k in range(1, self.data):
            pl.semaphore_signal(sem, inc=1, device_id=self.dp_peer(k)[1], device_id_type=MESH)
        pl.semaphore_wait(sem, self.n - 1 + self.data - 1)


def send(src, dst, ssem, rsem, to):
    return pltpu.make_async_remote_copy(
        src_ref=src, dst_ref=dst, send_sem=ssem, recv_sem=rsem, device_id=to, device_id_type=MESH
    )


class LineGather:
    def __init__(self, me, shard, full, rows, chunks, ssem, rsem):
        self.me, self.shard, self.full = me, shard, full
        self.rows, self.chunks, self.ssem, self.rsem = rows, chunks, ssem, rsem

    def part(self, owner, c):
        size = self.rows // self.chunks
        return rows_at(self.full, owner * self.rows + c * size, size)

    def copy(self, src, owner, c, way):
        me = self.me
        to = jnp.minimum(me.z + 1, me.n - 1) if way == 0 else jnp.maximum(me.z - 1, 0)
        return send(
            src,
            self.part(owner, c),
            self.ssem.at[way, owner, c],
            self.rsem.at[owner, c],
            (me.d, to),
        )

    def start(self):
        me = self.me
        size = self.rows // self.chunks
        for c in range(self.chunks):
            src = rows_at(self.shard, c * size, size)

            @pl.when(me.z < me.n - 1)
            def _():
                self.copy(src, me.z, c, 0).start()

            @pl.when(me.z > 0)
            def _():
                self.copy(src, me.z, c, 1).start()

    def step(self, s, c):
        me = self.me

        @pl.when(me.z >= s)
        def _():
            owner = me.z - s
            copy = self.copy(self.part(owner, c), owner, c, 0)
            copy.wait_recv()

            @pl.when(me.z < me.n - 1)
            def _():
                copy.start()

        @pl.when(me.z + s < me.n)
        def _():
            owner = me.z + s
            copy = self.copy(self.part(owner, c), owner, c, 1)
            copy.wait_recv()

            @pl.when(me.z > 0)
            def _():
                copy.start()

    def finish(self):
        me = self.me
        for c in range(self.chunks):
            for owner in range(me.n):

                @pl.when((me.z < me.n - 1) & (owner <= me.z))
                def _():
                    self.copy(self.part(owner, c), owner, c, 0).wait_send()

                @pl.when((me.z > 0) & (owner >= me.z))
                def _():
                    self.copy(self.part(owner, c), owner, c, 1).wait_send()


class ColumnGather:
    def __init__(self, me, shard, full, sems):
        self.me, self.shard, self.full = me, shard, full
        self.depth = shard.shape[0]
        self.rp = self.depth // PLANE
        self.cols = full.shape[1]
        self.zs, self.zr, self.ps, self.pr, self.fs = sems

    def part(self, src_z, piece):
        return rows_at(self.full, (src_z * PLANE + piece) * self.rp, self.rp)

    def across(self, k):
        me = self.me
        other, to = me.seq_peer(k)
        src = block_at(self.shard, me.piece * self.rp, self.rp, other * self.cols, self.cols)
        return send(src, self.part(me.z, me.piece), self.zs.at[k], self.zr.at[me.n - k], to)

    def came(self, k):
        me = self.me
        other, to = me.seq_peer(k)
        src = block_at(self.shard, me.piece * self.rp, self.rp, other * self.cols, self.cols)
        return send(src, self.part(other, me.piece), self.zs.at[k], self.zr.at[k], to)

    def shares(self, k):
        me = self.me
        other, unused = me.seq_peer(k)
        mine = self.part(other, me.piece)
        for j in range(1, CHIPS):
            to = me.chip_peer(j)[1]
            yield send(mine, mine, self.ps.at[k, j], self.pr.at[k, CHIPS - j], to)
        yield send(mine, mine, self.ps.at[k, 0], self.fs.at[1, k, 0], me.partner())

    def handed(self, k, j):
        me = self.me
        other, unused = me.seq_peer(k)
        chip = me.chip_peer(j)[0]
        return self.part(other, me.c * CHIPS + chip), self.part(other, (1 - me.c) * CHIPS + chip)

    def start(self):
        for k in range(self.me.n - 1, 0, -1):
            self.across(k).start()

    def share(self, k):
        self.came(k).wait_recv()
        for copy in self.shares(k):
            copy.start()

    def hand(self, k):
        me = self.me
        for j in range(1, CHIPS):
            got, unused = self.handed(k, j)
            send(got, got, self.ps.at[k, j], self.pr.at[k, j], me.chip_peer(j)[1]).wait_recv()
            send(got, got, self.fs.at[0, k, j], self.fs.at[1, k, j], me.partner()).start()

    def finish(self):
        me = self.me
        for k in range(1, me.n):
            self.across(k).wait_send()
            for copy in self.shares(k):
                copy.wait_send()
            other, unused = me.seq_peer(k)
            for j in range(CHIPS):
                unused, got = self.handed(k, j)
                copy = send(got, got, self.fs.at[0, k, j], self.fs.at[1, k, j], me.partner())
                copy.wait_recv()
                if j > 0:
                    copy.wait_send()


def column_sems(n):
    dma = pltpu.SemaphoreType.DMA
    return [dma((n,)), dma((n,)), dma((n, CHIPS)), dma((n, CHIPS)), dma((2, n, CHIPS))]


def gather_kernel(n, data, chunks, sm, x, g, wq, wu, SM, X, G, WQ, WU, *sems):
    me = Place(n, data)
    rows = x.shape[0]
    lsem, ss, sr, xs, xr, gs, gr = sems[:7]
    me.barrier()
    cq, cu = ColumnGather(me, wq, WQ, sems[7:12]), ColumnGather(me, wu, WU, sems[12:17])
    lx = LineGather(me, x, X, rows, chunks, xs, xr)
    lg = LineGather(me, g, G, rows, chunks, gs, gr)
    depth = wq.shape[0]
    own = [
        pltpu.make_async_copy(sm, SM.at[me.z], lsem.at[0]),
        pltpu.make_async_copy(x, rows_at(X, me.z * rows, rows), lsem.at[1]),
        pltpu.make_async_copy(g, rows_at(G, me.z * rows, rows), lsem.at[2]),
        pltpu.make_async_copy(
            block_at(wq, 0, depth, me.z * WQ.shape[1], WQ.shape[1]),
            rows_at(WQ, me.z * depth, depth),
            lsem.at[3],
        ),
        pltpu.make_async_copy(
            block_at(wu, 0, depth, me.z * WU.shape[1], WU.shape[1]),
            rows_at(WU, me.z * depth, depth),
            lsem.at[4],
        ),
    ]
    for copy in own:
        copy.start()

    def small(k, slot):
        return send(sm, SM.at[slot], ss.at[k], sr.at[slot], me.seq_peer(k)[1])

    for k in range(1, n):
        small(k, me.z).start()
    cq.start()
    cu.start()
    lx.start()
    lg.start()
    near = sorted({1, n - 1})
    for k in near:
        cq.share(k)
        cu.share(k)
    for c in range(chunks):
        lx.step(1, c)
    for k in range(1, n):
        if k not in near:
            cq.share(k)
            cu.share(k)
    for s in range(2, n):
        for c in range(chunks):
            lx.step(s, c)
    for k in range(1, n):
        cq.hand(k)
        cu.hand(k)
    for s in range(1, n):
        for c in range(chunks):
            lg.step(s, c)
    for k in range(1, n):
        small(k, me.z).wait_send()
        small(k, me.seq_peer(k)[0]).wait_recv()
    cq.finish()
    cu.finish()
    lx.finish()
    lg.finish()
    for copy in own:
        copy.wait()


def gather(n, data, sm, x, g, wq, wu):
    rows, width = x.shape
    depth = wq.shape[0]
    chunks = 4
    vm = pl.BlockSpec(memory_space=pltpu.VMEM)
    dma = pltpu.SemaphoreType.DMA
    sds = jax.ShapeDtypeStruct
    return pl.pallas_call(
        functools.partial(gather_kernel, n, data, chunks),
        out_shape=[
            sds((n,) + sm.shape, sm.dtype),
            sds((n * rows, width), x.dtype),
            sds((n * rows, width), x.dtype),
            sds((n * depth, wq.shape[1] // n), wq.dtype),
            sds((n * depth, wu.shape[1] // n), wu.dtype),
        ],
        in_specs=[vm] * 5,
        out_specs=[vm] * 5,
        scratch_shapes=[
            dma((5,)),
            dma((n,)),
            dma((n,)),
            dma((2, n, chunks)),
            dma((n, chunks)),
            dma((2, n, chunks)),
            dma((n, chunks)),
        ]
        + column_sems(n)
        + column_sems(n),
        compiler_params=pltpu.CompilerParams(
            collective_id=0, has_side_effects=True, vmem_limit_bytes=60 << 20
        ),
        name="gather",
    )(sm, x, g, wq, wu)


class RowReduce:
    def __init__(self, me, part, got, ssem, rsem):
        self.me, self.part, self.got, self.ssem, self.rsem = me, part, got, ssem, rsem
        self.rows = got.shape[1]

    def copy(self, k, slot):
        other, to = self.me.seq_peer(k)
        return send(
            rows_at(self.part, other * self.rows, self.rows),
            self.got.at[slot],
            self.ssem.at[k],
            self.rsem.at[slot],
            to,
        )

    def start(self):
        for k in range(1, self.me.n):
            self.copy(k, self.me.z).start()

    def wait(self):
        for k in range(1, self.me.n):
            self.copy(k, self.me.seq_peer(k)[0]).wait_recv()

    def finish(self):
        for k in range(1, self.me.n):
            self.copy(k, self.me.z).wait_send()


class GradReduce:
    def __init__(self, me, part, half, mine, chips, total, groups, sems):
        self.me, self.part, self.half, self.mine = me, part, half, mine
        self.chips, self.total, self.groups = chips, total, groups
        self.hs, self.hr, self.cs, self.cr, self.gs, self.gr = sems

    def swap(self):
        me = self.me
        return send(
            self.part.at[:, pl.ds((1 - me.c) * CHIPS, CHIPS)],
            self.half,
            self.hs,
            self.hr,
            me.partner(),
        )

    def to_chip(self, k, slot):
        other, to = self.me.chip_peer(k)
        return send(
            self.mine.at[:, other], self.chips.at[slot], self.cs.at[k], self.cr.at[slot], to
        )

    def start(self):
        self.swap().start()

    def chip_sums(self):
        me = self.me
        self.swap().wait_recv()
        for j in range(CHIPS):
            self.mine[:, j] = (
                self.part[:, me.c * CHIPS + j].astype(F32) + self.half[:, j].astype(F32)
            ).astype(BF)
        for k in range(1, CHIPS):
            self.to_chip(k, me.ch).start()

    def to_group(self, k, slot):
        me = self.me
        count = me.data // PLANE
        other = lax.rem(me.d // PLANE + k, count)
        return send(
            self.total,
            self.groups.at[slot],
            self.gs.at[k],
            self.gr.at[slot],
            (other * PLANE + me.r, me.z),
        )

    def sum_up(self):
        me = self.me
        for k in range(1, CHIPS):
            self.to_chip(k, me.chip_peer(k)[0]).wait_recv()
        total = self.mine[:, me.ch].astype(F32)
        for k in range(1, CHIPS):
            total = total + self.chips[me.chip_peer(k)[0]].astype(F32)
        self.total[...] = total.astype(BF)
        count = me.data // PLANE
        if count > 1:
            own = me.d // PLANE
            for k in range(1, count):
                self.to_group(k, own).start()
            for k in range(1, count):
                self.to_group(k, lax.rem(own + k, count)).wait_recv()
                self.to_group(k, own).wait_send()
            self.groups[own] = self.total[...]
            total = self.groups[0].astype(F32)
            for e in range(1, count):
                total = total + self.groups[e].astype(F32)
            self.total[...] = total.astype(BF)

    def finish(self):
        self.swap().wait_send()
        for k in range(1, CHIPS):
            self.to_chip(k, self.me.ch).wait_send()


class GradShare:
    def __init__(self, me, final, sems):
        self.me, self.final = me, final
        self.ss, self.sr, self.fs, self.fr = sems

    def copies(self):
        me = self.me
        mine = self.final.at[me.piece]
        for k in range(1, CHIPS):
            yield send(mine, mine, self.ss.at[k], self.sr.at[me.ch], me.chip_peer(k)[1])
        yield send(mine, mine, self.ss.at[0], self.fr.at[0], me.partner())

    def start(self):
        for copy in self.copies():
            copy.start()

    def handed(self, k):
        me = self.me
        got = self.final.at[me.c * CHIPS + me.chip_peer(k)[0]]
        return send(got, got, self.fs.at[k], self.fr.at[k], me.partner())

    def hand(self):
        me = self.me
        for k in range(1, CHIPS):
            chip, to = me.chip_peer(k)
            got = self.final.at[me.c * CHIPS + chip]
            send(got, got, self.ss.at[k], self.sr.at[chip], to).wait_recv()
            self.handed(k).start()

    def finish(self):
        me = self.me
        for copy in self.copies():
            copy.wait_send()
        for k in range(CHIPS):
            got = self.final.at[(1 - me.c) * CHIPS + me.chip_peer(k)[0]]
            copy = send(got, got, self.fs.at[k], self.fr.at[k], me.partner())
            copy.wait_recv()
            if k > 0:
                copy.wait_send()


class RowsBack:
    def __init__(self, me, total, final, ssem, rsem, lsem):
        self.me, self.total, self.final = me, total, final
        self.ssem, self.rsem, self.lsem = ssem, rsem, lsem

    def place(self, src_z):
        cols = self.total.shape[2]
        return self.final.at[
            self.me.piece, :, pl.ds(pl.multiple_of(src_z * cols, cols), cols)
        ]

    def copy(self, k, slot):
        other, to = self.me.seq_peer(k)
        return send(
            self.total.at[other], self.place(slot), self.ssem.at[k], self.rsem.at[slot], to
        )

    def own(self):
        me = self.me
        return pltpu.make_async_copy(self.total.at[me.z], self.place(me.z), self.lsem)

    def start(self):
        for k in range(1, self.me.n):
            self.copy(k, self.me.z).start()
        self.own().start()

    def wait(self):
        me = self.me
        for k in range(1, me.n):
            self.copy(k, me.seq_peer(k)[0]).wait_recv()
        self.own().wait()

    def finish(self):
        for k in range(1, self.me.n):
            self.copy(k, self.me.z).wait_send()


def reduce_kernel(n, data, *refs):
    (OP, DX, v1, v2, bias, x, g, UG, QG, DnG, DeG) = refs[:11]
    out, dx, small, fu, fq, fdn, fde = refs[11:18]
    scratch = list(refs[18:])
    me = Place(n, data)

    def take(count):
        got = scratch[:count]
        del scratch[:count]
        return got

    og, xg, zs, zr, v1g, v1s, v1r, v2m, v2g, v2s, v2r = take(11)
    reduces = []
    for part in (DnG, DeG, UG, QG):
        bufs = take(5)
        reduces.append(GradReduce(me, part, *bufs, take(6)))
    red_dn, red_de, red_u, red_q = reduces
    shares = [GradShare(me, final, take(4)) for final in (fdn, fde, fu, fq)]
    back_u = RowsBack(me, red_u.total, fu, *take(3))
    back_q = RowsBack(me, red_q.total, fq, *take(3))
    (dsem,) = take(1)
    assert not scratch
    ro = RowReduce(me, OP, og, zs.at[0], zr.at[0])
    rx = RowReduce(me, DX, xg, zs.at[1], zr.at[1])
    me.barrier()
    cs = v1g.shape[2]

    def small_z(k, slot):
        other, to = me.seq_peer(k)
        return send(
            v1.at[:, pl.ds(pl.multiple_of(other * cs, cs), cs)],
            v1g.at[slot],
            v1s.at[k],
            v1r.at[slot],
            to,
        )

    def small_dp(k, slot):
        return send(v2m, v2g.at[slot], v2s.at[k], v2r.at[slot], me.dp_peer(k)[1])

    for k in range(1, n):
        small_z(k, me.z).start()
    for red in reduces:
        red.start()
    ro.start()
    rx.start()
    for red in reduces:
        red.chip_sums()
    for k in range(1, n):
        small_z(k, me.seq_peer(k)[0]).wait_recv()
    v1g[me.z] = v1[:, pl.ds(pl.multiple_of(me.z * cs, cs), cs)]
    total = v1g[0]
    for k in range(1, n):
        total = total + v1g[k]
    v2m[0:8] = total
    v2m[8:16] = v2[...]
    for k in range(1, data):
        small_dp(k, me.d).start()
    own = []
    for i, (red, final) in enumerate(((red_dn, fdn), (red_de, fde))):
        red.sum_up()
        copy = pltpu.make_async_copy(red.total.at[0], final.at[me.piece], dsem.at[i])
        copy.start()
        own.append(copy)
    red_u.sum_up()
    back_u.start()
    red_q.sum_up()
    back_q.start()
    for copy in own:
        copy.wait()
    shares[0].start()
    shares[1].start()
    back_u.wait()
    shares[2].start()
    back_q.wait()
    shares[3].start()
    for share in shares:
        share.hand()
    for k in range(1, data):
        small_dp(k, me.dp_peer(k)[0]).wait_recv()
    v2g[me.d] = v2m[...]

    def add(i, acc):
        return acc + v2g[i]

    small[...] = lax.fori_loop(1, data, add, v2g[0])
    rows = x.shape[0]
    for red, base, result, extra in ((ro, x, out, bias), (rx, g, dx, None)):
        red.wait()
        step = rows // 4

        @pl.loop(0, 4)
        def _(i):
            at = pl.ds(pl.multiple_of(i * step, step), step)
            mine = pl.ds(pl.multiple_of(me.z * rows + i * step, step), step)
            acc = base[at].astype(F32) + red.part[mine].astype(F32)
            for k in range(1, n):
                acc = acc + red.got[me.seq_peer(k)[0], at].astype(F32)
            if extra is not None:
                acc = acc + extra[...]
            result[at] = acc.astype(BF)

        red.finish()
    for k in range(1, n):
        small_z(k, me.z).wait_send()
    for k in range(1, data):
        small_dp(k, me.d).wait_send()
    for red in reduces:
        red.finish()
    for share in shares:
        share.finish()
    back_u.finish()
    back_q.finish()


def reduce_all(n, data, OP, DX, v1, v2, bias, x, g, UG, QG, DnG, DeG):
    vm = pl.BlockSpec(memory_space=pltpu.VMEM)
    dma = pltpu.SemaphoreType.DMA
    sds = jax.ShapeDtypeStruct
    rows, width = x.shape
    groups = data // PLANE
    parts = []
    for whole in (DnG, DeG):
        lead, cols = whole.shape
        parts.append(whole.reshape(1, PLANE, lead // PLANE, cols))
    for whole in (UG, QG):
        lead, cols = whole.shape
        parts.append(whole.reshape(n, PLANE, lead // n // PLANE, cols))
    dn, de, u, q = parts
    scratch = [
        pltpu.VMEM((n, rows, width), BF),
        pltpu.VMEM((n, rows, width), BF),
        dma((2, n)),
        dma((2, n)),
        pltpu.VMEM((n, 8, width // n), F32),
        dma((n,)),
        dma((n,)),
        pltpu.VMEM((16, width // n), F32),
        pltpu.VMEM((data, 16, width // n), F32),
        dma((data,)),
        dma((data,)),
    ]
    for part in (dn, de, u, q):
        m, unused, rp, cols = part.shape
        scratch += [
            pltpu.VMEM((m, CHIPS, rp, cols), BF),
            pltpu.VMEM((m, CHIPS, rp, cols), BF),
            pltpu.VMEM((CHIPS, m, rp, cols), BF),
            pltpu.VMEM((m, rp, cols), BF),
            pltpu.VMEM((groups, m, rp, cols) if groups > 1 else (1, 1, 16, 128), BF),
            dma,
            dma,
            dma((CHIPS,)),
            dma((CHIPS,)),
            dma((groups,)),
            dma((groups,)),
        ]
    for unused in range(4):
        scratch += [dma((CHIPS,))] * 4
    scratch += [dma((n,)), dma((n,)), dma] * 2
    scratch += [dma((2,))]
    outs = [
        sds((rows, width), BF),
        sds((rows, width), BF),
        sds((16, width // n), F32),
        sds((PLANE, u.shape[2], u.shape[3] * n), BF),
        sds((PLANE, q.shape[2], q.shape[3] * n), BF),
        sds((PLANE,) + dn.shape[2:], BF),
        sds((PLANE,) + de.shape[2:], BF),
    ]
    return pl.pallas_call(
        functools.partial(reduce_kernel, n, data),
        out_shape=outs,
        in_specs=[vm] * 11,
        out_specs=[vm] * 7,
        scratch_shapes=scratch,
        compiler_params=pltpu.CompilerParams(
            collective_id=1, has_side_effects=True, vmem_limit_bytes=63 << 20
        ),
        name="reduce",
    )(OP, DX, v1, v2, bias, x, g, u, q, dn, de)


def layer_norm_parts(token_rows):
    average = jnp.mean(token_rows, axis=-1, keepdims=True)
    centered = token_rows - average
    variance = jnp.mean(centered * centered, axis=-1, keepdims=True)
    inverse = lax.rsqrt(variance + epsilon)
    return centered * inverse, inverse


def rotate(packed, positions, sign):
    half = ROT_DIM // 2
    freqs = 10000.0 ** (-jnp.arange(half, dtype=F32) * 2.0 / ROT_DIM)
    angles = positions.astype(F32)[:, None] * freqs[None, :]
    cosine = jnp.cos(angles)[:, None, None, :]
    sine = jnp.sin(angles)[:, None, None, :] * sign
    first = packed[..., :half]
    second = packed[..., half:ROT_DIM]
    turned = jnp.concatenate(
        [first * cosine - second * sine, second * cosine + first * sine, packed[..., ROT_DIM:]],
        axis=-1,
    )
    select = (jnp.arange(3) < 2)[:, None]
    return jnp.where(select, turned, packed)


def middle(X, G, WQ, WU, w_dense, w_down, b_qkv, b_up, vectors):
    length, width = X.shape
    heads = WQ.shape[1] // (3 * HEAD_DIM)
    scale = HEAD_DIM ** (-0.5)
    gain_one, shift_one, gain_two, shift_two = (vectors[i] for i in range(4))
    xhat, inverse = layer_norm_parts(X.astype(F32))
    norm_one = (xhat * gain_one + shift_one).astype(BF)
    norm_two = (xhat * gain_two + shift_two).astype(BF)
    packed = jnp.dot(norm_one, WQ, preferred_element_type=F32) + b_qkv.astype(F32)
    positions = jnp.arange(length, dtype=jnp.int32)
    packed = rotate(packed.reshape(length, heads, 3, HEAD_DIM), positions, 1.0).astype(BF)
    query, keys, values = packed[:, :, 0], packed[:, :, 1], packed[:, :, 2]
    scores = jnp.einsum("qhd,khd->hqk", query, keys, preferred_element_type=F32) * scale
    allowed = positions[:, None] >= positions[None, :]
    probs = jax.nn.softmax(jnp.where(allowed, scores, mask_fill), axis=-1)
    low = probs.astype(BF)
    context = jnp.einsum("hqk,khd->qhd", low, values, preferred_element_type=F32)
    context = context.astype(BF).reshape(length, heads * HEAD_DIM)
    hidden = jnp.dot(norm_two, WU, preferred_element_type=F32) + b_up.astype(F32)
    active = jax.nn.gelu(hidden, approximate=False).astype(BF)
    out = jnp.dot(context, w_dense, preferred_element_type=F32) + jnp.dot(
        active, w_down, preferred_element_type=F32
    )
    down_grad = jnp.einsum("tf,to->fo", active, G, preferred_element_type=F32)
    dense_grad = jnp.einsum("ti,to->io", context, G, preferred_element_type=F32)
    active_grad = jnp.einsum("to,fo->tf", G, w_down, preferred_element_type=F32)
    unused, pull = jax.vjp(lambda v: jax.nn.gelu(v, approximate=False), hidden)
    hidden_grad = pull(active_grad)[0].astype(BF)
    up_bias_grad = jnp.sum(hidden_grad.astype(F32), axis=0)
    up_grad = jnp.einsum("ti,tf->if", norm_two, hidden_grad, preferred_element_type=F32)
    norm_two_grad = jnp.einsum("tf,if->ti", hidden_grad, WU, preferred_element_type=F32)
    context_grad = jnp.einsum("to,io->ti", G, w_dense, preferred_element_type=F32).astype(BF)
    context_grad = context_grad.reshape(length, heads, HEAD_DIM)
    prob_grad = jnp.einsum("qhd,khd->hqk", context_grad, values, preferred_element_type=F32)
    weighted = jnp.sum(probs * prob_grad, axis=-1, keepdims=True)
    score_grad = (probs * (prob_grad - weighted)).astype(BF)
    query_grad = jnp.einsum("hqk,khd->qhd", score_grad, keys, preferred_element_type=F32) * scale
    key_grad = jnp.einsum("hqk,qhd->khd", score_grad, query, preferred_element_type=F32) * scale
    value_grad = jnp.einsum("hqk,qhd->khd", low, context_grad, preferred_element_type=F32)
    rotated_grad = jnp.stack([query_grad, key_grad, value_grad], axis=2).astype(BF).astype(F32)
    packed_grad = rotate(rotated_grad, positions, -1.0).reshape(length, -1).astype(BF)
    qkv_bias_grad = jnp.sum(packed_grad.astype(F32), axis=0)
    qkv_grad = jnp.einsum("ti,tj->ij", norm_one, packed_grad, preferred_element_type=F32)
    norm_one_grad = jnp.einsum("tj,ij->ti", packed_grad, WQ, preferred_element_type=F32)
    u = norm_one_grad * gain_one + norm_two_grad * gain_two
    mean_u = jnp.mean(u, axis=-1, keepdims=True)
    mean_ux = jnp.mean(u * xhat, axis=-1, keepdims=True)
    dx = inverse * (u - mean_u - xhat * mean_ux)
    sums = jnp.stack(
        [
            jnp.sum(norm_one_grad * xhat, axis=0),
            jnp.sum(norm_one_grad, axis=0),
            jnp.sum(norm_two_grad * xhat, axis=0),
            jnp.sum(norm_two_grad, axis=0),
        ]
    )
    return (
        out.astype(BF),
        dx.astype(BF),
        sums,
        up_bias_grad,
        qkv_bias_grad,
        up_grad.astype(BF),
        qkv_grad.astype(BF),
        down_grad.astype(BF),
        dense_grad.astype(BF),
    )


def per_device(
    n,
    data,
    layer_input,
    attn_gain,
    attn_shift,
    mlp_gain,
    mlp_shift,
    qkv_weight,
    qkv_bias,
    dense_weight,
    dense_bias,
    up_weight,
    up_bias,
    down_weight,
    down_bias,
    out_grad,
):
    unused, rows, width = layer_input.shape
    x = layer_input.reshape(rows, width)
    g = out_grad.reshape(rows, width)
    part = width // n
    small = jnp.stack(
        [attn_gain, attn_shift, mlp_gain, mlp_shift, dense_bias, down_bias, attn_gain, attn_gain]
    ).astype(F32)
    SM, X, G, WQ, WU = gather(n, data, small, x, g, qkv_weight, up_weight)
    vectors = jnp.swapaxes(SM, 0, 1).reshape(8, width)
    bias = (vectors[4] + vectors[5])[None]
    OP, DX, sums, bu, bq, UG, QG, DnG, DeG = middle(
        X, G, WQ, WU, dense_weight, down_weight, qkv_bias, up_bias, vectors
    )
    v1 = jnp.concatenate(
        [sums, jnp.sum(g.astype(F32), axis=0)[None], jnp.zeros((3, width), F32)], axis=0
    )
    v2 = jnp.concatenate([bu.reshape(4, part), bq.reshape(3, part), jnp.zeros((1, part), F32)])
    out, dx, tiny, fu, fq, fdn, fde = reduce_all(
        n, data, OP, DX, v1, v2, bias, x, g, UG, QG, DnG, DeG
    )
    return (
        out.reshape(layer_input.shape),
        dx.reshape(layer_input.shape),
        tiny[0],
        tiny[1],
        tiny[2],
        tiny[3],
        fq.reshape(part, -1).astype(F32),
        tiny[12:15].reshape(-1),
        fde.reshape(-1, width).astype(F32),
        tiny[4],
        fu.reshape(part, -1).astype(F32),
        tiny[8:12].reshape(-1),
        fdn.reshape(-1, width).astype(F32),
        tiny[4],
    )


def solution(mesh):
    tokens, row, vector = P("dp", "seq", None), P("seq", None), P("seq")
    in_specs = (tokens,) + (vector,) * 4 + (row, vector) * 4 + (tokens,)
    out_specs = (tokens, tokens) + (vector,) * 4 + (row, vector) * 4
    return jax.shard_map(
        functools.partial(per_device, mesh.shape["seq"], mesh.shape["dp"]),
        mesh=mesh,
        in_specs=in_specs,
        out_specs=out_specs,
        check_vma=False,
    )
```

```python
import functools
import math

import jax
import jax.numpy as jnp
import numpy as np
from jax import lax
from jax.experimental import pallas as pl
from jax.experimental.pallas import tpu as pltpu
from jax.sharding import PartitionSpec as P

HEADS = 16
HEAD_DIM = 64
ROT_DIM = 16
PLANE = 8
CHIPS = 4
epsilon = 1e-05
mask_fill = -1e30
MESH = pl.DeviceIdType.MESH
BF = jnp.bfloat16
F32 = jnp.float32


def rows_at(ref, start, count):
    return ref.at[pl.ds(pl.multiple_of(start, count), count)]


def block_at(ref, row, rows, col, cols):
    return ref.at[
        pl.ds(pl.multiple_of(row, rows), rows), pl.ds(pl.multiple_of(col, cols), cols)
    ]


class Place:
    def __init__(self, n, data):
        self.n, self.data = n, data
        self.d = lax.axis_index("dp")
        self.z = lax.axis_index("seq")
        self.base = self.d // PLANE * PLANE
        self.r = lax.rem(self.d, PLANE)
        self.ch = self.r // 2
        self.c = lax.rem(self.r, 2)
        self.piece = self.c * CHIPS + self.ch

    def seq_peer(self, k):
        other = lax.rem(self.z + k, self.n)
        return other, (self.d, other)

    def chip_peer(self, k):
        other = lax.rem(self.ch + k, CHIPS)
        return other, (self.base + other * 2 + self.c, self.z)

    def partner(self):
        return (self.base + self.ch * 2 + 1 - self.c, self.z)

    def dp_peer(self, k):
        other = lax.rem(self.d + k, self.data)
        return other, (other, self.z)

    def barrier(self):
        sem = pltpu.get_barrier_semaphore()
        for k in range(1, self.n):
            pl.semaphore_signal(sem, inc=1, device_id=self.seq_peer(k)[1], device_id_type=MESH)
        for k in range(1, self.data):
            pl.semaphore_signal(sem, inc=1, device_id=self.dp_peer(k)[1], device_id_type=MESH)
        pl.semaphore_wait(sem, self.n - 1 + self.data - 1)


def send(src, dst, ssem, rsem, to):
    return pltpu.make_async_remote_copy(
        src_ref=src, dst_ref=dst, send_sem=ssem, recv_sem=rsem, device_id=to, device_id_type=MESH
    )


class LineGather:
    def __init__(self, me, shard, full, rows, chunks, ssem, rsem):
        self.me, self.shard, self.full = me, shard, full
        self.rows, self.chunks, self.ssem, self.rsem = rows, chunks, ssem, rsem

    def part(self, owner, c):
        size = self.rows // self.chunks
        return rows_at(self.full, owner * self.rows + c * size, size)

    def copy(self, src, owner, c, way):
        me = self.me
        to = jnp.minimum(me.z + 1, me.n - 1) if way == 0 else jnp.maximum(me.z - 1, 0)
        return send(
            src,
            self.part(owner, c),
            self.ssem.at[way, owner, c],
            self.rsem.at[owner, c],
            (me.d, to),
        )

    def start(self):
        me = self.me
        size = self.rows // self.chunks
        for c in range(self.chunks):
            src = rows_at(self.shard, c * size, size)

            @pl.when(me.z < me.n - 1)
            def _():
                self.copy(src, me.z, c, 0).start()

            @pl.when(me.z > 0)
            def _():
                self.copy(src, me.z, c, 1).start()

    def step(self, s, c):
        me = self.me

        @pl.when(me.z >= s)
        def _():
            owner = me.z - s
            copy = self.copy(self.part(owner, c), owner, c, 0)
            copy.wait_recv()

            @pl.when(me.z < me.n - 1)
            def _():
                copy.start()

        @pl.when(me.z + s < me.n)
        def _():
            owner = me.z + s
            copy = self.copy(self.part(owner, c), owner, c, 1)
            copy.wait_recv()

            @pl.when(me.z > 0)
            def _():
                copy.start()

    def forward(self, s):
        me = self.me
        inner = (me.z > 0) & (me.z < me.n - 1)
        for c in range(self.chunks):
            for way, valid, owner in ((0, me.z >= s, me.z - s), (1, me.z + s < me.n, me.z + s)):

                @pl.when(inner & valid)
                def _():
                    copy = self.copy(self.part(owner, c), owner, c, way)
                    copy.wait_recv()
                    copy.start()

    def arrive(self, owner):
        me = self.me

        @pl.when(((me.z == 0) | (me.z == me.n - 1)) & (owner != me.z))
        def _():
            for c in range(self.chunks):
                self.copy(self.part(owner, c), owner, c, 0).wait_recv()

    def finish(self):
        me = self.me
        for c in range(self.chunks):
            for owner in range(me.n):

                @pl.when((me.z < me.n - 1) & (owner <= me.z))
                def _():
                    self.copy(self.part(owner, c), owner, c, 0).wait_send()

                @pl.when((me.z > 0) & (owner >= me.z))
                def _():
                    self.copy(self.part(owner, c), owner, c, 1).wait_send()


class ColumnGather:
    def __init__(self, me, shard, full, sems):
        self.me, self.shard, self.full = me, shard, full
        self.depth = shard.shape[0]
        self.rp = self.depth // PLANE
        self.cols = full.shape[1]
        self.zs, self.zr, self.ps, self.pr, self.fs = sems

    def part(self, src_z, piece):
        return rows_at(self.full, (src_z * PLANE + piece) * self.rp, self.rp)

    def across(self, k):
        me = self.me
        other, to = me.seq_peer(k)
        src = block_at(self.shard, me.piece * self.rp, self.rp, other * self.cols, self.cols)
        return send(src, self.part(me.z, me.piece), self.zs.at[k], self.zr.at[me.n - k], to)

    def came(self, k):
        me = self.me
        other, to = me.seq_peer(k)
        src = block_at(self.shard, me.piece * self.rp, self.rp, other * self.cols, self.cols)
        return send(src, self.part(other, me.piece), self.zs.at[k], self.zr.at[k], to)

    def shares(self, k):
        me = self.me
        other, unused = me.seq_peer(k)
        mine = self.part(other, me.piece)
        for j in range(1, CHIPS):
            to = me.chip_peer(j)[1]
            yield send(mine, mine, self.ps.at[k, j], self.pr.at[k, CHIPS - j], to)
        yield send(mine, mine, self.ps.at[k, 0], self.fs.at[1, k, 0], me.partner())

    def handed(self, k, j):
        me = self.me
        other, unused = me.seq_peer(k)
        chip = me.chip_peer(j)[0]
        return self.part(other, me.c * CHIPS + chip), self.part(other, (1 - me.c) * CHIPS + chip)

    def start(self):
        for k in range(self.me.n - 1, 0, -1):
            self.across(k).start()

    def share(self, k):
        self.came(k).wait_recv()
        for copy in self.shares(k):
            copy.start()

    def hand(self, k):
        me = self.me
        for j in range(1, CHIPS):
            got, unused = self.handed(k, j)
            send(got, got, self.ps.at[k, j], self.pr.at[k, j], me.chip_peer(j)[1]).wait_recv()
            send(got, got, self.fs.at[0, k, j], self.fs.at[1, k, j], me.partner()).start()

    def finish(self):
        me = self.me
        for k in range(1, me.n):
            self.across(k).wait_send()
            for copy in self.shares(k):
                copy.wait_send()
            other, unused = me.seq_peer(k)
            for j in range(CHIPS):
                unused, got = self.handed(k, j)
                copy = send(got, got, self.fs.at[0, k, j], self.fs.at[1, k, j], me.partner())
                copy.wait_recv()
                if j > 0:
                    copy.wait_send()


def column_sems(n):
    dma = pltpu.SemaphoreType.DMA
    return [dma((n,)), dma((n,)), dma((n, CHIPS)), dma((n, CHIPS)), dma((2, n, CHIPS))]


def gather_kernel(n, data, chunks, sm, x, g, wq, wu, SM, X, G, WQ, WU, *sems):
    me = Place(n, data)
    rows = x.shape[0]
    lsem, ss, sr, xs, xr, gs, gr = sems[:7]
    me.barrier()
    cq, cu = ColumnGather(me, wq, WQ, sems[7:12]), ColumnGather(me, wu, WU, sems[12:17])
    lx = LineGather(me, x, X, rows, chunks, xs, xr)
    lg = LineGather(me, g, G, rows, chunks, gs, gr)
    depth = wq.shape[0]
    own = [
        pltpu.make_async_copy(sm, SM.at[me.z], lsem.at[0]),
        pltpu.make_async_copy(x, rows_at(X, me.z * rows, rows), lsem.at[1]),
        pltpu.make_async_copy(g, rows_at(G, me.z * rows, rows), lsem.at[2]),
        pltpu.make_async_copy(
            block_at(wq, 0, depth, me.z * WQ.shape[1], WQ.shape[1]),
            rows_at(WQ, me.z * depth, depth),
            lsem.at[3],
        ),
        pltpu.make_async_copy(
            block_at(wu, 0, depth, me.z * WU.shape[1], WU.shape[1]),
            rows_at(WU, me.z * depth, depth),
            lsem.at[4],
        ),
    ]
    for copy in own:
        copy.start()

    def small(k, slot):
        return send(sm, SM.at[slot], ss.at[k], sr.at[slot], me.seq_peer(k)[1])

    for k in range(1, n):
        small(k, me.z).start()
    cq.start()
    cu.start()
    lx.start()
    lg.start()
    near = sorted({1, n - 1})
    for k in near:
        cq.share(k)
        cu.share(k)
    for c in range(chunks):
        lx.step(1, c)
    for k in range(1, n):
        if k not in near:
            cq.share(k)
            cu.share(k)
    for s in range(2, n):
        for c in range(chunks):
            lx.step(s, c)
    for k in range(1, n):
        cq.hand(k)
        cu.hand(k)
    for s in range(1, n):
        for c in range(chunks):
            lg.step(s, c)
    for k in range(1, n):
        small(k, me.z).wait_send()
        small(k, me.seq_peer(k)[0]).wait_recv()
    cq.finish()
    cu.finish()
    lx.finish()
    lg.finish()
    for copy in own:
        copy.wait()


def gather(n, data, sm, x, g, wq, wu):
    rows, width = x.shape
    depth = wq.shape[0]
    chunks = 4
    vm = pl.BlockSpec(memory_space=pltpu.VMEM)
    dma = pltpu.SemaphoreType.DMA
    sds = jax.ShapeDtypeStruct
    return pl.pallas_call(
        functools.partial(gather_kernel, n, data, chunks),
        out_shape=[
            sds((n,) + sm.shape, sm.dtype),
            sds((n * rows, width), x.dtype),
            sds((n * rows, width), x.dtype),
            sds((n * depth, wq.shape[1] // n), wq.dtype),
            sds((n * depth, wu.shape[1] // n), wu.dtype),
        ],
        in_specs=[vm] * 5,
        out_specs=[vm] * 5,
        scratch_shapes=[
            dma((5,)),
            dma((n,)),
            dma((n,)),
            dma((2, n, chunks)),
            dma((n, chunks)),
            dma((2, n, chunks)),
            dma((n, chunks)),
        ]
        + column_sems(n)
        + column_sems(n),
        compiler_params=pltpu.CompilerParams(
            collective_id=0, has_side_effects=True, vmem_limit_bytes=60 << 20
        ),
        name="gather",
    )(sm, x, g, wq, wu)


class RowReduce:
    def __init__(self, me, part, got, ssem, rsem):
        self.me, self.part, self.got, self.ssem, self.rsem = me, part, got, ssem, rsem
        self.rows = got.shape[1]

    def copy(self, k, slot):
        other, to = self.me.seq_peer(k)
        return send(
            rows_at(self.part, other * self.rows, self.rows),
            self.got.at[slot],
            self.ssem.at[k],
            self.rsem.at[slot],
            to,
        )

    def start(self):
        for k in range(1, self.me.n):
            self.copy(k, self.me.z).start()

    def wait(self):
        for k in range(1, self.me.n):
            self.copy(k, self.me.seq_peer(k)[0]).wait_recv()

    def finish(self):
        for k in range(1, self.me.n):
            self.copy(k, self.me.z).wait_send()


class GradReduce:
    def __init__(self, me, part, half, chips, total, groups, sems):
        self.me, self.part, self.half = me, part, half
        self.chips, self.total, self.groups = chips, total, groups
        self.hs, self.hr, self.cs, self.cr, self.gs, self.gr = sems

    def swap(self):
        me = self.me
        return send(
            self.part.at[:, pl.ds((1 - me.c) * CHIPS, CHIPS)],
            self.half,
            self.hs,
            self.hr,
            me.partner(),
        )

    def to_chip(self, k, slot):
        other, to = self.me.chip_peer(k)
        return send(
            self.part.at[:, self.me.c * CHIPS + other],
            self.chips.at[slot],
            self.cs.at[k],
            self.cr.at[slot],
            to,
        )

    def start(self):
        self.swap().start()

    def chip_sums(self):
        me = self.me
        self.swap().wait_recv()

        @pl.loop(0, CHIPS)
        def _(j):
            for m in range(self.half.shape[0]):
                self.part[m, me.c * CHIPS + j] = (
                    self.part[m, me.c * CHIPS + j].astype(F32) + self.half[m, j].astype(F32)
                ).astype(BF)

        for k in range(1, CHIPS):
            self.to_chip(k, CHIPS - k - 1).start()

    def to_group(self, k, slot):
        me = self.me
        count = me.data // PLANE
        other = lax.rem(me.d // PLANE + k, count)
        return send(
            self.total,
            self.groups.at[slot],
            self.gs.at[k],
            self.gr.at[slot],
            (other * PLANE + me.r, me.z),
        )

    def sum_up(self):
        me = self.me
        for k in range(1, CHIPS):
            self.to_chip(k, k - 1).wait_recv()
        for m in range(self.total.shape[0]):
            total = self.part[m, me.c * CHIPS + me.ch].astype(F32)
            for k in range(1, CHIPS):
                total = total + self.chips[k - 1, m].astype(F32)
            self.total[m] = total.astype(BF)
        count = me.data // PLANE
        if count > 1:
            own = me.d // PLANE
            for k in range(1, count):
                self.to_group(k, own).start()
            for k in range(1, count):
                self.to_group(k, lax.rem(own + k, count)).wait_recv()
                self.to_group(k, own).wait_send()
            self.groups[own] = self.total[...]
            total = self.groups[0].astype(F32)
            for e in range(1, count):
                total = total + self.groups[e].astype(F32)
            self.total[...] = total.astype(BF)

    def finish(self):
        self.swap().wait_send()
        for k in range(1, CHIPS):
            self.to_chip(k, CHIPS - k - 1).wait_send()


class GradShare:
    def __init__(self, me, final, sems):
        self.me, self.final = me, final
        self.ss, self.sr, self.fs, self.fr = sems

    def copies(self):
        me = self.me
        mine = self.final.at[me.piece]
        for k in range(1, CHIPS):
            yield send(mine, mine, self.ss.at[k], self.sr.at[me.ch], me.chip_peer(k)[1])
        yield send(mine, mine, self.ss.at[0], self.fr.at[0], me.partner())

    def start(self):
        for copy in self.copies():
            copy.start()

    def handed(self, k):
        me = self.me
        got = self.final.at[me.c * CHIPS + me.chip_peer(k)[0]]
        return send(got, got, self.fs.at[k], self.fr.at[k], me.partner())

    def hand(self):
        me = self.me
        for k in range(1, CHIPS):
            chip, to = me.chip_peer(k)
            got = self.final.at[me.c * CHIPS + chip]
            send(got, got, self.ss.at[k], self.sr.at[chip], to).wait_recv()
            self.handed(k).start()

    def finish(self):
        me = self.me
        for copy in self.copies():
            copy.wait_send()
        for k in range(CHIPS):
            got = self.final.at[(1 - me.c) * CHIPS + me.chip_peer(k)[0]]
            copy = send(got, got, self.fs.at[k], self.fr.at[k], me.partner())
            copy.wait_recv()
            if k > 0:
                copy.wait_send()


class RowsBack:
    def __init__(self, me, total, final, ssem, rsem, lsem):
        self.me, self.total, self.final = me, total, final
        self.ssem, self.rsem, self.lsem = ssem, rsem, lsem

    def place(self, src_z):
        cols = self.total.shape[2]
        return self.final.at[
            self.me.piece, :, pl.ds(pl.multiple_of(src_z * cols, cols), cols)
        ]

    def copy(self, k, slot):
        other, to = self.me.seq_peer(k)
        return send(
            self.total.at[other], self.place(slot), self.ssem.at[k], self.rsem.at[slot], to
        )

    def own(self):
        me = self.me
        return pltpu.make_async_copy(self.total.at[me.z], self.place(me.z), self.lsem)

    def start(self):
        for k in range(1, self.me.n):
            self.copy(k, self.me.z).start()
        self.own().start()

    def wait(self):
        me = self.me
        for k in range(1, me.n):
            self.copy(k, me.seq_peer(k)[0]).wait_recv()
        self.own().wait()

    def finish(self):
        for k in range(1, self.me.n):
            self.copy(k, self.me.z).wait_send()


def reduce_kernel(n, data, *refs):
    (OP, DX, v1, v2, bias, x, g, UG, QG, DnG, DeG) = refs[:11]
    out, dx, small, fu, fq, fdn, fde = refs[11:18]
    scratch = list(refs[18:])
    me = Place(n, data)

    def take(count):
        got = scratch[:count]
        del scratch[:count]
        return got

    og, xg, zs, zr, v1g, v1s, v1r, v2m, v2g, v2s, v2r = take(11)
    reduces = []
    for part in (DnG, DeG, UG, QG):
        bufs = take(4)
        reduces.append(GradReduce(me, part, *bufs, take(6)))
    red_dn, red_de, red_u, red_q = reduces
    shares = [GradShare(me, final, take(4)) for final in (fdn, fde, fu, fq)]
    back_u = RowsBack(me, red_u.total, fu, *take(3))
    back_q = RowsBack(me, red_q.total, fq, *take(3))
    (dsem,) = take(1)
    assert not scratch
    ro = RowReduce(me, OP, og, zs.at[0], zr.at[0])
    rx = RowReduce(me, DX, xg, zs.at[1], zr.at[1])
    me.barrier()
    cs = v1g.shape[2]

    def small_z(k, slot):
        other, to = me.seq_peer(k)
        return send(
            v1.at[:, pl.ds(pl.multiple_of(other * cs, cs), cs)],
            v1g.at[slot],
            v1s.at[k],
            v1r.at[slot],
            to,
        )

    def small_dp(k, slot):
        return send(v2m, v2g.at[slot], v2s.at[k], v2r.at[slot], me.dp_peer(k)[1])

    for k in range(1, n):
        small_z(k, me.z).start()
    for red in reduces:
        red.start()
    ro.start()
    rx.start()
    for red in reduces:
        red.chip_sums()
    for k in range(1, n):
        small_z(k, me.seq_peer(k)[0]).wait_recv()
    v1g[me.z] = v1[:, pl.ds(pl.multiple_of(me.z * cs, cs), cs)]
    total = v1g[0]
    for k in range(1, n):
        total = total + v1g[k]
    v2m[0:8] = total
    v2m[8:16] = v2[...]
    for k in range(1, data):
        small_dp(k, me.d).start()
    own = []
    for i, (red, final) in enumerate(((red_dn, fdn), (red_de, fde))):
        red.sum_up()
        copy = pltpu.make_async_copy(red.total.at[0], final.at[me.piece], dsem.at[i])
        copy.start()
        own.append(copy)
    red_u.sum_up()
    back_u.start()
    red_q.sum_up()
    back_q.start()
    for copy in own:
        copy.wait()
    shares[0].start()
    shares[1].start()
    back_u.wait()
    shares[2].start()
    back_q.wait()
    shares[3].start()
    for share in shares:
        share.hand()
    for k in range(1, data):
        small_dp(k, me.dp_peer(k)[0]).wait_recv()
    v2g[me.d] = v2m[...]

    def add(i, acc):
        return acc + v2g[i]

    small[...] = lax.fori_loop(1, data, add, v2g[0])
    rows = x.shape[0]
    for red, base, result, extra in ((ro, x, out, bias), (rx, g, dx, None)):
        red.wait()
        step = rows // 4

        @pl.loop(0, 4)
        def _(i):
            at = pl.ds(pl.multiple_of(i * step, step), step)
            mine = pl.ds(pl.multiple_of(me.z * rows + i * step, step), step)
            acc = base[at].astype(F32) + red.part[mine].astype(F32)
            for k in range(1, n):
                acc = acc + red.got[me.seq_peer(k)[0], at].astype(F32)
            if extra is not None:
                acc = acc + extra[...]
            result[at] = acc.astype(BF)

        red.finish()
    for k in range(1, n):
        small_z(k, me.z).wait_send()
    for k in range(1, data):
        small_dp(k, me.d).wait_send()
    for red in reduces:
        red.finish()
    for share in shares:
        share.finish()
    back_u.finish()
    back_q.finish()


def reduce_all(n, data, OP, DX, v1, v2, bias, x, g, UG, QG, DnG, DeG):
    vm = pl.BlockSpec(memory_space=pltpu.VMEM)
    dma = pltpu.SemaphoreType.DMA
    sds = jax.ShapeDtypeStruct
    rows, width = x.shape
    groups = data // PLANE
    parts = []
    for whole in (DnG, DeG):
        lead, cols = whole.shape
        parts.append(whole.reshape(1, PLANE, lead // PLANE, cols))
    for whole in (UG, QG):
        lead, cols = whole.shape
        parts.append(whole.reshape(n, PLANE, lead // n // PLANE, cols))
    dn, de, u, q = parts
    scratch = [
        pltpu.VMEM((n, rows, width), BF),
        pltpu.VMEM((n, rows, width), BF),
        dma((2, n)),
        dma((2, n)),
        pltpu.VMEM((n, 8, width // n), F32),
        dma((n,)),
        dma((n,)),
        pltpu.VMEM((16, width // n), F32),
        pltpu.VMEM((data, 16, width // n), F32),
        dma((data,)),
        dma((data,)),
    ]
    for part in (dn, de, u, q):
        m, unused, rp, cols = part.shape
        scratch += [
            pltpu.VMEM((m, CHIPS, rp, cols), BF),
            pltpu.VMEM((CHIPS - 1, m, rp, cols), BF),
            pltpu.VMEM((m, rp, cols), BF),
            pltpu.VMEM((groups, m, rp, cols) if groups > 1 else (1, 1, 16, 128), BF),
            dma,
            dma,
            dma((CHIPS,)),
            dma((CHIPS,)),
            dma((groups,)),
            dma((groups,)),
        ]
    for unused in range(4):
        scratch += [dma((CHIPS,))] * 4
    scratch += [dma((n,)), dma((n,)), dma] * 2
    scratch += [dma((2,))]
    outs = [
        sds((rows, width), BF),
        sds((rows, width), BF),
        sds((16, width // n), F32),
        sds((PLANE, u.shape[2], u.shape[3] * n), BF),
        sds((PLANE, q.shape[2], q.shape[3] * n), BF),
        sds((PLANE,) + dn.shape[2:], BF),
        sds((PLANE,) + de.shape[2:], BF),
    ]
    return pl.pallas_call(
        functools.partial(reduce_kernel, n, data),
        out_shape=outs,
        in_specs=[vm] * 11,
        out_specs=[vm] * 7,
        scratch_shapes=scratch,
        compiler_params=pltpu.CompilerParams(
            collective_id=1, has_side_effects=True, vmem_limit_bytes=63 << 20
        ),
        name="reduce",
    )(OP, DX, v1, v2, bias, x, g, u, q, dn, de)


def layer_norm_parts(token_rows):
    average = jnp.mean(token_rows, axis=-1, keepdims=True)
    centered = token_rows - average
    variance = jnp.mean(centered * centered, axis=-1, keepdims=True)
    inverse = lax.rsqrt(variance + epsilon)
    return centered * inverse, inverse


def rotate(packed, positions, sign):
    half = ROT_DIM // 2
    freqs = 10000.0 ** (-jnp.arange(half, dtype=F32) * 2.0 / ROT_DIM)
    angles = positions.astype(F32)[:, None] * freqs[None, :]
    cosine = jnp.cos(angles)[:, None, None, :]
    sine = jnp.sin(angles)[:, None, None, :] * sign
    first = packed[..., :half]
    second = packed[..., half:ROT_DIM]
    turned = jnp.concatenate(
        [first * cosine - second * sine, second * cosine + first * sine, packed[..., ROT_DIM:]],
        axis=-1,
    )
    select = (jnp.arange(3) < 2)[:, None]
    return jnp.where(select, turned, packed)


def middle(X, G, WQ, WU, w_dense, w_down, b_qkv, b_up, vectors):
    length, width = X.shape
    heads = WQ.shape[1] // (3 * HEAD_DIM)
    scale = HEAD_DIM ** (-0.5)
    gain_one, shift_one, gain_two, shift_two = (vectors[i] for i in range(4))
    xhat, inverse = layer_norm_parts(X.astype(F32))
    norm_one = (xhat * gain_one + shift_one).astype(BF)
    norm_two = (xhat * gain_two + shift_two).astype(BF)
    packed = jnp.dot(norm_one, WQ, preferred_element_type=F32) + b_qkv.astype(F32)
    positions = jnp.arange(length, dtype=jnp.int32)
    packed = rotate(packed.reshape(length, heads, 3, HEAD_DIM), positions, 1.0).astype(BF)
    query, keys, values = packed[:, :, 0], packed[:, :, 1], packed[:, :, 2]
    scores = jnp.einsum("qhd,khd->hqk", query, keys, preferred_element_type=F32) * scale
    allowed = positions[:, None] >= positions[None, :]
    probs = jax.nn.softmax(jnp.where(allowed, scores, mask_fill), axis=-1)
    low = probs.astype(BF)
    context = jnp.einsum("hqk,khd->qhd", low, values, preferred_element_type=F32)
    context = context.astype(BF).reshape(length, heads * HEAD_DIM)
    hidden = jnp.dot(norm_two, WU, preferred_element_type=F32) + b_up.astype(F32)
    active = jax.nn.gelu(hidden, approximate=False).astype(BF)
    out = jnp.dot(context, w_dense, preferred_element_type=F32) + jnp.dot(
        active, w_down, preferred_element_type=F32
    )
    down_grad = jnp.einsum("tf,to->fo", active, G, preferred_element_type=F32)
    dense_grad = jnp.einsum("ti,to->io", context, G, preferred_element_type=F32)
    active_grad = jnp.einsum("to,fo->tf", G, w_down, preferred_element_type=F32)
    unused, pull = jax.vjp(lambda v: jax.nn.gelu(v, approximate=False), hidden)
    hidden_grad = pull(active_grad)[0].astype(BF)
    up_bias_grad = jnp.sum(hidden_grad.astype(F32), axis=0)
    up_grad = jnp.einsum("ti,tf->if", norm_two, hidden_grad, preferred_element_type=F32)
    norm_two_grad = jnp.einsum("tf,if->ti", hidden_grad, WU, preferred_element_type=F32)
    context_grad = jnp.einsum("to,io->ti", G, w_dense, preferred_element_type=F32).astype(BF)
    context_grad = context_grad.reshape(length, heads, HEAD_DIM)
    prob_grad = jnp.einsum("qhd,khd->hqk", context_grad, values, preferred_element_type=F32)
    weighted = jnp.sum(probs * prob_grad, axis=-1, keepdims=True)
    score_grad = (probs * (prob_grad - weighted)).astype(BF)
    query_grad = jnp.einsum("hqk,khd->qhd", score_grad, keys, preferred_element_type=F32) * scale
    key_grad = jnp.einsum("hqk,qhd->khd", score_grad, query, preferred_element_type=F32) * scale
    value_grad = jnp.einsum("hqk,qhd->khd", low, context_grad, preferred_element_type=F32)
    rotated_grad = jnp.stack([query_grad, key_grad, value_grad], axis=2).astype(BF).astype(F32)
    packed_grad = rotate(rotated_grad, positions, -1.0).reshape(length, -1).astype(BF)
    qkv_bias_grad = jnp.sum(packed_grad.astype(F32), axis=0)
    qkv_grad = jnp.einsum("ti,tj->ij", norm_one, packed_grad, preferred_element_type=F32)
    norm_one_grad = jnp.einsum("tj,ij->ti", packed_grad, WQ, preferred_element_type=F32)
    u = norm_one_grad * gain_one + norm_two_grad * gain_two
    mean_u = jnp.mean(u, axis=-1, keepdims=True)
    mean_ux = jnp.mean(u * xhat, axis=-1, keepdims=True)
    dx = inverse * (u - mean_u - xhat * mean_ux)
    sums = jnp.stack(
        [
            jnp.sum(norm_one_grad * xhat, axis=0),
            jnp.sum(norm_one_grad, axis=0),
            jnp.sum(norm_two_grad * xhat, axis=0),
            jnp.sum(norm_two_grad, axis=0),
        ]
    )
    return (
        out.astype(BF),
        dx.astype(BF),
        sums,
        up_bias_grad,
        qkv_bias_grad,
        up_grad.astype(BF),
        qkv_grad.astype(BF),
        down_grad.astype(BF),
        dense_grad.astype(BF),
    )


NN = (((1,), (0,)), ((), ()))
NT = (((1,), (1,)), ((), ()))
TN = (((0,), (0,)), ((), ()))
ROOT_HALF = 0.7071067811865476
PDF_SCALE = 0.3989422804014327


def dot(left, right, dims=NN):
    return lax.dot_general(left, right, dims, preferred_element_type=F32)


def rotary_tables(length):
    half = ROT_DIM // 2
    freqs = 10000.0 ** (-jnp.arange(half, dtype=F32) * 2.0 / ROT_DIM)
    angles = jnp.arange(length, dtype=jnp.int32).astype(F32)[:, None] * freqs[None, :]
    cosine, sine = jnp.cos(angles), jnp.sin(angles)
    rest = HEAD_DIM - ROT_DIM
    keep, none, gap = jnp.ones((length, rest)), jnp.zeros((length, rest)), jnp.zeros_like(sine)
    same = jnp.concatenate([cosine, cosine, keep] * 2, axis=1)
    up = jnp.concatenate([-sine, gap, none] * 2, axis=1)
    down = jnp.concatenate([gap, sine, none] * 2, axis=1)
    return jnp.stack([same, up, down]).astype(F32)


class Layer:
    def __init__(self, rows, refs):
        self.rows = rows
        for name, ref in refs.items():
            setattr(self, name, ref)
        self.length, self.width = self.X.shape
        self.heads = self.Q.shape[0]
        self.block = min(256, self.length)

    def at(self, j, rows=None, part=0):
        rows = rows or self.rows
        return pl.ds(pl.multiple_of(j * self.rows + part * rows, rows), rows)

    def norm(self, j):
        step = 64

        @pl.loop(0, self.rows // step)
        def _(i):
            at = self.at(j, step, i)
            x = self.X[at].astype(F32)
            average = jnp.mean(x, axis=-1, keepdims=True)
            centered = x - average
            variance = jnp.mean(centered * centered, axis=-1, keepdims=True)
            inverse = lax.rsqrt(variance + epsilon)
            xhat = centered * inverse
            self.MEAN[at] = average
            self.INV[at] = inverse
            self.N1[at] = (xhat * self.VEC[0:1] + self.VEC[1:2]).astype(BF)
            self.N2[at] = (xhat * self.VEC[2:3] + self.VEC[3:4]).astype(BF)

    def turn(self, values, at, kind, sign):
        lanes = lax.broadcasted_iota(jnp.int32, values.shape, 1)
        turned = values * self.ROT[0, at] + sign * (
            pltpu.roll(values, 128 - ROT_DIM // 2, 1) * self.ROT[1, at]
            + pltpu.roll(values, ROT_DIM // 2, 1) * self.ROT[2, at]
        )
        if kind == 0:
            return turned
        return jnp.where((lanes >= HEAD_DIM) if kind == 1 else (lanes < HEAD_DIM), turned, values)

    def qkv(self, j):
        at = self.at(j)
        scale = HEAD_DIM ** (-0.5)
        packed = dot(self.N1[at], self.WQ[...])
        bias = self.BQ[...].astype(F32)
        places = [(self.Q, scale), (self.K, None), (self.V, None)]
        for t in range(packed.shape[1] // 128):
            cols = slice(t * 128, t * 128 + 128)
            low = self.turn(packed[:, cols] + bias[:, cols], at, t % 3, 1.0).astype(BF)
            for side in range(2):
                index = 2 * t + side
                ref, factor = places[index % 3]
                value = low[:, side * HEAD_DIM : side * HEAD_DIM + HEAD_DIM]
                ref[index // 3, at] = value if factor is None else value * jnp.asarray(factor, BF)

    def up(self, j):
        at = self.at(j)
        tile = 256

        @pl.loop(0, self.WU.shape[1] // tile)
        def _(i):
            cols = pl.ds(pl.multiple_of(i * tile, tile), tile)
            hidden = dot(self.N2[at], self.WU[:, cols]) + self.BU[:, cols].astype(F32)
            cdf = 0.5 + 0.5 * lax.erf(hidden * ROOT_HALF)
            self.ACT[at, cols] = (hidden * cdf).astype(BF)
            pdf = PDF_SCALE * jnp.exp(-0.5 * hidden * hidden)
            self.DG[at, cols] = cdf + hidden * pdf

    def down(self, j):
        at = self.at(j)
        self.ACC[at] = dot(self.ACT[at], self.WDN[...])

    def masked(self, scores):
        rows = lax.broadcasted_iota(jnp.int32, scores.shape, 0)
        cols = lax.broadcasted_iota(jnp.int32, scores.shape, 1)
        return jnp.where(rows >= cols, scores, mask_fill)

    def attend_block(self, m, qb):
        size = self.block
        mine, before = slice(qb * size, qb * size + size), slice(0, qb * size)
        sides = []
        for side in range(2):
            h = 2 * m + side
            q = self.Q[h, mine]
            near = self.masked(dot(q, self.K[h, mine], NT))
            top = jnp.max(near, axis=-1, keepdims=True)
            if qb:
                far = dot(q, self.K[h, before], NT)
                top = jnp.maximum(top, jnp.max(far, axis=-1, keepdims=True))
            near = jnp.exp(near - top)
            total = jnp.sum(near, axis=-1, keepdims=True)
            if qb:
                far = jnp.exp(far - top)
                total = total + jnp.sum(far, axis=-1, keepdims=True)
            inverse = 1.0 / total
            self.LSE[h, mine] = top + jnp.log(total)
            context = dot((near * inverse).astype(BF), self.V[h, mine])
            if qb:
                context = context + dot((far * inverse).astype(BF), self.V[h, before])
            sides.append(context.astype(BF))
        self.CTX[m, mine] = jnp.concatenate(sides, axis=1)

    def attend_part(self, qb):
        @pl.loop(0, self.heads // 2)
        def _(m):
            self.attend_block(m, qb)

    def out(self, j):
        at = self.at(j)
        total = self.ACC[at]
        for m in range(self.heads // 2):
            total = total + dot(self.CTX[m, at], self.WDE[m * 128 : m * 128 + 128])
        self.OP[at] = total.astype(BF)

    def mlp_back(self, j):
        at = self.at(j)
        tile = 256

        @pl.loop(0, self.WU.shape[1] // tile)
        def _(i):
            cols = pl.ds(pl.multiple_of(i * tile, tile), tile)
            active_grad = dot(self.G[at], self.WDN[cols], NT)
            self.HG[at, cols] = (active_grad * self.DG[at, cols]).astype(BF)

        self.ACC[at] = dot(self.HG[at], self.WU[...], NT)

    def context_grad(self, j):
        at = self.at(j)
        for m in range(self.heads // 2):
            self.DO[m, at] = dot(self.G[at], self.WDE[m * 128 : m * 128 + 128], NT).astype(BF)

    def back_block(self, m, qb):
        size = self.block
        mine, before = slice(qb * size, qb * size + size), slice(0, qb * size)
        scale = HEAD_DIM ** (-0.5)
        upstream = self.DO[m, mine]
        for side in range(2):
            h = 2 * m + side
            q = self.Q[h, mine]
            do = upstream[:, side * HEAD_DIM : side * HEAD_DIM + HEAD_DIM]
            lse = self.LSE[h, mine]
            near = jnp.exp(self.masked(dot(q, self.K[h, mine], NT)) - lse)
            near_grad = dot(do, self.V[h, mine], NT)
            weighted = jnp.sum(near * near_grad, axis=-1, keepdims=True)
            if qb:
                far = jnp.exp(dot(q, self.K[h, before], NT) - lse)
                far_grad = dot(do, self.V[h, before], NT)
                weighted = weighted + jnp.sum(far * far_grad, axis=-1, keepdims=True)
            self.DV[side, mine] = dot(near.astype(BF), do, TN)
            score = (near * (near_grad - weighted)).astype(BF)
            self.DK[side, mine] = dot(score, q, TN)
            query = dot(score, self.K[h, mine])
            if qb:
                self.DV[side, before] += dot(far.astype(BF), do, TN)
                score = (far * (far_grad - weighted)).astype(BF)
                self.DK[side, before] += dot(score, q, TN)
                query = query + dot(score, self.K[h, before])
            self.DQ[side, mine] = (query * scale).astype(BF)

    def unturn(self, m):
        size = self.block

        @pl.loop(0, self.length // size)
        def _(i):
            at = pl.ds(pl.multiple_of(i * size, size), size)
            q0, q1 = self.DQ[0, at], self.DQ[1, at]
            k0, k1 = self.DK[0, at].astype(BF), self.DK[1, at].astype(BF)
            v0, v1 = self.DV[0, at].astype(BF), self.DV[1, at].astype(BF)
            for kind, pair in enumerate(((q0, k0), (v0, q1), (k1, v1))):
                both = jnp.concatenate(pair, axis=1).astype(F32)
                cols = pl.ds(pl.multiple_of((3 * m + kind) * 128, 128), 128)
                self.PG[at, cols] = self.turn(both, at, kind, -1.0).astype(BF)

    def attend_back(self, m):
        for qb in range(self.length // self.block):
            self.back_block(m, qb)
        self.unturn(m)

    def zero_sums(self):
        self.SUMS[...] = jnp.zeros_like(self.SUMS)
        self.BUG[...] = jnp.zeros_like(self.BUG)
        self.BQG[...] = jnp.zeros_like(self.BQG)

    def input_back(self, j):
        step = 64

        @pl.loop(0, self.rows // step)
        def _(i):
            at = self.at(j, step, i)
            inverse = self.INV[at]
            xhat = (self.X[at].astype(F32) - self.MEAN[at]) * inverse
            one, two = dot(self.PG[at], self.WQ[...], NT), self.ACC[at]
            u = one * self.VEC[0:1] + two * self.VEC[2:3]
            mean_u = jnp.mean(u, axis=-1, keepdims=True)
            mean_ux = jnp.mean(u * xhat, axis=-1, keepdims=True)
            self.DX[at] = (inverse * (u - mean_u - xhat * mean_ux)).astype(BF)
            self.SUMS[0:1] += jnp.sum(one * xhat, axis=0, keepdims=True)
            self.SUMS[1:2] += jnp.sum(one, axis=0, keepdims=True)
            self.SUMS[2:3] += jnp.sum(two * xhat, axis=0, keepdims=True)
            self.SUMS[3:4] += jnp.sum(two, axis=0, keepdims=True)
            self.BQG[...] += jnp.sum(self.PG[at].astype(F32), axis=0, keepdims=True)
            self.BUG[...] += jnp.sum(self.HG[at].astype(F32), axis=0, keepdims=True)

    def weight_grad(self, left, right, put):
        tile = 256
        count = left.shape[1] // tile

        @pl.loop(0, count)
        def _(i):
            cols = pl.ds(pl.multiple_of(i * tile, tile), tile)
            put(i, dot(left[:, cols], right[...], TN).astype(BF))

    def down_grad(self, put):
        self.weight_grad(self.ACT, self.G, put)

    def up_grad(self, put):
        self.weight_grad(self.N2, self.HG, put)

    def qkv_grad(self, put):
        self.weight_grad(self.N1, self.PG, put)

    def dense_grad(self, put):
        for m in range(self.heads // 2):
            put(m, dot(self.CTX[m], self.G[...], TN).astype(BF))


def layer_scratch(length, width, heads, hidden):
    vm = pltpu.VMEM
    pairs, packed = heads // 2, heads * 3 * HEAD_DIM
    return dict(
        MEAN=vm((length, 1), F32),
        INV=vm((length, 1), F32),
        N1=vm((length, width), BF),
        N2=vm((length, width), BF),
        Q=vm((heads, length, HEAD_DIM), BF),
        K=vm((heads, length, HEAD_DIM), BF),
        V=vm((heads, length, HEAD_DIM), BF),
        ACT=vm((length, hidden), BF),
        DG=vm((length, hidden), F32),
        ACC=vm((length, width), F32),
        LSE=vm((heads, length, 1), F32),
        CTX=vm((pairs, length, 2 * HEAD_DIM), BF),
        DO=vm((pairs, length, 2 * HEAD_DIM), BF),
        HG=vm((length, hidden), BF),
        DQ=vm((2, length, HEAD_DIM), BF),
        DK=vm((2, length, HEAD_DIM), F32),
        DV=vm((2, length, HEAD_DIM), F32),
        PG=vm((length, packed), BF),
    )


class LineReduce:
    def __init__(self, me, part, got, ssem, rsem):
        self.me, self.part, self.got, self.ssem, self.rsem = me, part, got, ssem, rsem
        self.rows = got.shape[1]

    def copy(self, j, way):
        me = self.me
        to = jnp.minimum(me.z + 1, me.n - 1) if way == 0 else jnp.maximum(me.z - 1, 0)
        slot = j if way == 0 else jnp.where(j == to, me.n, j)
        return send(
            rows_at(self.part, j * self.rows, self.rows),
            self.got.at[slot],
            self.ssem.at[j],
            self.rsem.at[slot],
            (me.d, to),
        )

    def came(self, slot):
        me = self.me
        got = self.got.at[slot]
        return send(got, got, self.ssem.at[0], self.rsem.at[slot], (me.d, me.z))

    def start(self, j):
        me = self.me

        @pl.when((me.z == 0) & (j > 0))
        def _():
            self.copy(j, 0).start()

        @pl.when((me.z == me.n - 1) & (j < me.n - 1))
        def _():
            self.copy(j, 1).start()

    def add(self, j):
        step = 64

        @pl.loop(0, self.rows // step)
        def _(i):
            mine = pl.ds(pl.multiple_of(j * self.rows + i * step, step), step)
            here = pl.ds(pl.multiple_of(i * step, step), step)
            self.part[mine] = (
                self.part[mine].astype(F32) + self.got[j, here].astype(F32)
            ).astype(BF)

    def step(self, t):
        me = self.me
        n = me.n
        for way, e in ((0, t - me.z), (1, t - (n - 1 - me.z))):
            j = n - 1 - e if way == 0 else e
            valid = (me.z > 0) & (me.z < n - 1) & (e >= 0)
            valid = valid & ((j > me.z) if way == 0 else (j < me.z))

            @pl.when(valid)
            def _():
                self.came(j).wait_recv()
                self.add(j)
                self.copy(j, way).start()

    def total(self, base, extra, result, tmp):
        me = self.me

        @pl.when(me.z > 0)
        def _():
            self.came(me.z).wait_recv()

        @pl.when(me.z < me.n - 1)
        def _():
            self.came(me.n).wait_recv()

        step = 64

        @pl.loop(0, self.rows // step)
        def _(i):
            here = pl.ds(pl.multiple_of(i * step, step), step)
            mine = pl.ds(pl.multiple_of(me.z * self.rows + i * step, step), step)
            tmp[...] = base[mine].astype(F32) + self.part[mine].astype(F32)
            if extra is not None:
                tmp[...] += extra

            @pl.when(me.z > 0)
            def _():
                tmp[...] += self.got[me.z, here].astype(F32)

            @pl.when(me.z < me.n - 1)
            def _():
                tmp[...] += self.got[me.n, here].astype(F32)

            result[here] = tmp[...].astype(BF)

    def finish(self):
        me = self.me
        for j in range(me.n):

            @pl.when((j > me.z) & (me.z < me.n - 1))
            def _():
                self.copy(j, 0).wait_send()

            @pl.when((j < me.z) & (me.z > 0))
            def _():
                self.copy(j, 1).wait_send()


def nearest(n):
    return [sorted(range(n), key=lambda j: abs(j - z)) for z in range(n)]


def pick(table, z, k):
    value = jnp.int32(0)
    for at, row in enumerate(table):
        for index, entry in enumerate(row):
            if entry:
                value = jnp.where((z == at) & (k == index), entry, value)
    return value


VECTORS = 6


def layer_kernel(n, data, chunks, names, *refs):
    refs = list(refs)

    def take(count):
        got = refs[:count]
        del refs[:count]
        return got

    vectors = take(VECTORS)
    x, g, wq, wu, WDE, WDN, bq, bu, ROT = take(9)
    out, dx, small, fu, fq, fdn, fde = take(7)
    ins = dict(zip(names, take(len(names))))
    ins.update(WDE=WDE, WDN=WDN, BQ=bq, BU=bu, ROT=ROT)
    rows = out.shape[0]
    layer = Layer(rows, ins)
    me = Place(n, data)
    SM, sm = take(2)
    layer.DX = layer.OP
    lsem, ss, sr, xs, xr, gs, gr = take(7)
    cq, cu = ColumnGather(me, wq, layer.WQ, take(5)), ColumnGather(me, wu, layer.WU, take(5))
    og, xg, os, orr, ds, dr = take(6)
    v1, v1g, v1s, v1r, v2m, v2g, v2s, v2r = take(8)
    reduces = []
    for unused in range(4):
        part, half, chips, total, groups = take(5)
        reduces.append(GradReduce(me, part, half, chips, total, groups, take(6)))
    red_dn, red_de, red_u, red_q = reduces
    shares = [GradShare(me, final, take(4)) for final in (fdn, fde, fu, fq)]
    share_dn, share_de, share_u, share_q = shares
    back_u = RowsBack(me, red_u.total, fu, *take(3))
    back_q = RowsBack(me, red_q.total, fq, *take(3))
    (dsem,) = take(1)
    assert not refs
    lx = LineGather(me, x, layer.X, rows, chunks, xs, xr)
    lg = LineGather(me, g, layer.G, rows, chunks, gs, gr)
    ro = LineReduce(me, layer.OP, og, os, orr)
    rx = LineReduce(me, layer.DX, xg, ds, dr)
    near = nearest(n)
    far = [list(range(n - 1, -1, -1)) if 2 * z < n else list(range(n)) for z in range(n)]
    depth = wq.shape[0]
    part = depth

    own = [
        pltpu.make_async_copy(x, rows_at(layer.X, me.z * rows, rows), lsem.at[0]),
        pltpu.make_async_copy(g, rows_at(layer.G, me.z * rows, rows), lsem.at[1]),
        pltpu.make_async_copy(
            block_at(wq, 0, depth, me.z * layer.WQ.shape[1], layer.WQ.shape[1]),
            rows_at(layer.WQ, me.z * depth, depth),
            lsem.at[2],
        ),
        pltpu.make_async_copy(
            block_at(wu, 0, depth, me.z * layer.WU.shape[1], layer.WU.shape[1]),
            rows_at(layer.WU, me.z * depth, depth),
            lsem.at[3],
        ),
    ]
    for copy in own:
        copy.start()
    sm[...] = jnp.zeros_like(sm)
    for i, vector in enumerate(vectors):
        sm[i : i + 1] = vector[...].astype(F32)
    me.barrier()

    def tiny(k, slot):
        return send(sm, SM.at[slot], ss.at[k], sr.at[slot], me.seq_peer(k)[1])

    for k in range(1, n):
        tiny(k, me.z).start()
    cq.start()
    cu.start()
    lx.start()
    SM[me.z] = sm[...]
    layer.zero_sums()
    for k in range(1, n):
        tiny(k, me.seq_peer(k)[0]).wait_recv()
    for i in range(n):
        layer.VEC[:, i * part : i * part + part] = SM[i]
    near_k = sorted({1, n - 1})
    for k in near_k:
        cq.share(k)
        cu.share(k)
    lx.forward(1)
    for k in range(1, n):
        if k not in near_k:
            cq.share(k)
            cu.share(k)
    for s in range(2, n - 1):
        lx.forward(s)
    lg.start()
    own[0].wait()
    layer.norm(me.z)
    for k in range(1, n):
        cq.hand(k)
        cu.hand(k)
    own[2].wait()
    own[3].wait()
    cq.finish()
    cu.finish()

    @pl.loop(0, n)
    def _(k):
        j = pick(near, me.z, k)

        @pl.when(k > 0)
        def _():
            lx.arrive(j)
            layer.norm(j)

        layer.qkv(j)
        layer.up(j)
        layer.down(j)

    lg.forward(1)
    blocks = layer.length // layer.block
    for qb in range(blocks):
        layer.attend_part(qb)
        if qb == blocks // 2:
            for s in range(2, n - 1):
                lg.forward(s)

    @pl.loop(0, n)
    def _(k):
        j = pick(far, me.z, k)
        layer.out(j)
        ro.start(j)

    own[1].wait()
    layer.SUMS[4:5] = jnp.sum(layer.G[layer.at(me.z)].astype(F32), axis=0, keepdims=True)

    @pl.loop(0, n)
    def _(k):
        j = pick(near, me.z, k)
        lg.arrive(j)
        layer.mlp_back(j)
        layer.context_grad(j)

        @pl.when(k == n - 2)
        def _():
            ro.step(1)

    def put_dn(i, value):
        pieces = value.shape[0] // red_dn.part.shape[2]
        red_dn.part[0, pl.ds(i * pieces, pieces)] = value.reshape((pieces,) + red_dn.part.shape[2:])

    def put_de(m, value):
        pieces = value.shape[0] // red_de.part.shape[2]
        red_de.part[0, pl.ds(m * pieces, pieces)] = value.reshape((pieces,) + red_de.part.shape[2:])

    def put_u(i, value):
        red_u.part[i] = value.reshape(red_u.part.shape[1:])

    def put_q(i, value):
        red_q.part[i] = value.reshape(red_q.part.shape[1:])

    layer.down_grad(put_dn)
    red_dn.start()
    layer.dense_grad(put_de)
    red_de.start()
    layer.up_grad(put_u)
    red_u.start()
    for t in range(2, 2 * n - 5):
        ro.step(t)
    red_dn.chip_sums()
    red_de.chip_sums()
    red_u.chip_sums()
    copies = []

    def plane(i, red, final):
        red.sum_up()
        copy = pltpu.make_async_copy(red.total.at[0], final.at[me.piece], dsem.at[i])
        copy.start()
        copies.append(copy)

    pairs = layer.heads // 2
    for m in range(pairs):
        layer.attend_back(m)
        if m == 0:
            plane(0, red_dn, fdn)
            plane(1, red_de, fde)
    red_u.sum_up()
    back_u.start()
    for copy in copies:
        copy.wait()
    share_dn.start()
    share_de.start()
    ro.total(layer.X, layer.VEC[4:5] + layer.VEC[5:6], out, layer.TMP)
    ro.finish()

    @pl.loop(0, n)
    def _(k):
        j = pick(far, me.z, k)
        layer.input_back(j)
        rx.start(j)

    layer.qkv_grad(put_q)
    red_q.start()
    cs = part
    v1[...] = layer.SUMS[...]

    def small_z(k, slot):
        other, to = me.seq_peer(k)
        return send(
            v1.at[:, pl.ds(pl.multiple_of(other * cs, cs), cs)],
            v1g.at[slot],
            v1s.at[k],
            v1r.at[slot],
            to,
        )

    def small_dp(k, slot):
        return send(v2m, v2g.at[slot], v2s.at[k], v2r.at[slot], me.dp_peer(k)[1])

    for k in range(1, n):
        small_z(k, me.z).start()
    back_u.wait()
    share_u.start()
    share_dn.hand()
    share_de.hand()
    red_q.chip_sums()
    rx.step(1)
    for k in range(1, n):
        small_z(k, me.seq_peer(k)[0]).wait_recv()
    v1g[me.z] = v1[:, pl.ds(pl.multiple_of(me.z * cs, cs), cs)]
    total = v1g[0]
    for k in range(1, n):
        total = total + v1g[k]
    v2m[...] = jnp.zeros_like(v2m)
    v2m[0:8] = total
    for i in range(layer.BUG.shape[1] // cs):
        v2m[8 + i : 9 + i] = layer.BUG[:, i * cs : i * cs + cs]
    for i in range(layer.BQG.shape[1] // cs):
        v2m[12 + i : 13 + i] = layer.BQG[:, i * cs : i * cs + cs]
    for k in range(1, data):
        small_dp(k, me.d).start()
    red_q.sum_up()
    back_q.start()
    share_u.hand()
    for t in range(2, 2 * n - 5):
        rx.step(t)
    back_q.wait()
    share_q.start()
    for k in range(1, data):
        small_dp(k, me.dp_peer(k)[0]).wait_recv()
    v2g[me.d] = v2m[...]

    def add(i, acc):
        return acc + v2g[i]

    small[...] = lax.fori_loop(1, data, add, v2g[0])
    share_q.hand()
    rx.total(layer.G, None, dx, layer.TMP)
    rx.finish()
    lx.finish()
    lg.finish()
    for k in range(1, n):
        tiny(k, me.z).wait_send()
        small_z(k, me.z).wait_send()
    for k in range(1, data):
        small_dp(k, me.d).wait_send()
    for red in reduces:
        red.finish()
    for share in shares:
        share.finish()
    back_u.finish()
    back_q.finish()


def rotary_constant(length):
    half = ROT_DIM // 2
    freqs = np.float32(10000.0) ** (-np.arange(half, dtype=np.float32) * np.float32(2.0 / ROT_DIM))
    angles = np.arange(length, dtype=np.float32)[:, None] * freqs.astype(np.float32)[None, :]
    cosine, sine = np.cos(angles), np.sin(angles)
    rest = HEAD_DIM - ROT_DIM
    keep, none, gap = np.ones((length, rest)), np.zeros((length, rest)), np.zeros_like(sine)
    same = np.concatenate([cosine, cosine, keep] * 2, axis=1)
    up = np.concatenate([-sine, gap, none] * 2, axis=1)
    down = np.concatenate([gap, sine, none] * 2, axis=1)
    return np.stack([same, up, down]).astype(np.float32)


def whole_layer(n, data, vectors, x, g, wq, wu, w_dense, w_down, b_qkv, b_up):
    rows, width = x.shape
    length = n * rows
    packed, hidden = wq.shape[1] // n, wu.shape[1] // n
    heads = packed // (3 * HEAD_DIM)
    depth = wq.shape[0]
    chunks = 4
    groups = data // PLANE
    vm = pl.BlockSpec(memory_space=pltpu.VMEM)
    hbm = pl.BlockSpec(memory_space=pl.ANY)
    dma = pltpu.SemaphoreType.DMA
    sds = jax.ShapeDtypeStruct
    mem = pltpu.VMEM
    named = layer_scratch(length, width, heads, hidden)
    named.update(
        X=mem((length, width), BF),
        G=mem((length, width), BF),
        WQ=mem((width, packed), BF),
        WU=mem((width, hidden), BF),
        VEC=mem((8, width), F32),
        OP=mem((length, width), BF),
        SUMS=mem((8, width), F32),
        BUG=mem((1, hidden), F32),
        BQG=mem((1, packed), F32),
        TMP=mem((64, width), F32),
    )
    scratch = list(named.values())
    scratch += [mem((n, 8, depth), F32), mem((8, depth), F32)]
    scratch += [dma((4,)), dma((n,)), dma((n,))]
    scratch += [dma((2, n, chunks)), dma((n, chunks))] * 2
    scratch += column_sems(n) + column_sems(n)
    scratch += [mem((n + 1, rows, width), BF)] * 2
    scratch += [dma((n,)), dma((n + 1,))] * 2
    scratch += [mem((8, width), F32), mem((n, 8, depth), F32), dma((n,)), dma((n,))]
    scratch += [mem((16, depth), F32), mem((data, 16, depth), F32), dma((data,)), dma((data,))]
    shapes = [
        (1, hidden // PLANE, width),
        (1, packed // 3 // PLANE, width),
        (n, depth // PLANE, hidden),
        (n, depth // PLANE, packed),
    ]
    for m, rp, cols in shapes:
        scratch += [
            mem((m, PLANE, rp, cols), BF),
            mem((m, CHIPS, rp, cols), BF),
            mem((CHIPS - 1, m, rp, cols), BF),
            mem((m, rp, cols), BF),
            mem((groups, m, rp, cols) if groups > 1 else (1, 1, 16, 128), BF),
            dma,
            dma,
            dma((CHIPS,)),
            dma((CHIPS,)),
            dma((groups,)),
            dma((groups,)),
        ]
    for unused in range(4):
        scratch += [dma((CHIPS,))] * 4
    scratch += [dma((n,)), dma((n,)), dma] * 2
    scratch += [dma((4,))]
    outs = [
        sds((rows, width), BF),
        sds((rows, width), BF),
        sds((16, depth), F32),
        sds((PLANE, depth // PLANE, hidden * n), BF),
        sds((PLANE, depth // PLANE, packed * n), BF),
        sds((PLANE, hidden // PLANE, width), BF),
        sds((PLANE, packed // 3 // PLANE, width), BF),
    ]
    return pl.pallas_call(
        functools.partial(layer_kernel, n, data, chunks, list(named)),
        out_shape=outs,
        in_specs=[vm] * VECTORS + [hbm] * 4 + [vm] * 5,
        out_specs=[vm] * 3 + [hbm] * 4,
        scratch_shapes=scratch,
        compiler_params=pltpu.CompilerParams(
            collective_id=2, has_side_effects=True, vmem_limit_bytes=67043328
        ),
        name="layer",
    )(*vectors, x, g, wq, wu, w_dense, w_down, b_qkv, b_up, rotary_constant(length))


def fits(n, data, tokens, qkv, up):
    unused, rows, width = tokens
    length, depth = n * rows, qkv[0]
    return (
        length * (width + up[1] // n) <= 1024 * 2048
        and rows == 256
        and depth == 256
        and up[1] // n % 256 == 0
        and qkv[1] // n % (6 * HEAD_DIM) == 0
    )


def per_device(
    n,
    data,
    layer_input,
    attn_gain,
    attn_shift,
    mlp_gain,
    mlp_shift,
    qkv_weight,
    qkv_bias,
    dense_weight,
    dense_bias,
    up_weight,
    up_bias,
    down_weight,
    down_bias,
    out_grad,
):
    unused, rows, width = layer_input.shape
    x = layer_input.reshape(rows, width)
    g = out_grad.reshape(rows, width)
    part = width // n
    if fits(n, data, layer_input.shape, qkv_weight.shape, up_weight.shape):
        vectors = [
            v[None] for v in (attn_gain, attn_shift, mlp_gain, mlp_shift, dense_bias, down_bias)
        ]
        out, dx, tiny, fu, fq, fdn, fde = whole_layer(
            n, data, vectors, x, g, qkv_weight, up_weight, dense_weight, down_weight,
            qkv_bias[None], up_bias[None],
        )
    else:
        small = jnp.stack(
            [attn_gain, attn_shift, mlp_gain, mlp_shift, dense_bias, down_bias] + [attn_gain] * 2
        ).astype(F32)
        SM, X, G, WQ, WU = gather(n, data, small, x, g, qkv_weight, up_weight)
        vectors = jnp.swapaxes(SM, 0, 1).reshape(8, width)
        bias = (vectors[4] + vectors[5])[None]
        OP, DX, sums, bu, bq, UG, QG, DnG, DeG = middle(
            X, G, WQ, WU, dense_weight, down_weight, qkv_bias, up_bias, vectors
        )
        v1 = jnp.concatenate(
            [sums, jnp.sum(g.astype(F32), axis=0)[None], jnp.zeros((3, width), F32)], axis=0
        )
        v2 = jnp.concatenate(
            [bu.reshape(4, part), bq.reshape(3, part), jnp.zeros((1, part), F32)]
        )
        out, dx, tiny, fu, fq, fdn, fde = reduce_all(
            n, data, OP, DX, v1, v2, bias, x, g, UG, QG, DnG, DeG
        )
    return (
        out.reshape(layer_input.shape),
        dx.reshape(layer_input.shape),
        tiny[0],
        tiny[1],
        tiny[2],
        tiny[3],
        fq.reshape(part, -1).astype(F32),
        tiny[12:15].reshape(-1),
        fde.reshape(-1, width).astype(F32),
        tiny[4],
        fu.reshape(part, -1).astype(F32),
        tiny[8:12].reshape(-1),
        fdn.reshape(-1, width).astype(F32),
        tiny[4],
    )


def solution(mesh):
    tokens, row, vector = P("dp", "seq", None), P("seq", None), P("seq")
    in_specs = (tokens,) + (vector,) * 4 + (row, vector) * 4 + (tokens,)
    out_specs = (tokens, tokens) + (vector,) * 4 + (row, vector) * 4
    return jax.shard_map(
        functools.partial(per_device, mesh.shape["seq"], mesh.shape["dp"]),
        mesh=mesh,
        in_specs=in_specs,
        out_specs=out_specs,
        check_vma=False,
    )
```

```python
import functools
import math

import jax
import jax.numpy as jnp
import numpy as np
from jax import lax
from jax.experimental import pallas as pl
from jax.experimental.pallas import tpu as pltpu
from jax.sharding import PartitionSpec as P

HEADS = 16
HEAD_DIM = 64
ROT_DIM = 16
PLANE = 8
CHIPS = 4
epsilon = 1e-05
mask_fill = -1e30
MESH = pl.DeviceIdType.MESH
BF = jnp.bfloat16
F32 = jnp.float32


def rows_at(ref, start, count):
    return ref.at[pl.ds(pl.multiple_of(start, count), count)]


def block_at(ref, row, rows, col, cols):
    return ref.at[
        pl.ds(pl.multiple_of(row, rows), rows), pl.ds(pl.multiple_of(col, cols), cols)
    ]


class Place:
    def __init__(self, n, data):
        self.n, self.data = n, data
        self.d = lax.axis_index("dp")
        self.z = lax.axis_index("seq")
        self.base = self.d // PLANE * PLANE
        self.r = lax.rem(self.d, PLANE)
        self.ch = self.r // 2
        self.c = lax.rem(self.r, 2)
        self.piece = self.c * CHIPS + self.ch

    def seq_peer(self, k):
        other = lax.rem(self.z + k, self.n)
        return other, (self.d, other)

    def chip_peer(self, k):
        other = lax.rem(self.ch + k, CHIPS)
        return other, (self.base + other * 2 + self.c, self.z)

    def beside(self, way):
        other = self.ch + 1 - 2 * lax.rem(self.ch, 2) if way == 0 else lax.rem(self.ch + 2, CHIPS)
        return other, (self.base + other * 2 + self.c, self.z)

    def partner(self):
        return (self.base + self.ch * 2 + 1 - self.c, self.z)

    def dp_peer(self, k):
        other = lax.rem(self.d + k, self.data)
        return other, (other, self.z)

    def barrier(self):
        sem = pltpu.get_barrier_semaphore()
        for k in range(1, self.n):
            pl.semaphore_signal(sem, inc=1, device_id=self.seq_peer(k)[1], device_id_type=MESH)
        for k in range(1, self.data):
            pl.semaphore_signal(sem, inc=1, device_id=self.dp_peer(k)[1], device_id_type=MESH)
        pl.semaphore_wait(sem, self.n - 1 + self.data - 1)


def send(src, dst, ssem, rsem, to):
    return pltpu.make_async_remote_copy(
        src_ref=src, dst_ref=dst, send_sem=ssem, recv_sem=rsem, device_id=to, device_id_type=MESH
    )


class LineGather:
    def __init__(self, me, shard, full, rows, chunks, ssem, rsem):
        self.me, self.shard, self.full = me, shard, full
        self.rows, self.chunks, self.ssem, self.rsem = rows, chunks, ssem, rsem

    def part(self, owner, c):
        size = self.rows // self.chunks
        return rows_at(self.full, owner * self.rows + c * size, size)

    def copy(self, src, owner, c, way):
        me = self.me
        to = jnp.minimum(me.z + 1, me.n - 1) if way == 0 else jnp.maximum(me.z - 1, 0)
        return send(
            src,
            self.part(owner, c),
            self.ssem.at[way, owner, c],
            self.rsem.at[owner, c],
            (me.d, to),
        )

    def start(self):
        me = self.me
        size = self.rows // self.chunks
        for c in range(self.chunks):
            src = rows_at(self.shard, c * size, size)

            @pl.when(me.z < me.n - 1)
            def _():
                self.copy(src, me.z, c, 0).start()

            @pl.when(me.z > 0)
            def _():
                self.copy(src, me.z, c, 1).start()

    def step(self, s, c):
        me = self.me

        @pl.when(me.z >= s)
        def _():
            owner = me.z - s
            copy = self.copy(self.part(owner, c), owner, c, 0)
            copy.wait_recv()

            @pl.when(me.z < me.n - 1)
            def _():
                copy.start()

        @pl.when(me.z + s < me.n)
        def _():
            owner = me.z + s
            copy = self.copy(self.part(owner, c), owner, c, 1)
            copy.wait_recv()

            @pl.when(me.z > 0)
            def _():
                copy.start()

    def forward(self, s):
        me = self.me
        inner = (me.z > 0) & (me.z < me.n - 1)
        for c in range(self.chunks):
            for way, valid, owner in ((0, me.z >= s, me.z - s), (1, me.z + s < me.n, me.z + s)):

                @pl.when(inner & valid)
                def _():
                    copy = self.copy(self.part(owner, c), owner, c, way)
                    copy.wait_recv()
                    copy.start()

    def arrive(self, owner):
        me = self.me

        @pl.when(((me.z == 0) | (me.z == me.n - 1)) & (owner != me.z))
        def _():
            for c in range(self.chunks):
                self.copy(self.part(owner, c), owner, c, 0).wait_recv()

    def finish(self):
        me = self.me
        for c in range(self.chunks):
            for owner in range(me.n):

                @pl.when((me.z < me.n - 1) & (owner <= me.z))
                def _():
                    self.copy(self.part(owner, c), owner, c, 0).wait_send()

                @pl.when((me.z > 0) & (owner >= me.z))
                def _():
                    self.copy(self.part(owner, c), owner, c, 1).wait_send()


class ColumnGather:
    def __init__(self, me, shard, full, sems):
        self.me, self.shard, self.full = me, shard, full
        self.depth = shard.shape[0]
        self.rp = self.depth // PLANE
        self.cols = full.shape[1]
        self.zs, self.zr, self.ps, self.pr, self.fs = sems

    def part(self, src_z, piece):
        return rows_at(self.full, (src_z * PLANE + piece) * self.rp, self.rp)

    def across(self, k):
        me = self.me
        other, to = me.seq_peer(k)
        src = block_at(self.shard, me.piece * self.rp, self.rp, other * self.cols, self.cols)
        return send(src, self.part(me.z, me.piece), self.zs.at[k], self.zr.at[me.n - k], to)

    def came(self, k):
        me = self.me
        other, to = me.seq_peer(k)
        src = block_at(self.shard, me.piece * self.rp, self.rp, other * self.cols, self.cols)
        return send(src, self.part(other, me.piece), self.zs.at[k], self.zr.at[k], to)

    def shares(self, k):
        me = self.me
        other, unused = me.seq_peer(k)
        mine = self.part(other, me.piece)
        for j in range(1, CHIPS):
            to = me.chip_peer(j)[1]
            yield send(mine, mine, self.ps.at[k, j], self.pr.at[k, CHIPS - j], to)
        yield send(mine, mine, self.ps.at[k, 0], self.fs.at[1, k, 0], me.partner())

    def handed(self, k, j):
        me = self.me
        other, unused = me.seq_peer(k)
        chip = me.chip_peer(j)[0]
        return self.part(other, me.c * CHIPS + chip), self.part(other, (1 - me.c) * CHIPS + chip)

    def start(self):
        for k in range(self.me.n - 1, 0, -1):
            self.across(k).start()

    def share(self, k):
        self.came(k).wait_recv()
        for copy in self.shares(k):
            copy.start()

    def hand(self, k):
        me = self.me
        for j in range(1, CHIPS):
            got, unused = self.handed(k, j)
            send(got, got, self.ps.at[k, j], self.pr.at[k, j], me.chip_peer(j)[1]).wait_recv()
            send(got, got, self.fs.at[0, k, j], self.fs.at[1, k, j], me.partner()).start()

    def finish(self):
        me = self.me
        for k in range(1, me.n):
            self.across(k).wait_send()
            for copy in self.shares(k):
                copy.wait_send()
            other, unused = me.seq_peer(k)
            for j in range(CHIPS):
                unused, got = self.handed(k, j)
                copy = send(got, got, self.fs.at[0, k, j], self.fs.at[1, k, j], me.partner())
                copy.wait_recv()
                if j > 0:
                    copy.wait_send()


def column_sems(n):
    dma = pltpu.SemaphoreType.DMA
    return [dma((n,)), dma((n,)), dma((n, CHIPS)), dma((n, CHIPS)), dma((2, n, CHIPS))]


def gather_kernel(n, data, chunks, sm, x, g, wq, wu, SM, X, G, WQ, WU, *sems):
    me = Place(n, data)
    rows = x.shape[0]
    lsem, ss, sr, xs, xr, gs, gr = sems[:7]
    me.barrier()
    cq, cu = ColumnGather(me, wq, WQ, sems[7:12]), ColumnGather(me, wu, WU, sems[12:17])
    lx = LineGather(me, x, X, rows, chunks, xs, xr)
    lg = LineGather(me, g, G, rows, chunks, gs, gr)
    depth = wq.shape[0]
    own = [
        pltpu.make_async_copy(sm, SM.at[me.z], lsem.at[0]),
        pltpu.make_async_copy(x, rows_at(X, me.z * rows, rows), lsem.at[1]),
        pltpu.make_async_copy(g, rows_at(G, me.z * rows, rows), lsem.at[2]),
        pltpu.make_async_copy(
            block_at(wq, 0, depth, me.z * WQ.shape[1], WQ.shape[1]),
            rows_at(WQ, me.z * depth, depth),
            lsem.at[3],
        ),
        pltpu.make_async_copy(
            block_at(wu, 0, depth, me.z * WU.shape[1], WU.shape[1]),
            rows_at(WU, me.z * depth, depth),
            lsem.at[4],
        ),
    ]
    for copy in own:
        copy.start()

    def small(k, slot):
        return send(sm, SM.at[slot], ss.at[k], sr.at[slot], me.seq_peer(k)[1])

    for k in range(1, n):
        small(k, me.z).start()
    cq.start()
    cu.start()
    lx.start()
    lg.start()
    near = sorted({1, n - 1})
    for k in near:
        cq.share(k)
        cu.share(k)
    for c in range(chunks):
        lx.step(1, c)
    for k in range(1, n):
        if k not in near:
            cq.share(k)
            cu.share(k)
    for s in range(2, n):
        for c in range(chunks):
            lx.step(s, c)
    for k in range(1, n):
        cq.hand(k)
        cu.hand(k)
    for s in range(1, n):
        for c in range(chunks):
            lg.step(s, c)
    for k in range(1, n):
        small(k, me.z).wait_send()
        small(k, me.seq_peer(k)[0]).wait_recv()
    cq.finish()
    cu.finish()
    lx.finish()
    lg.finish()
    for copy in own:
        copy.wait()


def gather(n, data, sm, x, g, wq, wu):
    rows, width = x.shape
    depth = wq.shape[0]
    chunks = 4
    vm = pl.BlockSpec(memory_space=pltpu.VMEM)
    dma = pltpu.SemaphoreType.DMA
    sds = jax.ShapeDtypeStruct
    return pl.pallas_call(
        functools.partial(gather_kernel, n, data, chunks),
        out_shape=[
            sds((n,) + sm.shape, sm.dtype),
            sds((n * rows, width), x.dtype),
            sds((n * rows, width), x.dtype),
            sds((n * depth, wq.shape[1] // n), wq.dtype),
            sds((n * depth, wu.shape[1] // n), wu.dtype),
        ],
        in_specs=[vm] * 5,
        out_specs=[vm] * 5,
        scratch_shapes=[
            dma((5,)),
            dma((n,)),
            dma((n,)),
            dma((2, n, chunks)),
            dma((n, chunks)),
            dma((2, n, chunks)),
            dma((n, chunks)),
        ]
        + column_sems(n)
        + column_sems(n),
        compiler_params=pltpu.CompilerParams(
            collective_id=0, has_side_effects=True, vmem_limit_bytes=60 << 20
        ),
        name="gather",
    )(sm, x, g, wq, wu)


class RowReduce:
    def __init__(self, me, part, got, ssem, rsem):
        self.me, self.part, self.got, self.ssem, self.rsem = me, part, got, ssem, rsem
        self.rows = got.shape[1]

    def copy(self, k, slot):
        other, to = self.me.seq_peer(k)
        return send(
            rows_at(self.part, other * self.rows, self.rows),
            self.got.at[slot],
            self.ssem.at[k],
            self.rsem.at[slot],
            to,
        )

    def start(self):
        for k in range(1, self.me.n):
            self.copy(k, self.me.z).start()

    def wait(self):
        for k in range(1, self.me.n):
            self.copy(k, self.me.seq_peer(k)[0]).wait_recv()

    def finish(self):
        for k in range(1, self.me.n):
            self.copy(k, self.me.z).wait_send()


def halves(cols):
    middle = cols // 2 // 128 * 128
    return slice(0, middle), slice(middle, cols)


class GradReduce:
    def __init__(self, me, part, half, near, far, total, groups, sems):
        self.me, self.part, self.half, self.near, self.far = me, part, half, near, far
        self.total, self.groups = total, groups
        self.hs, self.hr, self.ns, self.nr, self.fs, self.fr, self.gs, self.gr = sems
        self.cols = halves(part.shape[3])

    def swap(self):
        me = self.me
        return send(
            self.part.at[:, pl.ds((1 - me.c) * CHIPS, CHIPS)],
            self.half,
            self.hs,
            self.hr,
            me.partner(),
        )

    def piece(self, way, index, other):
        me = self.me
        a, b = me.ch // 2, lax.rem(me.ch, 2)
        if way == 0:
            chip = index * 2 + (1 - b if other else b)
        else:
            chip = (1 - a if other else a) * 2 + index
        return me.c * CHIPS + chip

    def first(self, way, index):
        return send(
            self.part.at[:, self.piece(way, index, True), :, self.cols[way]],
            self.near[way].at[index],
            self.ns.at[way, index],
            self.nr.at[way, index],
            self.me.beside(way)[1],
        )

    def second(self, way):
        a, b = self.me.ch // 2, lax.rem(self.me.ch, 2)
        other = 1 - a if way == 0 else 1 - b
        return send(
            self.part.at[:, self.piece(way, other, False), :, self.cols[way]],
            self.far[way],
            self.fs.at[way],
            self.fr.at[way],
            self.me.beside(1 - way)[1],
        )

    def start(self):
        self.swap().start()

    def chip_sums(self):
        me = self.me
        self.swap().wait_recv()

        @pl.loop(0, CHIPS)
        def _(j):
            for m in range(self.half.shape[0]):
                self.part[m, me.c * CHIPS + j] = (
                    self.part[m, me.c * CHIPS + j].astype(F32) + self.half[m, j].astype(F32)
                ).astype(BF)

        for way in range(2):
            for index in range(2):
                self.first(way, index).start()

    def pair_sums(self):
        for way in range(2):
            for index in range(2):
                self.first(way, index).wait_recv()
            cols = self.cols[way]
            for index in range(2):
                piece = self.piece(way, index, False)
                for m in range(self.half.shape[0]):
                    self.part[m, piece, :, cols] = (
                        self.part[m, piece, :, cols].astype(F32)
                        + self.near[way][index, m].astype(F32)
                    ).astype(BF)
            self.second(way).start()

    def to_group(self, k, slot):
        me = self.me
        count = me.data // PLANE
        other = lax.rem(me.d // PLANE + k, count)
        return send(
            self.total,
            self.groups.at[slot],
            self.gs.at[k],
            self.gr.at[slot],
            (other * PLANE + me.r, me.z),
        )

    def sum_up(self):
        me = self.me
        for way in range(2):
            self.second(way).wait_recv()
            cols = self.cols[way]
            for m in range(self.total.shape[0]):
                self.total[m, :, cols] = (
                    self.part[m, me.piece, :, cols].astype(F32) + self.far[way][m].astype(F32)
                ).astype(BF)
        count = me.data // PLANE
        if count > 1:
            own = me.d // PLANE
            for k in range(1, count):
                self.to_group(k, own).start()
            for k in range(1, count):
                self.to_group(k, lax.rem(own + k, count)).wait_recv()
                self.to_group(k, own).wait_send()
            self.groups[own] = self.total[...]
            total = self.groups[0].astype(F32)
            for e in range(1, count):
                total = total + self.groups[e].astype(F32)
            self.total[...] = total.astype(BF)

    def finish(self):
        self.swap().wait_send()
        for way in range(2):
            for index in range(2):
                self.first(way, index).wait_send()
            self.second(way).wait_send()


def reduce_scratch(m, rp, cols, groups):
    mem, dma = pltpu.VMEM, pltpu.SemaphoreType.DMA
    widths = [part.stop - part.start for part in halves(cols)]
    return (
        [mem((m, CHIPS, rp, cols), BF)]
        + [mem((2, m, rp, width), BF) for width in widths]
        + [mem((m, rp, width), BF) for width in widths]
        + [
            mem((m, rp, cols), BF),
            mem((groups, m, rp, cols) if groups > 1 else (1, 1, 16, 128), BF),
            dma,
            dma,
            dma((2, 2)),
            dma((2, 2)),
            dma((2,)),
            dma((2,)),
            dma((groups,)),
            dma((groups,)),
        ]
    )


def take_reduce(me, part, take):
    half, near0, near1, far0, far1, total, groups = take(7)
    return GradReduce(me, part, half, (near0, near1), (far0, far1), total, groups, take(8))


class GradShare:
    def __init__(self, me, final, sems):
        self.me, self.final = me, final
        self.ss, self.sr, self.fs, self.fr, self.hs, self.hr = sems
        self.cols = halves(final.shape[2])

    def own(self, way):
        mine = self.final.at[self.me.piece]
        return send(mine, mine, self.ss.at[way], self.sr.at[way], self.me.beside(way)[1])

    def to_partner(self, index, chip, core):
        got = self.final.at[core * CHIPS + chip]
        return send(got, got, self.hs.at[index], self.hr.at[index], self.me.partner())

    def onward(self, way, chip):
        got = self.final.at[self.me.c * CHIPS + chip, :, self.cols[way]]
        return send(got, got, self.fs.at[way], self.fr.at[way], self.me.beside(1 - way)[1])

    def across(self):
        return CHIPS - 1 - self.me.ch

    def start(self):
        for way in range(2):
            self.own(way).start()
        self.to_partner(0, self.me.ch, self.me.c).start()

    def forward(self):
        me = self.me
        for way in range(2):
            chip = me.beside(way)[0]
            got = self.final.at[me.c * CHIPS + chip]
            send(got, got, self.ss.at[way], self.sr.at[way], me.beside(way)[1]).wait_recv()
            self.onward(way, chip).start()
            self.to_partner(1 + way, chip, me.c).start()

    def hand(self):
        for way in range(2):
            self.onward(way, self.across()).wait_recv()
        self.to_partner(3, self.across(), self.me.c).start()

    def finish(self):
        me = self.me
        chips = [me.ch, me.beside(0)[0], me.beside(1)[0], self.across()]
        for way in range(2):
            self.own(way).wait_send()
            self.onward(way, chips[1 + way]).wait_send()
        for index, chip in enumerate(chips):
            self.to_partner(index, chip, me.c).wait_send()
            self.to_partner(index, chip, 1 - me.c).wait_recv()


def share_sems():
    dma = pltpu.SemaphoreType.DMA
    return [dma((2,))] * 4 + [dma((4,))] * 2


class RowsBack:
    def __init__(self, me, total, final, ssem, rsem, lsem):
        self.me, self.total, self.final = me, total, final
        self.ssem, self.rsem, self.lsem = ssem, rsem, lsem

    def place(self, src_z):
        cols = self.total.shape[2]
        return self.final.at[
            self.me.piece, :, pl.ds(pl.multiple_of(src_z * cols, cols), cols)
        ]

    def copy(self, k, slot):
        other, to = self.me.seq_peer(k)
        return send(
            self.total.at[other], self.place(slot), self.ssem.at[k], self.rsem.at[slot], to
        )

    def own(self):
        me = self.me
        return pltpu.make_async_copy(self.total.at[me.z], self.place(me.z), self.lsem)

    def start(self):
        for k in range(1, self.me.n):
            self.copy(k, self.me.z).start()
        self.own().start()

    def wait(self):
        me = self.me
        for k in range(1, me.n):
            self.copy(k, me.seq_peer(k)[0]).wait_recv()
        self.own().wait()

    def finish(self):
        for k in range(1, self.me.n):
            self.copy(k, self.me.z).wait_send()


def reduce_kernel(n, data, *refs):
    (OP, DX, v1, v2, bias, x, g, UG, QG, DnG, DeG) = refs[:11]
    out, dx, small, fu, fq, fdn, fde = refs[11:18]
    scratch = list(refs[18:])
    me = Place(n, data)

    def take(count):
        got = scratch[:count]
        del scratch[:count]
        return got

    og, xg, zs, zr, v1g, v1s, v1r, v2m, v2g, v2s, v2r = take(11)
    reduces = []
    for part in (DnG, DeG, UG, QG):
        reduces.append(take_reduce(me, part, take))
    red_dn, red_de, red_u, red_q = reduces
    shares = [GradShare(me, final, take(6)) for final in (fdn, fde, fu, fq)]
    back_u = RowsBack(me, red_u.total, fu, *take(3))
    back_q = RowsBack(me, red_q.total, fq, *take(3))
    (dsem,) = take(1)
    assert not scratch
    ro = RowReduce(me, OP, og, zs.at[0], zr.at[0])
    rx = RowReduce(me, DX, xg, zs.at[1], zr.at[1])
    me.barrier()
    cs = v1g.shape[2]

    def small_z(k, slot):
        other, to = me.seq_peer(k)
        return send(
            v1.at[:, pl.ds(pl.multiple_of(other * cs, cs), cs)],
            v1g.at[slot],
            v1s.at[k],
            v1r.at[slot],
            to,
        )

    def small_dp(k, slot):
        return send(v2m, v2g.at[slot], v2s.at[k], v2r.at[slot], me.dp_peer(k)[1])

    for k in range(1, n):
        small_z(k, me.z).start()
    for red in reduces:
        red.start()
    ro.start()
    rx.start()
    for red in reduces:
        red.chip_sums()
    for red in reduces:
        red.pair_sums()
    for k in range(1, n):
        small_z(k, me.seq_peer(k)[0]).wait_recv()
    v1g[me.z] = v1[:, pl.ds(pl.multiple_of(me.z * cs, cs), cs)]
    total = v1g[0]
    for k in range(1, n):
        total = total + v1g[k]
    v2m[0:8] = total
    v2m[8:16] = v2[...]
    for k in range(1, data):
        small_dp(k, me.d).start()
    own = []
    for i, (red, final) in enumerate(((red_dn, fdn), (red_de, fde))):
        red.sum_up()
        copy = pltpu.make_async_copy(red.total.at[0], final.at[me.piece], dsem.at[i])
        copy.start()
        own.append(copy)
    red_u.sum_up()
    back_u.start()
    red_q.sum_up()
    back_q.start()
    for copy in own:
        copy.wait()
    shares[0].start()
    shares[1].start()
    back_u.wait()
    shares[2].start()
    back_q.wait()
    shares[3].start()
    for share in shares:
        share.forward()
    for share in shares:
        share.hand()
    for k in range(1, data):
        small_dp(k, me.dp_peer(k)[0]).wait_recv()
    v2g[me.d] = v2m[...]

    def add(i, acc):
        return acc + v2g[i]

    small[...] = lax.fori_loop(1, data, add, v2g[0])
    rows = x.shape[0]
    for red, base, result, extra in ((ro, x, out, bias), (rx, g, dx, None)):
        red.wait()
        step = rows // 4

        @pl.loop(0, 4)
        def _(i):
            at = pl.ds(pl.multiple_of(i * step, step), step)
            mine = pl.ds(pl.multiple_of(me.z * rows + i * step, step), step)
            acc = base[at].astype(F32) + red.part[mine].astype(F32)
            for k in range(1, n):
                acc = acc + red.got[me.seq_peer(k)[0], at].astype(F32)
            if extra is not None:
                acc = acc + extra[...]
            result[at] = acc.astype(BF)

        red.finish()
    for k in range(1, n):
        small_z(k, me.z).wait_send()
    for k in range(1, data):
        small_dp(k, me.d).wait_send()
    for red in reduces:
        red.finish()
    for share in shares:
        share.finish()
    back_u.finish()
    back_q.finish()


def reduce_all(n, data, OP, DX, v1, v2, bias, x, g, UG, QG, DnG, DeG):
    vm = pl.BlockSpec(memory_space=pltpu.VMEM)
    dma = pltpu.SemaphoreType.DMA
    sds = jax.ShapeDtypeStruct
    rows, width = x.shape
    groups = data // PLANE
    parts = []
    for whole in (DnG, DeG):
        lead, cols = whole.shape
        parts.append(whole.reshape(1, PLANE, lead // PLANE, cols))
    for whole in (UG, QG):
        lead, cols = whole.shape
        parts.append(whole.reshape(n, PLANE, lead // n // PLANE, cols))
    dn, de, u, q = parts
    scratch = [
        pltpu.VMEM((n, rows, width), BF),
        pltpu.VMEM((n, rows, width), BF),
        dma((2, n)),
        dma((2, n)),
        pltpu.VMEM((n, 8, width // n), F32),
        dma((n,)),
        dma((n,)),
        pltpu.VMEM((16, width // n), F32),
        pltpu.VMEM((data, 16, width // n), F32),
        dma((data,)),
        dma((data,)),
    ]
    for part in (dn, de, u, q):
        m, unused, rp, cols = part.shape
        scratch += reduce_scratch(m, rp, cols, groups)
    for unused in range(4):
        scratch += share_sems()
    scratch += [dma((n,)), dma((n,)), dma] * 2
    scratch += [dma((2,))]
    outs = [
        sds((rows, width), BF),
        sds((rows, width), BF),
        sds((16, width // n), F32),
        sds((PLANE, u.shape[2], u.shape[3] * n), BF),
        sds((PLANE, q.shape[2], q.shape[3] * n), BF),
        sds((PLANE,) + dn.shape[2:], BF),
        sds((PLANE,) + de.shape[2:], BF),
    ]
    return pl.pallas_call(
        functools.partial(reduce_kernel, n, data),
        out_shape=outs,
        in_specs=[vm] * 11,
        out_specs=[vm] * 7,
        scratch_shapes=scratch,
        compiler_params=pltpu.CompilerParams(
            collective_id=1, has_side_effects=True, vmem_limit_bytes=63 << 20
        ),
        name="reduce",
    )(OP, DX, v1, v2, bias, x, g, u, q, dn, de)


def layer_norm_parts(token_rows):
    average = jnp.mean(token_rows, axis=-1, keepdims=True)
    centered = token_rows - average
    variance = jnp.mean(centered * centered, axis=-1, keepdims=True)
    inverse = lax.rsqrt(variance + epsilon)
    return centered * inverse, inverse


def rotate(packed, positions, sign):
    half = ROT_DIM // 2
    freqs = 10000.0 ** (-jnp.arange(half, dtype=F32) * 2.0 / ROT_DIM)
    angles = positions.astype(F32)[:, None] * freqs[None, :]
    cosine = jnp.cos(angles)[:, None, None, :]
    sine = jnp.sin(angles)[:, None, None, :] * sign
    first = packed[..., :half]
    second = packed[..., half:ROT_DIM]
    turned = jnp.concatenate(
        [first * cosine - second * sine, second * cosine + first * sine, packed[..., ROT_DIM:]],
        axis=-1,
    )
    select = (jnp.arange(3) < 2)[:, None]
    return jnp.where(select, turned, packed)


def middle(X, G, WQ, WU, w_dense, w_down, b_qkv, b_up, vectors):
    length, width = X.shape
    heads = WQ.shape[1] // (3 * HEAD_DIM)
    scale = HEAD_DIM ** (-0.5)
    gain_one, shift_one, gain_two, shift_two = (vectors[i] for i in range(4))
    xhat, inverse = layer_norm_parts(X.astype(F32))
    norm_one = (xhat * gain_one + shift_one).astype(BF)
    norm_two = (xhat * gain_two + shift_two).astype(BF)
    packed = jnp.dot(norm_one, WQ, preferred_element_type=F32) + b_qkv.astype(F32)
    positions = jnp.arange(length, dtype=jnp.int32)
    packed = rotate(packed.reshape(length, heads, 3, HEAD_DIM), positions, 1.0).astype(BF)
    query, keys, values = packed[:, :, 0], packed[:, :, 1], packed[:, :, 2]
    scores = jnp.einsum("qhd,khd->hqk", query, keys, preferred_element_type=F32) * scale
    allowed = positions[:, None] >= positions[None, :]
    probs = jax.nn.softmax(jnp.where(allowed, scores, mask_fill), axis=-1)
    low = probs.astype(BF)
    context = jnp.einsum("hqk,khd->qhd", low, values, preferred_element_type=F32)
    context = context.astype(BF).reshape(length, heads * HEAD_DIM)
    hidden = jnp.dot(norm_two, WU, preferred_element_type=F32) + b_up.astype(F32)
    active = jax.nn.gelu(hidden, approximate=False).astype(BF)
    out = jnp.dot(context, w_dense, preferred_element_type=F32) + jnp.dot(
        active, w_down, preferred_element_type=F32
    )
    down_grad = jnp.einsum("tf,to->fo", active, G, preferred_element_type=F32)
    dense_grad = jnp.einsum("ti,to->io", context, G, preferred_element_type=F32)
    active_grad = jnp.einsum("to,fo->tf", G, w_down, preferred_element_type=F32)
    unused, pull = jax.vjp(lambda v: jax.nn.gelu(v, approximate=False), hidden)
    hidden_grad = pull(active_grad)[0].astype(BF)
    up_bias_grad = jnp.sum(hidden_grad.astype(F32), axis=0)
    up_grad = jnp.einsum("ti,tf->if", norm_two, hidden_grad, preferred_element_type=F32)
    norm_two_grad = jnp.einsum("tf,if->ti", hidden_grad, WU, preferred_element_type=F32)
    context_grad = jnp.einsum("to,io->ti", G, w_dense, preferred_element_type=F32).astype(BF)
    context_grad = context_grad.reshape(length, heads, HEAD_DIM)
    prob_grad = jnp.einsum("qhd,khd->hqk", context_grad, values, preferred_element_type=F32)
    weighted = jnp.sum(probs * prob_grad, axis=-1, keepdims=True)
    score_grad = (probs * (prob_grad - weighted)).astype(BF)
    query_grad = jnp.einsum("hqk,khd->qhd", score_grad, keys, preferred_element_type=F32) * scale
    key_grad = jnp.einsum("hqk,qhd->khd", score_grad, query, preferred_element_type=F32) * scale
    value_grad = jnp.einsum("hqk,qhd->khd", low, context_grad, preferred_element_type=F32)
    rotated_grad = jnp.stack([query_grad, key_grad, value_grad], axis=2).astype(BF).astype(F32)
    packed_grad = rotate(rotated_grad, positions, -1.0).reshape(length, -1).astype(BF)
    qkv_bias_grad = jnp.sum(packed_grad.astype(F32), axis=0)
    qkv_grad = jnp.einsum("ti,tj->ij", norm_one, packed_grad, preferred_element_type=F32)
    norm_one_grad = jnp.einsum("tj,ij->ti", packed_grad, WQ, preferred_element_type=F32)
    u = norm_one_grad * gain_one + norm_two_grad * gain_two
    mean_u = jnp.mean(u, axis=-1, keepdims=True)
    mean_ux = jnp.mean(u * xhat, axis=-1, keepdims=True)
    dx = inverse * (u - mean_u - xhat * mean_ux)
    sums = jnp.stack(
        [
            jnp.sum(norm_one_grad * xhat, axis=0),
            jnp.sum(norm_one_grad, axis=0),
            jnp.sum(norm_two_grad * xhat, axis=0),
            jnp.sum(norm_two_grad, axis=0),
        ]
    )
    return (
        out.astype(BF),
        dx.astype(BF),
        sums,
        up_bias_grad,
        qkv_bias_grad,
        up_grad.astype(BF),
        qkv_grad.astype(BF),
        down_grad.astype(BF),
        dense_grad.astype(BF),
    )


NN = (((1,), (0,)), ((), ()))
NT = (((1,), (1,)), ((), ()))
TN = (((0,), (0,)), ((), ()))
ROOT_HALF = 0.7071067811865476
PDF_SCALE = 0.3989422804014327


def dot(left, right, dims=NN):
    return lax.dot_general(left, right, dims, preferred_element_type=F32)


def rotary_tables(length):
    half = ROT_DIM // 2
    freqs = 10000.0 ** (-jnp.arange(half, dtype=F32) * 2.0 / ROT_DIM)
    angles = jnp.arange(length, dtype=jnp.int32).astype(F32)[:, None] * freqs[None, :]
    cosine, sine = jnp.cos(angles), jnp.sin(angles)
    rest = HEAD_DIM - ROT_DIM
    keep, none, gap = jnp.ones((length, rest)), jnp.zeros((length, rest)), jnp.zeros_like(sine)
    same = jnp.concatenate([cosine, cosine, keep] * 2, axis=1)
    up = jnp.concatenate([-sine, gap, none] * 2, axis=1)
    down = jnp.concatenate([gap, sine, none] * 2, axis=1)
    return jnp.stack([same, up, down]).astype(F32)


class Layer:
    def __init__(self, rows, refs):
        self.rows = rows
        for name, ref in refs.items():
            setattr(self, name, ref)
        self.length, self.width = self.X.shape
        self.heads = self.Q.shape[0]
        self.block = min(256, self.length)

    def at(self, j, rows=None, part=0):
        rows = rows or self.rows
        return pl.ds(pl.multiple_of(j * self.rows + part * rows, rows), rows)

    def norm(self, j):
        step = 64

        @pl.loop(0, self.rows // step)
        def _(i):
            at = self.at(j, step, i)
            x = self.X[at].astype(F32)
            average = jnp.mean(x, axis=-1, keepdims=True)
            centered = x - average
            variance = jnp.mean(centered * centered, axis=-1, keepdims=True)
            inverse = lax.rsqrt(variance + epsilon)
            xhat = centered * inverse
            self.STAT[at, 0:1] = average
            self.STAT[at, 1:2] = inverse
            self.N1[at] = (xhat * self.VEC[0:1] + self.VEC[1:2]).astype(BF)
            self.N2[at] = (xhat * self.VEC[2:3] + self.VEC[3:4]).astype(BF)

    def turn(self, values, at, kind, sign):
        lanes = lax.broadcasted_iota(jnp.int32, values.shape, 1)
        turned = values * self.ROT[0, at] + sign * (
            pltpu.roll(values, 128 - ROT_DIM // 2, 1) * self.ROT[1, at]
            + pltpu.roll(values, ROT_DIM // 2, 1) * self.ROT[2, at]
        )
        if kind == 0:
            return turned
        return jnp.where((lanes >= HEAD_DIM) if kind == 1 else (lanes < HEAD_DIM), turned, values)

    def qkv(self, j):
        at = self.at(j)
        scale = HEAD_DIM ** (-0.5)
        packed = dot(self.N1[at], self.WQ[...])
        bias = self.BQ[...]
        places = [(self.Q, scale), (self.K, None), (self.V, None)]
        for t in range(packed.shape[1] // 128):
            cols = slice(t * 128, t * 128 + 128)
            low = self.turn(packed[:, cols] + bias[:, cols], at, t % 3, 1.0).astype(BF)
            for side in range(2):
                index = 2 * t + side
                ref, factor = places[index % 3]
                value = low[:, side * HEAD_DIM : side * HEAD_DIM + HEAD_DIM]
                ref[index // 3, at] = value if factor is None else value * jnp.asarray(factor, BF)

    def up(self, j):
        at = self.at(j)
        tile = 256

        for i in range(self.WU.shape[1] // tile):
            cols = slice(i * tile, i * tile + tile)
            hidden = dot(self.N2[at], self.WU[:, cols]) + self.BU[:, cols]
            cdf = 0.5 + 0.5 * lax.erf(hidden * ROOT_HALF)
            self.ACT[at, cols] = (hidden * cdf).astype(BF)
            pdf = PDF_SCALE * jnp.exp(-0.5 * hidden * hidden)
            self.DG[at, cols] = cdf + hidden * pdf

    def down(self, j):
        at = self.at(j)
        self.ACC[at] = dot(self.ACT[at], self.WDN[...])

    def masked(self, scores):
        rows = lax.broadcasted_iota(jnp.int32, scores.shape, 0)
        cols = lax.broadcasted_iota(jnp.int32, scores.shape, 1)
        return jnp.where(rows >= cols, scores, mask_fill)

    def attend_block(self, m, qb):
        size = self.block
        mine, before = slice(qb * size, qb * size + size), slice(0, qb * size)
        sides = []
        for side in range(2):
            h = 2 * m + side
            q = self.Q[h, mine]
            near = self.masked(dot(q, self.K[h, mine], NT))
            top = jnp.max(near, axis=-1, keepdims=True)
            if qb:
                far = dot(q, self.K[h, before], NT)
                top = jnp.maximum(top, jnp.max(far, axis=-1, keepdims=True))
            near = jnp.exp(near - top)
            total = jnp.sum(near, axis=-1, keepdims=True)
            if qb:
                far = jnp.exp(far - top)
                total = total + jnp.sum(far, axis=-1, keepdims=True)
            inverse = 1.0 / total
            self.LSE[h, mine] = top + jnp.log(total)
            context = dot((near * inverse).astype(BF), self.V[h, mine])
            if qb:
                context = context + dot((far * inverse).astype(BF), self.V[h, before])
            sides.append(context.astype(BF))
        self.CTX[m, mine] = jnp.concatenate(sides, axis=1)

    def attend_part(self, qb):
        @pl.loop(0, self.heads // 2)
        def _(m):
            self.attend_block(m, qb)

    def out(self, j):
        at = self.at(j)
        total = self.ACC[at]
        for m in range(self.heads // 2):
            total = total + dot(self.CTX[m, at], self.WDE[m * 128 : m * 128 + 128])
        self.OP[at] = total.astype(BF)

    def mlp_back(self, j):
        at = self.at(j)
        tile = 256

        for i in range(self.WU.shape[1] // tile):
            cols = slice(i * tile, i * tile + tile)
            active_grad = dot(self.G[at], self.WDN[cols], NT)
            self.HG[at, cols] = (active_grad * self.DG[at, cols]).astype(BF)

        self.ACC[at] = dot(self.HG[at], self.WU[...], NT)

    def context_grad(self, j):
        at = self.at(j)
        for m in range(self.heads // 2):
            self.DO[m, at] = dot(self.G[at], self.WDE[m * 128 : m * 128 + 128], NT).astype(BF)

    def back_block(self, m, qb):
        size = self.block
        mine, before = slice(qb * size, qb * size + size), slice(0, qb * size)
        scale = HEAD_DIM ** (-0.5)
        upstream = self.DO[m, mine]
        values, keys, queries, values_before, keys_before = [], [], [], [], []
        for side in range(2):
            h = 2 * m + side
            q = self.Q[h, mine]
            do = upstream[:, side * HEAD_DIM : side * HEAD_DIM + HEAD_DIM]
            lse = self.LSE[h, mine]
            near = jnp.exp(self.masked(dot(q, self.K[h, mine], NT)) - lse)
            near_grad = dot(do, self.V[h, mine], NT)
            weighted = jnp.sum(near * near_grad, axis=-1, keepdims=True)
            if qb:
                far = jnp.exp(dot(q, self.K[h, before], NT) - lse)
                far_grad = dot(do, self.V[h, before], NT)
                weighted = weighted + jnp.sum(far * far_grad, axis=-1, keepdims=True)
            values.append(dot(near.astype(BF), do, TN))
            score = (near * (near_grad - weighted)).astype(BF)
            keys.append(dot(score, q, TN))
            query = dot(score, self.K[h, mine])
            if qb:
                values_before.append(dot(far.astype(BF), do, TN))
                score = (far * (far_grad - weighted)).astype(BF)
                keys_before.append(dot(score, q, TN))
                query = query + dot(score, self.K[h, before])
            queries.append((query * scale).astype(BF))
        self.DV[m, mine] += jnp.concatenate(values, axis=1)
        self.DK[m, mine] += jnp.concatenate(keys, axis=1)
        self.DQ[m, mine] = jnp.concatenate(queries, axis=1)
        if qb:
            self.DV[m, before] += jnp.concatenate(values_before, axis=1)
            self.DK[m, before] += jnp.concatenate(keys_before, axis=1)

    def attend_back(self, j, m):
        for qb in range(self.length // self.block):

            @pl.when(j == qb)
            def _():
                self.back_block(m, qb)

    def unturn(self, j):
        at = self.at(j)
        for m in range(self.heads // 2):
            q = self.DQ[m, at].astype(F32)
            k = pltpu.roll(self.DK[m, at], HEAD_DIM, 1).astype(BF).astype(F32)
            v = self.DV[m, at].astype(BF).astype(F32)
            left = lax.broadcasted_iota(jnp.int32, q.shape, 1) < HEAD_DIM
            for kind, pair in enumerate(((q, k), (v, q), (k, v))):
                both = jnp.where(left, *pair)
                cols = slice((3 * m + kind) * 128, (3 * m + kind) * 128 + 128)
                self.PG[at, cols] = self.turn(both, at, kind, -1.0).astype(BF)

    def zero_sums(self):
        self.SUMS[...] = jnp.zeros_like(self.SUMS)
        self.COLS[...] = jnp.zeros_like(self.COLS)
        self.DK[...] = jnp.zeros_like(self.DK)
        self.DV[...] = jnp.zeros_like(self.DV)
        self.BUG[...] = jnp.zeros_like(self.BUG)
        self.BQG[...] = jnp.zeros_like(self.BQG)

    def input_back(self, j):
        self.TMP[...] = dot(self.PG[self.at(j)], self.WQ[...], NT)
        ones = jnp.ones((8, self.rows), BF)
        self.BQG[...] += dot(ones, self.PG[self.at(j)])[0:1]
        self.BUG[...] += dot(ones, self.HG[self.at(j)])[0:1]
        step = 32

        @pl.loop(0, self.rows // step)
        def _(i):
            at = self.at(j, step, i)
            here = pl.ds(pl.multiple_of(i * step, step), step)
            inverse = self.STAT[at, 1:2]
            xhat = (self.X[at].astype(F32) - self.STAT[at, 0:1]) * inverse
            one, two = self.TMP[here], self.ACC[at]
            u = one * self.VEC[0:1] + two * self.VEC[2:3]
            mean_u = jnp.mean(u, axis=-1, keepdims=True)
            mean_ux = jnp.mean(u * xhat, axis=-1, keepdims=True)
            self.DX[at] = (inverse * (u - mean_u - xhat * mean_ux)).astype(BF)
            for row, value in enumerate((one * xhat, one, two * xhat, two)):
                folded = value[0:8]
                for r in range(8, step, 8):
                    folded = folded + value[r : r + 8]
                self.COLS[row] += folded

    def fold_sums(self):
        for row in range(4):
            self.SUMS[row : row + 1] = jnp.sum(self.COLS[row], axis=0, keepdims=True)

    def weight_grad(self, left, right, put):
        tile = 256
        count = left.shape[1] // tile

        @pl.loop(0, count)
        def _(i):
            cols = pl.ds(pl.multiple_of(i * tile, tile), tile)
            put(i, dot(left[:, cols], right[...], TN).astype(BF))

    def down_grad(self, put):
        self.weight_grad(self.ACT, self.G, put)

    def up_grad(self, put):
        self.weight_grad(self.N2, self.HG, put)

    def qkv_grad(self, put):
        self.weight_grad(self.N1, self.PG, put)

    def dense_grad(self, put):
        for m in range(self.heads // 2):
            put(m, dot(self.CTX[m], self.G[...], TN).astype(BF))


def layer_scratch(length, width, heads, hidden):
    vm = pltpu.VMEM
    pairs, packed = heads // 2, heads * 3 * HEAD_DIM
    return dict(
        STAT=vm((length, 2), F32),
        N1=vm((length, width), BF),
        N2=vm((length, width), BF),
        Q=vm((heads, length, HEAD_DIM), BF),
        K=vm((heads, length, HEAD_DIM), BF),
        V=vm((heads, length, HEAD_DIM), BF),
        ACT=vm((length, hidden), BF),
        DG=vm((length, hidden), F32),
        ACC=vm((length, width), F32),
        LSE=vm((heads, length, 1), F32),
        CTX=vm((pairs, length, 2 * HEAD_DIM), BF),
        DO=vm((pairs, length, 2 * HEAD_DIM), BF),
        HG=vm((length, hidden), BF),
        DQ=vm((pairs, length, 2 * HEAD_DIM), BF),
        DK=vm((pairs, length, 2 * HEAD_DIM), F32),
        DV=vm((pairs, length, 2 * HEAD_DIM), F32),
        PG=vm((length, packed), BF),
    )


class LineReduce:
    def __init__(self, me, part, got, ssem, rsem):
        self.me, self.part, self.got, self.ssem, self.rsem = me, part, got, ssem, rsem
        self.parts, self.rows = got.shape[1:3]

    def copy(self, j, p, way):
        me = self.me
        to = jnp.minimum(me.z + 1, me.n - 1) if way == 0 else jnp.maximum(me.z - 1, 0)
        slot = j if way == 0 else jnp.where(j == to, me.n, j)
        return send(
            rows_at(self.part, (j * self.parts + p) * self.rows, self.rows),
            self.got.at[slot, p],
            self.ssem.at[j, p],
            self.rsem.at[slot, p],
            (me.d, to),
        )

    def came(self, slot, p):
        me = self.me
        got = self.got.at[slot, p]
        return send(got, got, self.ssem.at[0, p], self.rsem.at[slot, p], (me.d, me.z))

    def start(self, j, which=None):
        me = self.me
        for p in range(self.parts) if which is None else which:

            @pl.when((me.z == 0) & (j > 0))
            def _():
                self.copy(j, p, 0).start()

            @pl.when((me.z == me.n - 1) & (j < me.n - 1))
            def _():
                self.copy(j, p, 1).start()

    def add(self, j, p):
        step = 64

        @pl.loop(0, self.rows // step)
        def _(i):
            mine = pl.ds(pl.multiple_of((j * self.parts + p) * self.rows + i * step, step), step)
            here = pl.ds(pl.multiple_of(i * step, step), step)
            self.part[mine] = (
                self.part[mine].astype(F32) + self.got[j, p, here].astype(F32)
            ).astype(BF)

    def step(self, t):
        me = self.me
        n = me.n
        for p in range(self.parts):
            for way, e in ((0, t - me.z), (1, t - (n - 1 - me.z))):
                j = n - 1 - e if way == 0 else e
                valid = (me.z > 0) & (me.z < n - 1) & (e >= 0)
                valid = valid & ((j > me.z) if way == 0 else (j < me.z))

                @pl.when(valid)
                def _():
                    self.came(j, p).wait_recv()
                    self.add(j, p)
                    self.copy(j, p, way).start()

    def total(self, base, extra, result, tmp):
        me = self.me
        step = 64
        for p in range(self.parts):

            @pl.when(me.z > 0)
            def _():
                self.came(me.z, p).wait_recv()

            @pl.when(me.z < me.n - 1)
            def _():
                self.came(me.n, p).wait_recv()

            @pl.loop(0, self.rows // step)
            def _(i):
                at = p * self.rows + i * step
                here = pl.ds(pl.multiple_of(i * step, step), step)
                there = pl.ds(pl.multiple_of(at, step), step)
                mine = pl.ds(pl.multiple_of(me.z * self.parts * self.rows + at, step), step)
                tmp[here] = base[mine].astype(F32) + self.part[mine].astype(F32)
                if extra is not None:
                    tmp[here] += extra

                @pl.when(me.z > 0)
                def _():
                    tmp[here] += self.got[me.z, p, here].astype(F32)

                @pl.when(me.z < me.n - 1)
                def _():
                    tmp[here] += self.got[me.n, p, here].astype(F32)

                result[there] = tmp[here].astype(BF)

    def finish(self):
        me = self.me
        for j in range(me.n):
            for p in range(self.parts):

                @pl.when((j > me.z) & (me.z < me.n - 1))
                def _():
                    self.copy(j, p, 0).wait_send()

                @pl.when((j < me.z) & (me.z > 0))
                def _():
                    self.copy(j, p, 1).wait_send()


def nearest(n):
    return [sorted(range(n), key=lambda j: abs(j - z)) for z in range(n)]


def pick(table, z, k):
    value = jnp.int32(0)
    for at, row in enumerate(table):
        for index, entry in enumerate(row):
            if entry:
                value = jnp.where((z == at) & (k == index), entry, value)
    return value


VECTORS = 6


def layer_kernel(n, data, chunks, names, *refs):
    refs = list(refs)

    def take(count):
        got = refs[:count]
        del refs[:count]
        return got

    vectors = take(VECTORS)
    x, g, wq, wu, WDE, WDN, bq, bu, ROT = take(9)
    out, dx, small, fu, fq, fdn, fde = take(7)
    ins = dict(zip(names, take(len(names))))
    ins.update(WDE=WDE, WDN=WDN, ROT=ROT)
    rows = out.shape[0]
    layer = Layer(rows, ins)
    me = Place(n, data)
    SM, sm = take(2)
    layer.DX = layer.ACT
    lsem, ss, sr, xs, xr, gs, gr = take(7)
    cq, cu = ColumnGather(me, wq, layer.WQ, take(5)), ColumnGather(me, wu, layer.WU, take(5))
    og, xg, os, orr, ds, dr = take(6)
    v1, v1g, v1s, v1r, v2m, v2g, v2s, v2r = take(8)
    reduces = []
    for unused in range(4):
        reduces.append(take_reduce(me, take(1)[0], take))
    red_dn, red_de, red_u, red_q = reduces
    shares = [GradShare(me, final, take(6)) for final in (fdn, fde, fu, fq)]
    share_dn, share_de, share_u, share_q = shares
    back_u = RowsBack(me, red_u.total, fu, *take(3))
    back_q = RowsBack(me, red_q.total, fq, *take(3))
    (dsem,) = take(1)
    assert not refs
    lx = LineGather(me, x, layer.X, rows, chunks, xs, xr)
    lg = LineGather(me, g, layer.G, rows, chunks, gs, gr)
    ro = LineReduce(me, layer.OP, og, os, orr)
    rx = LineReduce(me, layer.ACT, xg, ds, dr)
    near = nearest(n)
    far = [list(range(n - 1, -1, -1)) if 2 * z < n else list(range(n)) for z in range(n)]
    depth = wq.shape[0]
    part = depth

    own = [
        pltpu.make_async_copy(x, rows_at(layer.X, me.z * rows, rows), lsem.at[0]),
        pltpu.make_async_copy(g, rows_at(layer.G, me.z * rows, rows), lsem.at[1]),
        pltpu.make_async_copy(
            block_at(wq, 0, depth, me.z * layer.WQ.shape[1], layer.WQ.shape[1]),
            rows_at(layer.WQ, me.z * depth, depth),
            lsem.at[2],
        ),
        pltpu.make_async_copy(
            block_at(wu, 0, depth, me.z * layer.WU.shape[1], layer.WU.shape[1]),
            rows_at(layer.WU, me.z * depth, depth),
            lsem.at[3],
        ),
    ]
    for copy in own:
        copy.start()
    sm[...] = jnp.zeros_like(sm)
    for i, vector in enumerate(vectors):
        sm[i] = vector[...].astype(F32)
    layer.BQ[0] = bq[...].astype(F32)
    layer.BU[0] = bu[...].astype(F32)
    me.barrier()

    def tiny(k, slot):
        return send(sm, SM.at[slot], ss.at[k], sr.at[slot], me.seq_peer(k)[1])

    for k in range(1, n):
        tiny(k, me.z).start()
    cq.start()
    cu.start()
    lx.start()
    SM[me.z] = sm[...]
    layer.zero_sums()
    for k in range(1, n):
        tiny(k, me.seq_peer(k)[0]).wait_recv()
    for i in range(n):
        layer.VEC[:, i * part : i * part + part] = SM[i]
    near_k = sorted({1, n - 1})
    for k in near_k:
        cq.share(k)
        cu.share(k)
    lx.forward(1)
    for k in range(1, n):
        if k not in near_k:
            cq.share(k)
            cu.share(k)
    for s in range(2, n - 1):
        lx.forward(s)
    lg.start()
    own[0].wait()
    layer.norm(me.z)
    for k in range(1, n):
        cq.hand(k)
        cu.hand(k)
    own[2].wait()
    own[3].wait()
    cq.finish()
    cu.finish()

    @pl.loop(0, n)
    def _(k):
        j = pick(near, me.z, k)

        @pl.when(k > 0)
        def _():
            lx.arrive(j)
            layer.norm(j)

        layer.qkv(j)
        layer.up(j)
        layer.down(j)

    lg.forward(1)
    blocks = layer.length // layer.block
    for qb in range(blocks):
        layer.attend_part(qb)
        if qb == blocks // 2:
            for s in range(2, n - 1):
                lg.forward(s)

    @pl.loop(0, n)
    def _(k):
        j = pick(far, me.z, k)
        layer.out(j)
        ro.start(j)

    own[1].wait()
    layer.SUMS[4:5] = jnp.sum(layer.G[layer.at(me.z)].astype(F32), axis=0, keepdims=True)

    def put(red):
        def store(i, value):
            parts, unused, rp, cols = red.part.shape
            pieces = value.shape[0] // rp
            if parts == 1:
                red.part[0, pl.ds(i * pieces, pieces)] = value.reshape(pieces, rp, cols)
            else:
                red.part[i] = value.reshape(pieces, rp, cols)

        return store

    pairs = layer.heads // 2

    @pl.loop(0, n)
    def _(k):
        j = pick(near, me.z, k)
        lg.arrive(j)

        @pl.when(k == n - 1)
        def _():
            ro.step(1)
            layer.down_grad(put(red_dn))
            red_dn.start()
            layer.dense_grad(put(red_de))
            red_de.start()

        layer.mlp_back(j)
        layer.context_grad(j)

        @pl.when(k == n - 1)
        def _():
            layer.up_grad(put(red_u))
            red_u.start()
            red_dn.chip_sums()
            red_de.chip_sums()

        @pl.loop(0, pairs)
        def _(m):
            layer.attend_back(j, m)

            @pl.when((k == n - 1) & (m == 0))
            def _():
                red_u.chip_sums()

    red_dn.pair_sums()
    red_de.pair_sums()
    for t in range(2, 2 * n - 5):
        ro.step(t)
    copies = [
        pltpu.make_async_copy(red.total.at[0], final.at[me.piece], dsem.at[i])
        for i, (red, final) in enumerate(((red_dn, fdn), (red_de, fde)))
    ]

    @pl.loop(0, n)
    def _(j):
        layer.unturn(j)

    @pl.loop(0, n)
    def _(k):
        j = pick(far, me.z, k)
        layer.input_back(j)

        @pl.when(k == 0)
        def _():
            rx.start(j)
            layer.qkv_grad(put(red_q))
            red_q.start()
            red_u.pair_sums()

        @pl.when(k == 1)
        def _():
            rx.start(j, (0,))
            red_q.chip_sums()
            red_dn.sum_up()
            red_de.sum_up()
            for copy in copies:
                copy.start()

        @pl.when(k == n - 2)
        def _():
            for copy in copies:
                copy.wait()
            share_dn.start()
            share_de.start()
            red_u.sum_up()
            back_u.start()

    red_q.pair_sums()
    layer.fold_sums()
    cs = part
    v1[...] = layer.SUMS[...]

    def small_z(k, slot):
        other, to = me.seq_peer(k)
        return send(
            v1.at[:, pl.ds(pl.multiple_of(other * cs, cs), cs)],
            v1g.at[slot],
            v1s.at[k],
            v1r.at[slot],
            to,
        )

    def small_dp(k, slot):
        return send(v2m, v2g.at[slot], v2s.at[k], v2r.at[slot], me.dp_peer(k)[1])

    for k in range(1, n):
        small_z(k, me.z).start()
    rx.start(pick(far, me.z, 1), (1,))
    rx.step(1)
    share_dn.forward()
    share_de.forward()
    red_q.sum_up()
    back_q.start()
    for k in range(2, n - 1):
        rx.start(pick(far, me.z, k))
    share_dn.hand()
    share_de.hand()
    ro.total(layer.X, layer.VEC[4:5] + layer.VEC[5:6], out, layer.TMP)
    back_u.wait()
    share_u.start()
    for t in range(2, 2 * n - 5):
        rx.step(t)
    back_q.wait()
    share_q.start()
    for k in range(1, n):
        small_z(k, me.seq_peer(k)[0]).wait_recv()
    v1g[me.z] = v1[:, pl.ds(pl.multiple_of(me.z * cs, cs), cs)]
    total = v1g[0]
    for k in range(1, n):
        total = total + v1g[k]
    v2m[...] = jnp.zeros_like(v2m)
    v2m[0:8] = total
    for i in range(layer.BUG.shape[1] // cs):
        v2m[8 + i : 9 + i] = layer.BUG[:, i * cs : i * cs + cs]
    for i in range(layer.BQG.shape[1] // cs):
        v2m[12 + i : 13 + i] = layer.BQG[:, i * cs : i * cs + cs]
    for k in range(1, data):
        small_dp(k, me.d).start()
    share_u.forward()
    for k in range(1, data):
        small_dp(k, me.dp_peer(k)[0]).wait_recv()
    v2g[me.d] = v2m[...]

    def add(i, acc):
        return acc + v2g[i]

    small[...] = lax.fori_loop(1, data, add, v2g[0])
    share_q.forward()
    share_u.hand()
    share_q.hand()
    rx.total(layer.G, None, dx, layer.TMP)
    ro.finish()
    rx.finish()
    lx.finish()
    lg.finish()
    for k in range(1, n):
        tiny(k, me.z).wait_send()
        small_z(k, me.z).wait_send()
    for k in range(1, data):
        small_dp(k, me.d).wait_send()
    for red in reduces:
        red.finish()
    for share in shares:
        share.finish()
    back_u.finish()
    back_q.finish()


def rotary_constant(length):
    half = ROT_DIM // 2
    freqs = np.float32(10000.0) ** (-np.arange(half, dtype=np.float32) * np.float32(2.0 / ROT_DIM))
    angles = np.arange(length, dtype=np.float32)[:, None] * freqs.astype(np.float32)[None, :]
    cosine, sine = np.cos(angles), np.sin(angles)
    rest = HEAD_DIM - ROT_DIM
    keep, none, gap = np.ones((length, rest)), np.zeros((length, rest)), np.zeros_like(sine)
    same = np.concatenate([cosine, cosine, keep] * 2, axis=1)
    up = np.concatenate([-sine, gap, none] * 2, axis=1)
    down = np.concatenate([gap, sine, none] * 2, axis=1)
    return np.stack([same, up, down]).astype(np.float32)


def whole_layer(n, data, vectors, x, g, wq, wu, w_dense, w_down, b_qkv, b_up):
    rows, width = x.shape
    length = n * rows
    packed, hidden = wq.shape[1] // n, wu.shape[1] // n
    heads = packed // (3 * HEAD_DIM)
    depth = wq.shape[0]
    chunks = 4
    groups = data // PLANE
    vm = pl.BlockSpec(memory_space=pltpu.VMEM)
    hbm = pl.BlockSpec(memory_space=pl.ANY)
    dma = pltpu.SemaphoreType.DMA
    sds = jax.ShapeDtypeStruct
    mem = pltpu.VMEM
    named = layer_scratch(length, width, heads, hidden)
    named.update(
        X=mem((length, width), BF),
        G=mem((length, width), BF),
        WQ=mem((width, packed), BF),
        WU=mem((width, hidden), BF),
        VEC=mem((8, width), F32),
        OP=mem((length, width), BF),
        SUMS=mem((8, width), F32),
        BUG=mem((1, hidden), F32),
        BQG=mem((1, packed), F32),
        BQ=mem((1, packed), F32),
        BU=mem((1, hidden), F32),
        TMP=mem((rows, width), F32),
        COLS=mem((4, 8, width), F32),
    )
    scratch = list(named.values())
    scratch += [mem((n, 8, depth), F32), mem((8, depth), F32)]
    scratch += [dma((4,)), dma((n,)), dma((n,))]
    scratch += [dma((2, n, chunks)), dma((n, chunks))] * 2
    scratch += column_sems(n) + column_sems(n)
    scratch += [mem((n + 1, 2, rows // 2, width), BF)] * 2
    scratch += [dma((n, 2)), dma((n + 1, 2))] * 2
    scratch += [mem((8, width), F32), mem((n, 8, depth), F32), dma((n,)), dma((n,))]
    scratch += [mem((16, depth), F32), mem((data, 16, depth), F32), dma((data,)), dma((data,))]
    shapes = [
        (1, hidden // PLANE, width),
        (1, packed // 3 // PLANE, width),
        (n, depth // PLANE, hidden),
        (n, depth // PLANE, packed),
    ]
    for m, rp, cols in shapes:
        scratch += [mem((m, PLANE, rp, cols), BF)] + reduce_scratch(m, rp, cols, groups)
    for unused in range(4):
        scratch += share_sems()
    scratch += [dma((n,)), dma((n,)), dma] * 2
    scratch += [dma((4,))]
    outs = [
        sds((rows, width), BF),
        sds((rows, width), BF),
        sds((16, depth), F32),
        sds((PLANE, depth // PLANE, hidden * n), BF),
        sds((PLANE, depth // PLANE, packed * n), BF),
        sds((PLANE, hidden // PLANE, width), BF),
        sds((PLANE, packed // 3 // PLANE, width), BF),
    ]
    return pl.pallas_call(
        functools.partial(layer_kernel, n, data, chunks, list(named)),
        out_shape=outs,
        in_specs=[vm] * VECTORS + [hbm] * 4 + [vm] * 5,
        out_specs=[vm] * 3 + [hbm] * 4,
        scratch_shapes=scratch,
        compiler_params=pltpu.CompilerParams(
            collective_id=2, has_side_effects=True, vmem_limit_bytes=67043328
        ),
        name="layer",
    )(*vectors, x, g, wq, wu, w_dense, w_down, b_qkv, b_up, rotary_constant(length))


def fits(n, data, tokens, qkv, up):
    unused, rows, width = tokens
    length, depth = n * rows, qkv[0]
    return (
        length * (width + up[1] // n) <= 1024 * 2048
        and rows == 256
        and depth == 256
        and up[1] // n == width
        and up[1] // n % 256 == 0
        and qkv[1] // n % (6 * HEAD_DIM) == 0
    )


def per_device(
    n,
    data,
    layer_input,
    attn_gain,
    attn_shift,
    mlp_gain,
    mlp_shift,
    qkv_weight,
    qkv_bias,
    dense_weight,
    dense_bias,
    up_weight,
    up_bias,
    down_weight,
    down_bias,
    out_grad,
):
    unused, rows, width = layer_input.shape
    x = layer_input.reshape(rows, width)
    g = out_grad.reshape(rows, width)
    part = width // n
    if fits(n, data, layer_input.shape, qkv_weight.shape, up_weight.shape):
        vectors = (attn_gain, attn_shift, mlp_gain, mlp_shift, dense_bias, down_bias)
        out, dx, tiny, fu, fq, fdn, fde = whole_layer(
            n, data, vectors, x, g, qkv_weight, up_weight, dense_weight, down_weight,
            qkv_bias, up_bias,
        )
    else:
        small = jnp.stack(
            [attn_gain, attn_shift, mlp_gain, mlp_shift, dense_bias, down_bias] + [attn_gain] * 2
        ).astype(F32)
        SM, X, G, WQ, WU = gather(n, data, small, x, g, qkv_weight, up_weight)
        vectors = jnp.swapaxes(SM, 0, 1).reshape(8, width)
        bias = (vectors[4] + vectors[5])[None]
        OP, DX, sums, bu, bq, UG, QG, DnG, DeG = middle(
            X, G, WQ, WU, dense_weight, down_weight, qkv_bias, up_bias, vectors
        )
        v1 = jnp.concatenate(
            [sums, jnp.sum(g.astype(F32), axis=0)[None], jnp.zeros((3, width), F32)], axis=0
        )
        v2 = jnp.concatenate(
            [bu.reshape(4, part), bq.reshape(3, part), jnp.zeros((1, part), F32)]
        )
        out, dx, tiny, fu, fq, fdn, fde = reduce_all(
            n, data, OP, DX, v1, v2, bias, x, g, UG, QG, DnG, DeG
        )
    results = finish(part, out, dx, tiny, fu, fq, fdn, fde)
    return tuple(r.reshape(layer_input.shape) for r in results[:2]) + tuple(results[2:])


def finish_kernel(part, out, dx, tiny, fu, fq, fdn, fde, *results):
    (o_out, o_dx, ag, ash, mg, ms, gq, bq, gde, bde, gu, bu, gdn, bdn) = results
    o_out[...] = out[...]
    o_dx[...] = dx[...]
    for source, result in ((fq, gq), (fde, gde), (fu, gu), (fdn, gdn)):
        result[...] = source[...].astype(F32)

    @pl.when(pl.program_id(0) == 0)
    def _():
        for row, result in enumerate((ag, ash, mg, ms, bde)):
            result[...] = tiny[row]
        bdn[...] = tiny[4]
        for base, result in ((8, bu), (12, bq)):
            for i in range(result.shape[0] // part):
                result[i * part : i * part + part] = tiny[base + i]


def finish(part, out, dx, tiny, fu, fq, fdn, fde):
    steps = PLANE
    sds = jax.ShapeDtypeStruct

    def tile(rows, cols):
        return pl.BlockSpec((rows // steps, cols), lambda i: (i, 0))

    def line(size):
        return sds((size,), F32), pl.BlockSpec((size,), lambda i: (0,))

    wide = [a.reshape(-1, a.shape[-1]) for a in (fu, fq, fdn, fde)]
    gu, gq, gdn, gde = ((sds(a.shape, F32), tile(*a.shape)) for a in wide)
    tokens = (sds(out.shape, BF), tile(*out.shape))
    vector = line(part)
    shapes, specs = zip(
        tokens, tokens, vector, vector, vector, vector, gq, line(fq.shape[-1] // (fu.shape[-1] // gdn[0].shape[0])),
        gde, vector, gu, line(gdn[0].shape[0]), gdn, vector,
    )
    return pl.pallas_call(
        functools.partial(finish_kernel, part),
        grid=(steps,),
        out_shape=shapes,
        in_specs=[tile(*out.shape), tile(*out.shape), pl.BlockSpec(tiny.shape, lambda i: (0, 0))]
        + [tile(*a.shape) for a in wide],
        out_specs=specs,
        compiler_params=pltpu.CompilerParams(vmem_limit_bytes=63 << 20),
        name="finish",
    )(out, dx, tiny, *wide)


def solution(mesh):
    tokens, row, vector = P("dp", "seq", None), P("seq", None), P("seq")
    in_specs = (tokens,) + (vector,) * 4 + (row, vector) * 4 + (tokens,)
    out_specs = (tokens, tokens) + (vector,) * 4 + (row, vector) * 4
    return jax.shard_map(
        functools.partial(per_device, mesh.shape["seq"], mesh.shape["dp"]),
        mesh=mesh,
        in_specs=in_specs,
        out_specs=out_specs,
        check_vma=False,
    )
```

```python
import functools
import math

import jax
import jax.numpy as jnp
import numpy as np
from jax import lax
from jax.experimental import pallas as pl
from jax.experimental.pallas import tpu as pltpu
from jax.sharding import PartitionSpec as P

HEADS = 16
HEAD_DIM = 64
ROT_DIM = 16
PLANE = 8
CHIPS = 4
epsilon = 1e-05
mask_fill = -1e30
MESH = pl.DeviceIdType.MESH
BF = jnp.bfloat16
F32 = jnp.float32


def rows_at(ref, start, count):
    return ref.at[pl.ds(pl.multiple_of(start, count), count)]


def block_at(ref, row, rows, col, cols):
    return ref.at[
        pl.ds(pl.multiple_of(row, rows), rows), pl.ds(pl.multiple_of(col, cols), cols)
    ]


class Place:
    def __init__(self, n, data):
        self.n, self.data = n, data
        self.d = lax.axis_index("dp")
        self.z = lax.axis_index("seq")
        self.base = self.d // PLANE * PLANE
        self.r = lax.rem(self.d, PLANE)
        self.ch = self.r // 2
        self.c = lax.rem(self.r, 2)
        self.piece = self.c * CHIPS + self.ch

    def seq_peer(self, k):
        other = lax.rem(self.z + k, self.n)
        return other, (self.d, other)

    def chip_peer(self, k):
        other = lax.rem(self.ch + k, CHIPS)
        return other, (self.base + other * 2 + self.c, self.z)

    def beside(self, way):
        other = self.ch + 1 - 2 * lax.rem(self.ch, 2) if way == 0 else lax.rem(self.ch + 2, CHIPS)
        return other, (self.base + other * 2 + self.c, self.z)

    def partner(self):
        return (self.base + self.ch * 2 + 1 - self.c, self.z)

    def dp_peer(self, k):
        other = lax.rem(self.d + k, self.data)
        return other, (other, self.z)

    def barrier(self):
        self.greet()
        self.met()

    def greet(self):
        sem = pltpu.get_barrier_semaphore()
        for k in range(1, self.n):
            pl.semaphore_signal(sem, inc=1, device_id=self.seq_peer(k)[1], device_id_type=MESH)
        for k in range(1, self.data):
            pl.semaphore_signal(sem, inc=1, device_id=self.dp_peer(k)[1], device_id_type=MESH)

    def met(self):
        pl.semaphore_wait(pltpu.get_barrier_semaphore(), self.n - 1 + self.data - 1)


def send(src, dst, ssem, rsem, to):
    return pltpu.make_async_remote_copy(
        src_ref=src, dst_ref=dst, send_sem=ssem, recv_sem=rsem, device_id=to, device_id_type=MESH
    )


class LineGather:
    def __init__(self, me, shard, full, rows, chunks, ssem, rsem):
        self.me, self.shard, self.full = me, shard, full
        self.rows, self.chunks, self.ssem, self.rsem = rows, chunks, ssem, rsem

    def part(self, owner, c):
        size = self.rows // self.chunks
        return rows_at(self.full, owner * self.rows + c * size, size)

    def copy(self, src, owner, c, way):
        me = self.me
        to = jnp.minimum(me.z + 1, me.n - 1) if way == 0 else jnp.maximum(me.z - 1, 0)
        return send(
            src,
            self.part(owner, c),
            self.ssem.at[way, owner, c],
            self.rsem.at[owner, c],
            (me.d, to),
        )

    def start(self):
        me = self.me
        size = self.rows // self.chunks
        for c in range(self.chunks):
            src = rows_at(self.shard, c * size, size)

            @pl.when(me.z < me.n - 1)
            def _():
                self.copy(src, me.z, c, 0).start()

            @pl.when(me.z > 0)
            def _():
                self.copy(src, me.z, c, 1).start()

    def step(self, s, c):
        me = self.me

        @pl.when(me.z >= s)
        def _():
            owner = me.z - s
            copy = self.copy(self.part(owner, c), owner, c, 0)
            copy.wait_recv()

            @pl.when(me.z < me.n - 1)
            def _():
                copy.start()

        @pl.when(me.z + s < me.n)
        def _():
            owner = me.z + s
            copy = self.copy(self.part(owner, c), owner, c, 1)
            copy.wait_recv()

            @pl.when(me.z > 0)
            def _():
                copy.start()

    def forward(self, s):
        me = self.me
        inner = (me.z > 0) & (me.z < me.n - 1)
        for c in range(self.chunks):
            for way, valid, owner in ((0, me.z >= s, me.z - s), (1, me.z + s < me.n, me.z + s)):

                @pl.when(inner & valid)
                def _():
                    copy = self.copy(self.part(owner, c), owner, c, way)
                    copy.wait_recv()
                    copy.start()

    def arrive(self, owner):
        me = self.me

        @pl.when(((me.z == 0) | (me.z == me.n - 1)) & (owner != me.z))
        def _():
            for c in range(self.chunks):
                self.copy(self.part(owner, c), owner, c, 0).wait_recv()

    def finish(self):
        me = self.me
        for c in range(self.chunks):
            for owner in range(me.n):

                @pl.when((me.z < me.n - 1) & (owner <= me.z))
                def _():
                    self.copy(self.part(owner, c), owner, c, 0).wait_send()

                @pl.when((me.z > 0) & (owner >= me.z))
                def _():
                    self.copy(self.part(owner, c), owner, c, 1).wait_send()


class ColumnGather:
    def __init__(self, me, shard, full, sems):
        self.me, self.shard, self.full = me, shard, full
        self.depth = shard.shape[0]
        self.rp = self.depth // PLANE
        self.cols = full.shape[1]
        self.zs, self.zr, self.ps, self.pr, self.fs = sems

    def part(self, src_z, piece):
        return rows_at(self.full, (src_z * PLANE + piece) * self.rp, self.rp)

    def across(self, k):
        me = self.me
        other, to = me.seq_peer(k)
        src = block_at(self.shard, me.piece * self.rp, self.rp, other * self.cols, self.cols)
        return send(src, self.part(me.z, me.piece), self.zs.at[k], self.zr.at[me.n - k], to)

    def came(self, k):
        me = self.me
        other, to = me.seq_peer(k)
        src = block_at(self.shard, me.piece * self.rp, self.rp, other * self.cols, self.cols)
        return send(src, self.part(other, me.piece), self.zs.at[k], self.zr.at[k], to)

    def shares(self, k):
        me = self.me
        other, unused = me.seq_peer(k)
        mine = self.part(other, me.piece)
        for j in range(1, CHIPS):
            to = me.chip_peer(j)[1]
            yield send(mine, mine, self.ps.at[k, j], self.pr.at[k, CHIPS - j], to)
        yield send(mine, mine, self.ps.at[k, 0], self.fs.at[1, k, 0], me.partner())

    def handed(self, k, j):
        me = self.me
        other, unused = me.seq_peer(k)
        chip = me.chip_peer(j)[0]
        return self.part(other, me.c * CHIPS + chip), self.part(other, (1 - me.c) * CHIPS + chip)

    def start(self):
        for k in range(self.me.n - 1, 0, -1):
            self.across(k).start()

    def share(self, k):
        self.came(k).wait_recv()
        for copy in self.shares(k):
            copy.start()

    def hand(self, k):
        me = self.me
        for j in range(1, CHIPS):
            got, unused = self.handed(k, j)
            send(got, got, self.ps.at[k, j], self.pr.at[k, j], me.chip_peer(j)[1]).wait_recv()
            send(got, got, self.fs.at[0, k, j], self.fs.at[1, k, j], me.partner()).start()

    def finish(self):
        me = self.me
        for k in range(1, me.n):
            self.across(k).wait_send()
            for copy in self.shares(k):
                copy.wait_send()
            other, unused = me.seq_peer(k)
            for j in range(CHIPS):
                unused, got = self.handed(k, j)
                copy = send(got, got, self.fs.at[0, k, j], self.fs.at[1, k, j], me.partner())
                copy.wait_recv()
                if j > 0:
                    copy.wait_send()


def column_sems(n):
    dma = pltpu.SemaphoreType.DMA
    return [dma((n,)), dma((n,)), dma((n, CHIPS)), dma((n, CHIPS)), dma((2, n, CHIPS))]


def gather_kernel(n, data, chunks, sm, x, g, wq, wu, SM, X, G, WQ, WU, *sems):
    me = Place(n, data)
    rows = x.shape[0]
    lsem, ss, sr, xs, xr, gs, gr = sems[:7]
    me.barrier()
    cq, cu = ColumnGather(me, wq, WQ, sems[7:12]), ColumnGather(me, wu, WU, sems[12:17])
    lx = LineGather(me, x, X, rows, chunks, xs, xr)
    lg = LineGather(me, g, G, rows, chunks, gs, gr)
    depth = wq.shape[0]
    own = [
        pltpu.make_async_copy(sm, SM.at[me.z], lsem.at[0]),
        pltpu.make_async_copy(x, rows_at(X, me.z * rows, rows), lsem.at[1]),
        pltpu.make_async_copy(g, rows_at(G, me.z * rows, rows), lsem.at[2]),
        pltpu.make_async_copy(
            block_at(wq, 0, depth, me.z * WQ.shape[1], WQ.shape[1]),
            rows_at(WQ, me.z * depth, depth),
            lsem.at[3],
        ),
        pltpu.make_async_copy(
            block_at(wu, 0, depth, me.z * WU.shape[1], WU.shape[1]),
            rows_at(WU, me.z * depth, depth),
            lsem.at[4],
        ),
    ]
    for copy in own:
        copy.start()

    def small(k, slot):
        return send(sm, SM.at[slot], ss.at[k], sr.at[slot], me.seq_peer(k)[1])

    for k in range(1, n):
        small(k, me.z).start()
    cq.start()
    cu.start()
    lx.start()
    lg.start()
    near = sorted({1, n - 1})
    for k in near:
        cq.share(k)
        cu.share(k)
    for c in range(chunks):
        lx.step(1, c)
    for k in range(1, n):
        if k not in near:
            cq.share(k)
            cu.share(k)
    for s in range(2, n):
        for c in range(chunks):
            lx.step(s, c)
    for k in range(1, n):
        cq.hand(k)
        cu.hand(k)
    for s in range(1, n):
        for c in range(chunks):
            lg.step(s, c)
    for k in range(1, n):
        small(k, me.z).wait_send()
        small(k, me.seq_peer(k)[0]).wait_recv()
    cq.finish()
    cu.finish()
    lx.finish()
    lg.finish()
    for copy in own:
        copy.wait()


def gather(n, data, sm, x, g, wq, wu):
    rows, width = x.shape
    depth = wq.shape[0]
    chunks = 4
    vm = pl.BlockSpec(memory_space=pltpu.VMEM)
    dma = pltpu.SemaphoreType.DMA
    sds = jax.ShapeDtypeStruct
    return pl.pallas_call(
        functools.partial(gather_kernel, n, data, chunks),
        out_shape=[
            sds((n,) + sm.shape, sm.dtype),
            sds((n * rows, width), x.dtype),
            sds((n * rows, width), x.dtype),
            sds((n * depth, wq.shape[1] // n), wq.dtype),
            sds((n * depth, wu.shape[1] // n), wu.dtype),
        ],
        in_specs=[vm] * 5,
        out_specs=[vm] * 5,
        scratch_shapes=[
            dma((5,)),
            dma((n,)),
            dma((n,)),
            dma((2, n, chunks)),
            dma((n, chunks)),
            dma((2, n, chunks)),
            dma((n, chunks)),
        ]
        + column_sems(n)
        + column_sems(n),
        compiler_params=pltpu.CompilerParams(
            collective_id=0, has_side_effects=True, vmem_limit_bytes=60 << 20
        ),
        name="gather",
    )(sm, x, g, wq, wu)


class RowReduce:
    def __init__(self, me, part, got, ssem, rsem):
        self.me, self.part, self.got, self.ssem, self.rsem = me, part, got, ssem, rsem
        self.rows = got.shape[1]

    def copy(self, k, slot):
        other, to = self.me.seq_peer(k)
        return send(
            rows_at(self.part, other * self.rows, self.rows),
            self.got.at[slot],
            self.ssem.at[k],
            self.rsem.at[slot],
            to,
        )

    def start(self):
        for k in range(1, self.me.n):
            self.copy(k, self.me.z).start()

    def wait(self):
        for k in range(1, self.me.n):
            self.copy(k, self.me.seq_peer(k)[0]).wait_recv()

    def finish(self):
        for k in range(1, self.me.n):
            self.copy(k, self.me.z).wait_send()


def halves(cols):
    middle = cols // 2 // 128 * 128
    return slice(0, middle), slice(middle, cols)


class GradReduce:
    def __init__(self, me, part, half, near, far, total, groups, sems):
        self.me, self.part, self.half, self.near, self.far = me, part, half, near, far
        self.total, self.groups = total, groups
        self.hs, self.hr, self.ns, self.nr, self.fs, self.fr, self.gs, self.gr = sems
        self.cols = halves(part.shape[3])

    def swap(self):
        me = self.me
        return send(
            self.part.at[:, pl.ds((1 - me.c) * CHIPS, CHIPS)],
            self.half,
            self.hs,
            self.hr,
            me.partner(),
        )

    def piece(self, way, index, other):
        me = self.me
        a, b = me.ch // 2, lax.rem(me.ch, 2)
        if way == 0:
            chip = index * 2 + (1 - b if other else b)
        else:
            chip = (1 - a if other else a) * 2 + index
        return me.c * CHIPS + chip

    def first(self, way, index):
        return send(
            self.part.at[:, self.piece(way, index, True), :, self.cols[way]],
            self.near[way].at[index],
            self.ns.at[way, index],
            self.nr.at[way, index],
            self.me.beside(way)[1],
        )

    def second(self, way):
        a, b = self.me.ch // 2, lax.rem(self.me.ch, 2)
        other = 1 - a if way == 0 else 1 - b
        return send(
            self.part.at[:, self.piece(way, other, False), :, self.cols[way]],
            self.far[way],
            self.fs.at[way],
            self.fr.at[way],
            self.me.beside(1 - way)[1],
        )

    def start(self):
        self.swap().start()

    def chip_sums(self):
        me = self.me
        self.swap().wait_recv()

        @pl.loop(0, CHIPS)
        def _(j):
            for m in range(self.half.shape[0]):
                self.part[m, me.c * CHIPS + j] = (
                    self.part[m, me.c * CHIPS + j].astype(F32) + self.half[m, j].astype(F32)
                ).astype(BF)

        for way in range(2):
            for index in range(2):
                self.first(way, index).start()

    def pair_sums(self):
        for way in range(2):
            for index in range(2):
                self.first(way, index).wait_recv()
            cols = self.cols[way]
            for index in range(2):
                piece = self.piece(way, index, False)
                for m in range(self.half.shape[0]):
                    self.part[m, piece, :, cols] = (
                        self.part[m, piece, :, cols].astype(F32)
                        + self.near[way][index, m].astype(F32)
                    ).astype(BF)
            self.second(way).start()

    def to_group(self, k, slot):
        me = self.me
        count = me.data // PLANE
        other = lax.rem(me.d // PLANE + k, count)
        return send(
            self.total,
            self.groups.at[slot],
            self.gs.at[k],
            self.gr.at[slot],
            (other * PLANE + me.r, me.z),
        )

    def sum_up(self):
        me = self.me
        for way in range(2):
            self.second(way).wait_recv()
            cols = self.cols[way]
            for m in range(self.total.shape[0]):
                self.total[m, :, cols] = (
                    self.part[m, me.piece, :, cols].astype(F32) + self.far[way][m].astype(F32)
                ).astype(BF)
        count = me.data // PLANE
        if count > 1:
            own = me.d // PLANE
            for k in range(1, count):
                self.to_group(k, own).start()
            for k in range(1, count):
                self.to_group(k, lax.rem(own + k, count)).wait_recv()
                self.to_group(k, own).wait_send()
            self.groups[own] = self.total[...]
            total = self.groups[0].astype(F32)
            for e in range(1, count):
                total = total + self.groups[e].astype(F32)
            self.total[...] = total.astype(BF)

    def finish(self):
        self.swap().wait_send()
        for way in range(2):
            for index in range(2):
                self.first(way, index).wait_send()
            self.second(way).wait_send()


def reduce_scratch(m, rp, cols, groups):
    mem, dma = pltpu.VMEM, pltpu.SemaphoreType.DMA
    widths = [part.stop - part.start for part in halves(cols)]
    return (
        [mem((m, CHIPS, rp, cols), BF)]
        + [mem((2, m, rp, width), BF) for width in widths]
        + [mem((m, rp, width), BF) for width in widths]
        + [
            mem((m, rp, cols), BF),
            mem((groups, m, rp, cols) if groups > 1 else (1, 1, 16, 128), BF),
            dma,
            dma,
            dma((2, 2)),
            dma((2, 2)),
            dma((2,)),
            dma((2,)),
            dma((groups,)),
            dma((groups,)),
        ]
    )


def take_reduce(me, part, take):
    half, near0, near1, far0, far1, total, groups = take(7)
    return GradReduce(me, part, half, (near0, near1), (far0, far1), total, groups, take(8))


class GradShare:
    def __init__(self, me, final, sems):
        self.me, self.final = me, final
        self.ss, self.sr, self.fs, self.fr, self.hs, self.hr = sems
        self.cols = halves(final.shape[2])

    def own(self, way, source=None):
        mine = self.final.at[self.me.piece]
        return send(
            mine if source is None else source,
            mine,
            self.ss.at[way],
            self.sr.at[way],
            self.me.beside(way)[1],
        )

    def to_partner(self, index, chip, core, source=None):
        got = self.final.at[core * CHIPS + chip]
        return send(
            got if source is None else source,
            got,
            self.hs.at[index],
            self.hr.at[index],
            self.me.partner(),
        )

    def onward(self, way, chip):
        got = self.final.at[self.me.c * CHIPS + chip, :, self.cols[way]]
        return send(got, got, self.fs.at[way], self.fr.at[way], self.me.beside(1 - way)[1])

    def across(self):
        return CHIPS - 1 - self.me.ch

    def start(self, source=None):
        for way in range(2):
            self.own(way, source).start()
        self.to_partner(0, self.me.ch, self.me.c, source).start()

    def forward(self):
        me = self.me
        for way in range(2):
            chip = me.beside(way)[0]
            got = self.final.at[me.c * CHIPS + chip]
            send(got, got, self.ss.at[way], self.sr.at[way], me.beside(way)[1]).wait_recv()
            self.onward(way, chip).start()
            self.to_partner(1 + way, chip, me.c).start()

    def hand(self):
        for way in range(2):
            self.onward(way, self.across()).wait_recv()
        self.to_partner(3, self.across(), self.me.c).start()

    def finish(self):
        me = self.me
        chips = [me.ch, me.beside(0)[0], me.beside(1)[0], self.across()]
        for way in range(2):
            self.own(way).wait_send()
            self.onward(way, chips[1 + way]).wait_send()
        for index, chip in enumerate(chips):
            self.to_partner(index, chip, me.c).wait_send()
            self.to_partner(index, chip, 1 - me.c).wait_recv()


def share_sems():
    dma = pltpu.SemaphoreType.DMA
    return [dma((2,))] * 4 + [dma((4,))] * 2


class RowsBack:
    def __init__(self, me, total, final, ssem, rsem, lsem):
        self.me, self.total, self.final = me, total, final
        self.ssem, self.rsem, self.lsem = ssem, rsem, lsem

    def place(self, src_z):
        cols = self.total.shape[2]
        return self.final.at[
            self.me.piece, :, pl.ds(pl.multiple_of(src_z * cols, cols), cols)
        ]

    def copy(self, k, slot):
        other, to = self.me.seq_peer(k)
        return send(
            self.total.at[other], self.place(slot), self.ssem.at[k], self.rsem.at[slot], to
        )

    def own(self):
        me = self.me
        return pltpu.make_async_copy(self.total.at[me.z], self.place(me.z), self.lsem)

    def start(self):
        for k in range(1, self.me.n):
            self.copy(k, self.me.z).start()
        self.own().start()

    def wait(self):
        me = self.me
        for k in range(1, me.n):
            self.copy(k, me.seq_peer(k)[0]).wait_recv()
        self.own().wait()

    def finish(self):
        for k in range(1, self.me.n):
            self.copy(k, self.me.z).wait_send()


def reduce_kernel(n, data, *refs):
    (OP, DX, v1, v2, bias, x, g, UG, QG, DnG, DeG) = refs[:11]
    out, dx, small, fu, fq, fdn, fde = refs[11:18]
    scratch = list(refs[18:])
    me = Place(n, data)

    def take(count):
        got = scratch[:count]
        del scratch[:count]
        return got

    og, xg, zs, zr, v1g, v1s, v1r, v2m, v2g, v2s, v2r = take(11)
    reduces = []
    for part in (DnG, DeG, UG, QG):
        reduces.append(take_reduce(me, part, take))
    red_dn, red_de, red_u, red_q = reduces
    shares = [GradShare(me, final, take(6)) for final in (fdn, fde, fu, fq)]
    back_u = RowsBack(me, red_u.total, fu, *take(3))
    back_q = RowsBack(me, red_q.total, fq, *take(3))
    (dsem,) = take(1)
    assert not scratch
    ro = RowReduce(me, OP, og, zs.at[0], zr.at[0])
    rx = RowReduce(me, DX, xg, zs.at[1], zr.at[1])
    me.barrier()
    cs = v1g.shape[2]

    def small_z(k, slot):
        other, to = me.seq_peer(k)
        return send(
            v1.at[:, pl.ds(pl.multiple_of(other * cs, cs), cs)],
            v1g.at[slot],
            v1s.at[k],
            v1r.at[slot],
            to,
        )

    def small_dp(k, slot):
        return send(v2m, v2g.at[slot], v2s.at[k], v2r.at[slot], me.dp_peer(k)[1])

    for k in range(1, n):
        small_z(k, me.z).start()
    for red in reduces:
        red.start()
    ro.start()
    rx.start()
    for red in reduces:
        red.chip_sums()
    for red in reduces:
        red.pair_sums()
    for k in range(1, n):
        small_z(k, me.seq_peer(k)[0]).wait_recv()
    v1g[me.z] = v1[:, pl.ds(pl.multiple_of(me.z * cs, cs), cs)]
    total = v1g[0]
    for k in range(1, n):
        total = total + v1g[k]
    v2m[0:8] = total
    v2m[8:16] = v2[...]
    for k in range(1, data):
        small_dp(k, me.d).start()
    own = []
    for i, (red, final) in enumerate(((red_dn, fdn), (red_de, fde))):
        red.sum_up()
        copy = pltpu.make_async_copy(red.total.at[0], final.at[me.piece], dsem.at[i])
        copy.start()
        own.append(copy)
    red_u.sum_up()
    back_u.start()
    red_q.sum_up()
    back_q.start()
    for copy in own:
        copy.wait()
    shares[0].start()
    shares[1].start()
    back_u.wait()
    shares[2].start()
    back_q.wait()
    shares[3].start()
    for share in shares:
        share.forward()
    for share in shares:
        share.hand()
    for k in range(1, data):
        small_dp(k, me.dp_peer(k)[0]).wait_recv()
    v2g[me.d] = v2m[...]

    def add(i, acc):
        return acc + v2g[i]

    small[...] = lax.fori_loop(1, data, add, v2g[0])
    rows = x.shape[0]
    for red, base, result, extra in ((ro, x, out, bias), (rx, g, dx, None)):
        red.wait()
        step = rows // 4

        @pl.loop(0, 4)
        def _(i):
            at = pl.ds(pl.multiple_of(i * step, step), step)
            mine = pl.ds(pl.multiple_of(me.z * rows + i * step, step), step)
            acc = base[at].astype(F32) + red.part[mine].astype(F32)
            for k in range(1, n):
                acc = acc + red.got[me.seq_peer(k)[0], at].astype(F32)
            if extra is not None:
                acc = acc + extra[...]
            result[at] = acc.astype(BF)

        red.finish()
    for k in range(1, n):
        small_z(k, me.z).wait_send()
    for k in range(1, data):
        small_dp(k, me.d).wait_send()
    for red in reduces:
        red.finish()
    for share in shares:
        share.finish()
    back_u.finish()
    back_q.finish()


def reduce_all(n, data, OP, DX, v1, v2, bias, x, g, UG, QG, DnG, DeG):
    vm = pl.BlockSpec(memory_space=pltpu.VMEM)
    dma = pltpu.SemaphoreType.DMA
    sds = jax.ShapeDtypeStruct
    rows, width = x.shape
    groups = data // PLANE
    parts = []
    for whole in (DnG, DeG):
        lead, cols = whole.shape
        parts.append(whole.reshape(1, PLANE, lead // PLANE, cols))
    for whole in (UG, QG):
        lead, cols = whole.shape
        parts.append(whole.reshape(n, PLANE, lead // n // PLANE, cols))
    dn, de, u, q = parts
    scratch = [
        pltpu.VMEM((n, rows, width), BF),
        pltpu.VMEM((n, rows, width), BF),
        dma((2, n)),
        dma((2, n)),
        pltpu.VMEM((n, 8, width // n), F32),
        dma((n,)),
        dma((n,)),
        pltpu.VMEM((16, width // n), F32),
        pltpu.VMEM((data, 16, width // n), F32),
        dma((data,)),
        dma((data,)),
    ]
    for part in (dn, de, u, q):
        m, unused, rp, cols = part.shape
        scratch += reduce_scratch(m, rp, cols, groups)
    for unused in range(4):
        scratch += share_sems()
    scratch += [dma((n,)), dma((n,)), dma] * 2
    scratch += [dma((2,))]
    outs = [
        sds((rows, width), BF),
        sds((rows, width), BF),
        sds((16, width // n), F32),
        sds((PLANE, u.shape[2], u.shape[3] * n), BF),
        sds((PLANE, q.shape[2], q.shape[3] * n), BF),
        sds((PLANE,) + dn.shape[2:], BF),
        sds((PLANE,) + de.shape[2:], BF),
    ]
    return pl.pallas_call(
        functools.partial(reduce_kernel, n, data),
        out_shape=outs,
        in_specs=[vm] * 11,
        out_specs=[vm] * 7,
        scratch_shapes=scratch,
        compiler_params=pltpu.CompilerParams(
            collective_id=1, has_side_effects=True, vmem_limit_bytes=63 << 20
        ),
        name="reduce",
    )(OP, DX, v1, v2, bias, x, g, u, q, dn, de)


def layer_norm_parts(token_rows):
    average = jnp.mean(token_rows, axis=-1, keepdims=True)
    centered = token_rows - average
    variance = jnp.mean(centered * centered, axis=-1, keepdims=True)
    inverse = lax.rsqrt(variance + epsilon)
    return centered * inverse, inverse


def rotate(packed, positions, sign):
    half = ROT_DIM // 2
    freqs = 10000.0 ** (-jnp.arange(half, dtype=F32) * 2.0 / ROT_DIM)
    angles = positions.astype(F32)[:, None] * freqs[None, :]
    cosine = jnp.cos(angles)[:, None, None, :]
    sine = jnp.sin(angles)[:, None, None, :] * sign
    first = packed[..., :half]
    second = packed[..., half:ROT_DIM]
    turned = jnp.concatenate(
        [first * cosine - second * sine, second * cosine + first * sine, packed[..., ROT_DIM:]],
        axis=-1,
    )
    select = (jnp.arange(3) < 2)[:, None]
    return jnp.where(select, turned, packed)


def middle(X, G, WQ, WU, w_dense, w_down, b_qkv, b_up, vectors):
    length, width = X.shape
    heads = WQ.shape[1] // (3 * HEAD_DIM)
    scale = HEAD_DIM ** (-0.5)
    gain_one, shift_one, gain_two, shift_two = (vectors[i] for i in range(4))
    xhat, inverse = layer_norm_parts(X.astype(F32))
    norm_one = (xhat * gain_one + shift_one).astype(BF)
    norm_two = (xhat * gain_two + shift_two).astype(BF)
    packed = jnp.dot(norm_one, WQ, preferred_element_type=F32) + b_qkv.astype(F32)
    positions = jnp.arange(length, dtype=jnp.int32)
    packed = rotate(packed.reshape(length, heads, 3, HEAD_DIM), positions, 1.0).astype(BF)
    query, keys, values = packed[:, :, 0], packed[:, :, 1], packed[:, :, 2]
    scores = jnp.einsum("qhd,khd->hqk", query, keys, preferred_element_type=F32) * scale
    allowed = positions[:, None] >= positions[None, :]
    probs = jax.nn.softmax(jnp.where(allowed, scores, mask_fill), axis=-1)
    low = probs.astype(BF)
    context = jnp.einsum("hqk,khd->qhd", low, values, preferred_element_type=F32)
    context = context.astype(BF).reshape(length, heads * HEAD_DIM)
    hidden = jnp.dot(norm_two, WU, preferred_element_type=F32) + b_up.astype(F32)
    active = jax.nn.gelu(hidden, approximate=False).astype(BF)
    out = jnp.dot(context, w_dense, preferred_element_type=F32) + jnp.dot(
        active, w_down, preferred_element_type=F32
    )
    down_grad = jnp.einsum("tf,to->fo", active, G, preferred_element_type=F32)
    dense_grad = jnp.einsum("ti,to->io", context, G, preferred_element_type=F32)
    active_grad = jnp.einsum("to,fo->tf", G, w_down, preferred_element_type=F32)
    unused, pull = jax.vjp(lambda v: jax.nn.gelu(v, approximate=False), hidden)
    hidden_grad = pull(active_grad)[0].astype(BF)
    up_bias_grad = jnp.sum(hidden_grad.astype(F32), axis=0)
    up_grad = jnp.einsum("ti,tf->if", norm_two, hidden_grad, preferred_element_type=F32)
    norm_two_grad = jnp.einsum("tf,if->ti", hidden_grad, WU, preferred_element_type=F32)
    context_grad = jnp.einsum("to,io->ti", G, w_dense, preferred_element_type=F32).astype(BF)
    context_grad = context_grad.reshape(length, heads, HEAD_DIM)
    prob_grad = jnp.einsum("qhd,khd->hqk", context_grad, values, preferred_element_type=F32)
    weighted = jnp.sum(probs * prob_grad, axis=-1, keepdims=True)
    score_grad = (probs * (prob_grad - weighted)).astype(BF)
    query_grad = jnp.einsum("hqk,khd->qhd", score_grad, keys, preferred_element_type=F32) * scale
    key_grad = jnp.einsum("hqk,qhd->khd", score_grad, query, preferred_element_type=F32) * scale
    value_grad = jnp.einsum("hqk,qhd->khd", low, context_grad, preferred_element_type=F32)
    rotated_grad = jnp.stack([query_grad, key_grad, value_grad], axis=2).astype(BF).astype(F32)
    packed_grad = rotate(rotated_grad, positions, -1.0).reshape(length, -1).astype(BF)
    qkv_bias_grad = jnp.sum(packed_grad.astype(F32), axis=0)
    qkv_grad = jnp.einsum("ti,tj->ij", norm_one, packed_grad, preferred_element_type=F32)
    norm_one_grad = jnp.einsum("tj,ij->ti", packed_grad, WQ, preferred_element_type=F32)
    u = norm_one_grad * gain_one + norm_two_grad * gain_two
    mean_u = jnp.mean(u, axis=-1, keepdims=True)
    mean_ux = jnp.mean(u * xhat, axis=-1, keepdims=True)
    dx = inverse * (u - mean_u - xhat * mean_ux)
    sums = jnp.stack(
        [
            jnp.sum(norm_one_grad * xhat, axis=0),
            jnp.sum(norm_one_grad, axis=0),
            jnp.sum(norm_two_grad * xhat, axis=0),
            jnp.sum(norm_two_grad, axis=0),
        ]
    )
    return (
        out.astype(BF),
        dx.astype(BF),
        sums,
        up_bias_grad,
        qkv_bias_grad,
        up_grad.astype(BF),
        qkv_grad.astype(BF),
        down_grad.astype(BF),
        dense_grad.astype(BF),
    )


NN = (((1,), (0,)), ((), ()))
NT = (((1,), (1,)), ((), ()))
TN = (((0,), (0,)), ((), ()))
ROOT_HALF = 0.7071067811865476
PDF_SCALE = 0.3989422804014327


def dot(left, right, dims=NN):
    return lax.dot_general(left, right, dims, preferred_element_type=F32)


def rotary_tables(length):
    half = ROT_DIM // 2
    freqs = 10000.0 ** (-jnp.arange(half, dtype=F32) * 2.0 / ROT_DIM)
    angles = jnp.arange(length, dtype=jnp.int32).astype(F32)[:, None] * freqs[None, :]
    cosine, sine = jnp.cos(angles), jnp.sin(angles)
    rest = HEAD_DIM - ROT_DIM
    keep, none, gap = jnp.ones((length, rest)), jnp.zeros((length, rest)), jnp.zeros_like(sine)
    same = jnp.concatenate([cosine, cosine, keep] * 2, axis=1)
    up = jnp.concatenate([-sine, gap, none] * 2, axis=1)
    down = jnp.concatenate([gap, sine, none] * 2, axis=1)
    return jnp.stack([same, up, down]).astype(F32)


class Layer:
    def __init__(self, rows, refs):
        self.rows = rows
        for name, ref in refs.items():
            setattr(self, name, ref)
        self.length, self.width = self.X.shape
        self.heads = self.Q.shape[0]
        self.block = min(256, self.length)

    def at(self, j, rows=None, part=0):
        rows = rows or self.rows
        return pl.ds(pl.multiple_of(j * self.rows + part * rows, rows), rows)

    def norm(self, j):
        step = 64

        @pl.loop(0, self.rows // step)
        def _(i):
            at = self.at(j, step, i)
            x = self.X[at].astype(F32)
            average = jnp.mean(x, axis=-1, keepdims=True)
            centered = x - average
            variance = jnp.mean(centered * centered, axis=-1, keepdims=True)
            inverse = lax.rsqrt(variance + epsilon)
            xhat = centered * inverse
            self.STAT[at, 0:1] = average
            self.STAT[at, 1:2] = inverse
            self.N1[at] = (xhat * self.VEC[0:1] + self.VEC[1:2]).astype(BF)
            self.N2[at] = (xhat * self.VEC[2:3] + self.VEC[3:4]).astype(BF)

    def turn(self, values, at, kind, sign):
        lanes = lax.broadcasted_iota(jnp.int32, values.shape, 1)
        turned = values * self.ROT[0, at] + sign * (
            pltpu.roll(values, 128 - ROT_DIM // 2, 1) * self.ROT[1, at]
            + pltpu.roll(values, ROT_DIM // 2, 1) * self.ROT[2, at]
        )
        if kind == 0:
            return turned
        return jnp.where((lanes >= HEAD_DIM) if kind == 1 else (lanes < HEAD_DIM), turned, values)

    def qkv(self, j):
        at = self.at(j)
        scale = HEAD_DIM ** (-0.5)
        packed = dot(self.N1[at], self.WQ[...])
        bias = self.BQ[...]
        places = [(self.Q, scale, None), (self.K, None, self.KT), (self.V, None, self.VT)]
        for t in range(packed.shape[1] // 128):
            cols = slice(t * 128, t * 128 + 128)
            low = self.turn(packed[:, cols] + bias[:, cols], at, t % 3, 1.0).astype(BF)
            across = low.T
            for side in range(2):
                index = 2 * t + side
                ref, factor, turned = places[index % 3]
                half = slice(side * HEAD_DIM, side * HEAD_DIM + HEAD_DIM)
                value = low[:, half]
                ref[index // 3, at] = value if factor is None else value * jnp.asarray(factor, BF)
                if turned is not None:
                    turned[index // 3, :, at] = across[half]

    def up(self, j):
        at = self.at(j)
        tile = 256

        for i in range(self.WU.shape[1] // tile):
            cols = slice(i * tile, i * tile + tile)
            hidden = dot(self.N2[at], self.WU[:, cols]) + self.BU[:, cols]
            cdf = 0.5 + 0.5 * lax.erf(hidden * ROOT_HALF)
            self.ACT[at, cols] = (hidden * cdf).astype(BF)
            pdf = PDF_SCALE * jnp.exp(-0.5 * hidden * hidden)
            self.DG[at, cols] = cdf + hidden * pdf

    def down(self, j):
        at = self.at(j)
        self.ACC[at] = dot(self.ACT[at], self.WDN[...])

    def masked(self, scores):
        rows = lax.broadcasted_iota(jnp.int32, scores.shape, 0)
        cols = lax.broadcasted_iota(jnp.int32, scores.shape, 1)
        return jnp.where(rows <= cols, scores, mask_fill)

    def attend_block(self, m, qb):
        size = self.block
        mine, before = slice(qb * size, qb * size + size), slice(0, qb * size)
        sides = []
        for side in range(2):
            h = 2 * m + side
            q = self.Q[h, mine]
            near = self.masked(dot(self.K[h, mine], q, NT))
            top = jnp.max(near, axis=0, keepdims=True)
            if qb:
                far = dot(self.K[h, before], q, NT)
                top = jnp.maximum(top, jnp.max(far, axis=0, keepdims=True))
            near = jnp.exp(near - top)
            total = jnp.sum(near, axis=0, keepdims=True)
            if qb:
                far = jnp.exp(far - top)
                total = total + jnp.sum(far, axis=0, keepdims=True)
            inverse = 1.0 / total
            self.LSE[h, :, mine] = top + jnp.log(total)
            context = dot(self.VT[h, :, mine], (near * inverse).astype(BF))
            if qb:
                context = context + dot(self.VT[h, :, before], (far * inverse).astype(BF))
            sides.append(context.astype(BF))
        self.CTX[m, mine] = jnp.concatenate(sides, axis=0).T

    def attend_part(self, qb):
        @pl.loop(0, self.heads // 2)
        def _(m):
            self.attend_block(m, qb)

    def out(self, j):
        at = self.at(j)
        total = self.ACC[at]
        for m in range(self.heads // 2):
            total = total + dot(self.CTX[m, at], self.WDE[m * 128 : m * 128 + 128])
        self.OP[at] = total.astype(BF)

    def mlp_back(self, j):
        at = self.at(j)
        tile = 256

        for i in range(self.WU.shape[1] // tile):
            cols = slice(i * tile, i * tile + tile)
            active_grad = dot(self.G[at], self.WDN[cols], NT)
            self.HG[at, cols] = (active_grad * self.DG[at, cols]).astype(BF)

        self.ACC[at] = dot(self.HG[at], self.WU[...], NT)

    def context_grad(self, j):
        at = self.at(j)
        for m in range(self.heads // 2):
            self.DO[m, at] = dot(self.G[at], self.WDE[m * 128 : m * 128 + 128], NT).astype(BF)

    def back_block(self, m, qb):
        size = self.block
        mine, before = slice(qb * size, qb * size + size), slice(0, qb * size)
        scale = HEAD_DIM ** (-0.5)
        upstream = self.DO[m, mine]
        values, keys, queries, values_before, keys_before = [], [], [], [], []
        for side in range(2):
            h = 2 * m + side
            q = self.Q[h, mine]
            do = upstream[:, side * HEAD_DIM : side * HEAD_DIM + HEAD_DIM]
            lse = self.LSE[h, :, mine]
            near = jnp.exp(self.masked(dot(self.K[h, mine], q, NT)) - lse)
            near_grad = dot(self.V[h, mine], do, NT)
            weighted = jnp.sum(near * near_grad, axis=0, keepdims=True)
            if qb:
                far = jnp.exp(dot(self.K[h, before], q, NT) - lse)
                far_grad = dot(self.V[h, before], do, NT)
                weighted = weighted + jnp.sum(far * far_grad, axis=0, keepdims=True)
            values.append(dot(near.astype(BF), do))
            score = (near * (near_grad - weighted)).astype(BF)
            keys.append(dot(score, q))
            query = dot(self.KT[h, :, mine], score)
            if qb:
                values_before.append(dot(far.astype(BF), do))
                score = (far * (far_grad - weighted)).astype(BF)
                keys_before.append(dot(score, q))
                query = query + dot(self.KT[h, :, before], score)
            queries.append((query * scale).astype(BF))
        self.DV[m, mine] += jnp.concatenate(values, axis=1)
        self.DK[m, mine] += jnp.concatenate(keys, axis=1)
        self.DQ[m, mine] = jnp.concatenate(queries, axis=0).T
        if qb:
            self.DV[m, before] += jnp.concatenate(values_before, axis=1)
            self.DK[m, before] += jnp.concatenate(keys_before, axis=1)

    def attend_back(self, j, m):
        for qb in range(self.length // self.block):

            @pl.when(j == qb)
            def _():
                self.back_block(m, qb)

    def unturn(self, j):
        at = self.at(j)
        for m in range(self.heads // 2):
            q = self.DQ[m, at].astype(F32)
            k = pltpu.roll(self.DK[m, at], HEAD_DIM, 1).astype(BF).astype(F32)
            v = self.DV[m, at].astype(BF).astype(F32)
            left = lax.broadcasted_iota(jnp.int32, q.shape, 1) < HEAD_DIM
            for kind, pair in enumerate(((q, k), (v, q), (k, v))):
                both = jnp.where(left, *pair)
                cols = slice((3 * m + kind) * 128, (3 * m + kind) * 128 + 128)
                self.PG[at, cols] = self.turn(both, at, kind, -1.0).astype(BF)

    def zero_sums(self):
        self.SUMS[...] = jnp.zeros_like(self.SUMS)
        self.COLS[...] = jnp.zeros_like(self.COLS)
        self.DK[...] = jnp.zeros_like(self.DK)
        self.DV[...] = jnp.zeros_like(self.DV)
        self.BUG[...] = jnp.zeros_like(self.BUG)
        self.BQG[...] = jnp.zeros_like(self.BQG)

    def input_back(self, j):
        self.TMP[...] = dot(self.PG[self.at(j)], self.WQ[...], NT)
        ones = jnp.ones((8, self.rows), BF)
        self.BQG[...] += dot(ones, self.PG[self.at(j)])[0:1]
        self.BUG[...] += dot(ones, self.HG[self.at(j)])[0:1]
        step = 32

        @pl.loop(0, self.rows // step)
        def _(i):
            at = self.at(j, step, i)
            here = pl.ds(pl.multiple_of(i * step, step), step)
            inverse = self.STAT[at, 1:2]
            xhat = (self.X[at].astype(F32) - self.STAT[at, 0:1]) * inverse
            one, two = self.TMP[here], self.ACC[at]
            u = one * self.VEC[0:1] + two * self.VEC[2:3]
            mean_u = jnp.mean(u, axis=-1, keepdims=True)
            mean_ux = jnp.mean(u * xhat, axis=-1, keepdims=True)
            self.DX[at] = (inverse * (u - mean_u - xhat * mean_ux)).astype(BF)
            for row, value in enumerate((one * xhat, one, two * xhat, two)):
                folded = value[0:8]
                for r in range(8, step, 8):
                    folded = folded + value[r : r + 8]
                self.COLS[row] += folded

    def fold_sums(self):
        for row in range(4):
            self.SUMS[row : row + 1] = jnp.sum(self.COLS[row], axis=0, keepdims=True)

    def weight_grad(self, left, right, put, at):
        tile = 256

        @pl.loop(0, left.shape[1] // tile)
        def _(i):
            cols = pl.ds(pl.multiple_of(i * tile, tile), tile)
            put(i, dot(left[at, cols], right[at], TN))

    def down_grad(self, put, at, core, half_done):
        tile = 256
        count = self.ACT.shape[1] // tile

        @pl.loop(0, count)
        def _(k):
            i = lax.rem(k + (1 - core) * (count // 2), count)
            cols = pl.ds(pl.multiple_of(i * tile, tile), tile)
            put(i, dot(self.ACT[at, cols], self.G[at], TN))

            @pl.when(k == count // 2 - 1)
            def _():
                half_done()

    def up_grad(self, put, at):
        self.weight_grad(self.N2, self.HG, put, at)

    def qkv_grad(self, put):
        self.weight_grad(self.N1, self.PG, put, slice(0, self.length))

    def dense_grad(self, put, at):
        for m in range(self.heads // 2):
            put(m, dot(self.CTX[m, at], self.G[at], TN))


def layer_scratch(length, width, heads, hidden):
    vm = pltpu.VMEM
    pairs, packed = heads // 2, heads * 3 * HEAD_DIM
    return dict(
        STAT=vm((length, 2), F32),
        N1=vm((length, width), BF),
        N2=vm((length, width), BF),
        Q=vm((heads, length, HEAD_DIM), BF),
        K=vm((heads, length, HEAD_DIM), BF),
        V=vm((heads, length, HEAD_DIM), BF),
        ACT=vm((length, hidden), BF),
        DG=vm((length, hidden), F32),
        ACC=vm((length, width), F32),
        LSE=vm((heads, 1, length), F32),
        KT=vm((heads, HEAD_DIM, length), BF),
        VT=vm((heads, HEAD_DIM, length), BF),
        CTX=vm((pairs, length, 2 * HEAD_DIM), BF),
        DO=vm((pairs, length, 2 * HEAD_DIM), BF),
        HG=vm((length, hidden), BF),
        DQ=vm((pairs, length, 2 * HEAD_DIM), BF),
        DK=vm((pairs, length, 2 * HEAD_DIM), F32),
        DV=vm((pairs, length, 2 * HEAD_DIM), F32),
        PG=vm((length, packed), BF),
    )


class LineReduce:
    def __init__(self, me, part, got, ssem, rsem):
        self.me, self.part, self.got, self.ssem, self.rsem = me, part, got, ssem, rsem
        self.parts, self.rows = got.shape[1:3]

    def copy(self, j, p, way):
        me = self.me
        to = jnp.minimum(me.z + 1, me.n - 1) if way == 0 else jnp.maximum(me.z - 1, 0)
        slot = j if way == 0 else jnp.where(j == to, me.n, j)
        return send(
            rows_at(self.part, (j * self.parts + p) * self.rows, self.rows),
            self.got.at[slot, p],
            self.ssem.at[j, p],
            self.rsem.at[slot, p],
            (me.d, to),
        )

    def came(self, slot, p):
        me = self.me
        got = self.got.at[slot, p]
        return send(got, got, self.ssem.at[0, p], self.rsem.at[slot, p], (me.d, me.z))

    def start(self, j, which=None):
        me = self.me
        for p in range(self.parts) if which is None else which:

            @pl.when((me.z == 0) & (j > 0))
            def _():
                self.copy(j, p, 0).start()

            @pl.when((me.z == me.n - 1) & (j < me.n - 1))
            def _():
                self.copy(j, p, 1).start()

    def add(self, j, p):
        step = 64

        @pl.loop(0, self.rows // step)
        def _(i):
            mine = pl.ds(pl.multiple_of((j * self.parts + p) * self.rows + i * step, step), step)
            here = pl.ds(pl.multiple_of(i * step, step), step)
            self.part[mine] = (
                self.part[mine].astype(F32) + self.got[j, p, here].astype(F32)
            ).astype(BF)

    def step(self, t, which=None):
        me = self.me
        n = me.n
        for p in range(self.parts) if which is None else which:
            for way, e in ((0, t - me.z), (1, t - (n - 1 - me.z))):
                j = n - 1 - e if way == 0 else e
                valid = (me.z > 0) & (me.z < n - 1) & (e >= 0)
                valid = valid & ((j > me.z) if way == 0 else (j < me.z))

                @pl.when(valid)
                def _():
                    self.came(j, p).wait_recv()
                    self.add(j, p)
                    self.copy(j, p, way).start()

    def total(self, base, extra, result, tmp):
        me = self.me
        step = 64
        for p in range(self.parts):

            @pl.when(me.z > 0)
            def _():
                self.came(me.z, p).wait_recv()

            @pl.when(me.z < me.n - 1)
            def _():
                self.came(me.n, p).wait_recv()

            @pl.loop(0, self.rows // step)
            def _(i):
                at = p * self.rows + i * step
                here = pl.ds(pl.multiple_of(i * step, step), step)
                there = pl.ds(pl.multiple_of(at, step), step)
                mine = pl.ds(pl.multiple_of(me.z * self.parts * self.rows + at, step), step)
                tmp[here] = base[mine].astype(F32) + self.part[mine].astype(F32)
                if extra is not None:
                    tmp[here] += extra

                @pl.when(me.z > 0)
                def _():
                    tmp[here] += self.got[me.z, p, here].astype(F32)

                @pl.when(me.z < me.n - 1)
                def _():
                    tmp[here] += self.got[me.n, p, here].astype(F32)

                result[there] = tmp[here].astype(BF)

    def finish(self):
        me = self.me
        for j in range(me.n):
            for p in range(self.parts):

                @pl.when((j > me.z) & (me.z < me.n - 1))
                def _():
                    self.copy(j, p, 0).wait_send()

                @pl.when((j < me.z) & (me.z > 0))
                def _():
                    self.copy(j, p, 1).wait_send()


def nearest(n):
    return [sorted(range(n), key=lambda j: abs(j - z)) for z in range(n)]


def pick(table, z, k):
    value = jnp.int32(0)
    for at, row in enumerate(table):
        for index, entry in enumerate(row):
            if entry:
                value = jnp.where((z == at) & (k == index), entry, value)
    return value


VECTORS = 6


def layer_kernel(n, data, chunks, names, *refs):
    refs = list(refs)

    def take(count):
        got = refs[:count]
        del refs[:count]
        return got

    vectors = take(VECTORS)
    x, g, wq, wu, wde, wdn, rot, bq, bu = take(9)
    out, dx, small, fu, fq, fdn, fde = take(7)
    ins = dict(zip(names, take(len(names))))
    rows = out.shape[0]
    layer = Layer(rows, ins)
    me = Place(n, data)
    SM, sm = take(2)
    layer.DX = layer.ACT
    lsem, ss, sr, xs, xr, gs, gr = take(7)
    cq, cu = ColumnGather(me, wq, layer.WQ, take(5)), ColumnGather(me, wu, layer.WU, take(5))
    og, xg, os, orr, ds, dr = take(6)
    v1, v1g, v1s, v1r, v2m, v2g, v2s, v2r = take(8)
    reduces = []
    for unused in range(4):
        reduces.append(take_reduce(me, take(1)[0], take))
    red_dn, red_de, red_u, red_q = reduces
    shares = [GradShare(me, final, take(6)) for final in (fdn, fde, fu, fq)]
    share_dn, share_de, share_u, share_q = shares
    back_u = RowsBack(me, red_u.total, fu, *take(3))
    back_q = RowsBack(me, red_q.total, fq, *take(3))
    (dsem,) = take(1)
    assert not refs
    lx = LineGather(me, x, layer.X, rows, chunks, xs, xr)
    lg = LineGather(me, g, layer.G, rows, chunks, gs, gr)
    ro = LineReduce(me, layer.OP, og, os, orr)
    rx = LineReduce(me, layer.ACT, xg, ds, dr)
    near = nearest(n)
    far = [list(range(n - 1, -1, -1)) if 2 * z < n else list(range(n)) for z in range(n)]
    depth = wq.shape[0]
    part = depth

    own = [
        pltpu.make_async_copy(x, rows_at(layer.X, me.z * rows, rows), lsem.at[0]),
        pltpu.make_async_copy(g, rows_at(layer.G, me.z * rows, rows), lsem.at[1]),
        pltpu.make_async_copy(
            block_at(wq, 0, depth, me.z * layer.WQ.shape[1], layer.WQ.shape[1]),
            rows_at(layer.WQ, me.z * depth, depth),
            lsem.at[2],
        ),
        pltpu.make_async_copy(
            block_at(wu, 0, depth, me.z * layer.WU.shape[1], layer.WU.shape[1]),
            rows_at(layer.WU, me.z * depth, depth),
            lsem.at[3],
        ),
    ]
    own += [
        pltpu.make_async_copy(source, place, lsem.at[4 + i])
        for i, (source, place) in enumerate(
            ((wde, layer.WDE), (wdn, layer.WDN), (rot, layer.ROT))
        )
    ]
    me.greet()
    for copy in own:
        copy.start()
    sm[...] = jnp.zeros_like(sm)
    for i, vector in enumerate(vectors):
        sm[i] = vector[...].astype(F32)
    layer.BQ[0] = bq[...].astype(F32)
    layer.BU[0] = bu[...].astype(F32)
    me.met()

    def tiny(k, slot):
        return send(sm, SM.at[slot], ss.at[k], sr.at[slot], me.seq_peer(k)[1])

    for k in range(1, n):
        tiny(k, me.z).start()
    cq.start()
    cu.start()
    lx.start()
    SM[me.z] = sm[...]
    layer.zero_sums()
    for k in range(1, n):
        tiny(k, me.seq_peer(k)[0]).wait_recv()
    for i in range(n):
        layer.VEC[:, i * part : i * part + part] = SM[i]
    near_k = sorted({1, n - 1})
    for k in near_k:
        cq.share(k)
        cu.share(k)
    lx.forward(1)
    for k in range(1, n):
        if k not in near_k:
            cq.share(k)
            cu.share(k)
    for s in range(2, n - 1):
        lx.forward(s)
    lg.start()
    own[0].wait()
    layer.norm(me.z)
    for k in range(1, n):
        cq.hand(k)
        cu.hand(k)
    for i in (2, 3, 4, 5, 6):
        own[i].wait()
    cq.finish()
    cu.finish()

    @pl.loop(0, n)
    def _(k):
        j = pick(near, me.z, k)

        @pl.when(k > 0)
        def _():
            lx.arrive(j)
            layer.norm(j)

        layer.qkv(j)
        layer.up(j)
        layer.down(j)

    lg.forward(1)
    blocks = layer.length // layer.block
    for qb in range(blocks):
        layer.attend_part(qb)
        if qb == blocks // 2:
            for s in range(2, n - 1):
                lg.forward(s)

    @pl.loop(0, n)
    def _(k):
        j = pick(far, me.z, k)
        layer.out(j)
        ro.start(j)

    own[1].wait()
    layer.SUMS[4:5] = jnp.sum(layer.G[layer.at(me.z)].astype(F32), axis=0, keepdims=True)

    def put(red):
        def store(i, value):
            parts, unused, rp, cols = red.part.shape
            pieces = value.shape[0] // rp
            value = value.reshape(pieces, rp, cols)
            at = (0, pl.ds(i * pieces, pieces)) if parts == 1 else (i,)
            red.part[at] = value.astype(BF)

        return store

    pairs = layer.heads // 2
    every = slice(0, layer.length)

    @pl.loop(0, n)
    def _(k):
        j = pick(near, me.z, k)
        lg.arrive(j)

        @pl.when(k == n - 1)
        def _():
            layer.down_grad(put(red_dn), every, me.c, red_dn.start)
            layer.dense_grad(put(red_de), every)
            red_de.start()
            red_dn.chip_sums()

        layer.mlp_back(j)
        layer.context_grad(j)

        @pl.when(k == n - 1)
        def _():
            red_de.chip_sums()
            layer.up_grad(put(red_u), every)
            red_u.start()

        @pl.loop(0, pairs)
        def _(m):
            layer.attend_back(j, m)

            @pl.when((k == n - 1) & (m == 0))
            def _():
                red_u.chip_sums()

        @pl.when(k == n - 2)
        def _():
            ro.step(1)

    red_dn.pair_sums()
    red_de.pair_sums()
    for t in range(2, 2 * n - 5):
        ro.step(t)
    copies = [
        pltpu.make_async_copy(red.total.at[0], final.at[me.piece], dsem.at[i])
        for i, (red, final) in enumerate(((red_dn, fdn), (red_de, fde)))
    ]

    @pl.loop(0, n)
    def _(j):
        layer.unturn(j)

    layer.qkv_grad(put(red_q))
    red_q.start()

    @pl.loop(0, n)
    def _(k):
        j = pick(far, me.z, k)
        layer.input_back(j)

        @pl.when(k == 0)
        def _():
            rx.start(j, (0,))
            red_u.pair_sums()
            red_q.chip_sums()
            red_dn.sum_up()
            red_de.sum_up()
            for copy in copies:
                copy.start()
            share_dn.start(red_dn.total.at[0])
            share_de.start(red_de.total.at[0])

        @pl.when(k == 1)
        def _():
            red_u.sum_up()
            back_u.start()
            rx.start(pick(far, me.z, 0), (1,))
            rx.start(j, (0,))

        @pl.when(k == n - 2)
        def _():
            red_q.pair_sums()

    rx.start(pick(far, me.z, 1), (1,))
    layer.fold_sums()
    cs = part
    v1[...] = layer.SUMS[...]

    def small_z(k, slot):
        other, to = me.seq_peer(k)
        return send(
            v1.at[:, pl.ds(pl.multiple_of(other * cs, cs), cs)],
            v1g.at[slot],
            v1s.at[k],
            v1r.at[slot],
            to,
        )

    def small_dp(k, slot):
        return send(v2m, v2g.at[slot], v2s.at[k], v2r.at[slot], me.dp_peer(k)[1])

    for k in range(1, n):
        small_z(k, me.z).start()
    rx.step(1, (0,))
    back_u.wait()
    share_u.start()
    rx.step(1, (1,))
    share_dn.forward()
    share_de.forward()
    red_q.sum_up()
    back_q.start()
    for k in range(2, n - 1):
        rx.start(pick(far, me.z, k))
    ro.total(layer.X, layer.VEC[4:5] + layer.VEC[5:6], out, layer.TMP)
    back_q.wait()
    share_q.start()
    for t in range(2, 2 * n - 5):
        rx.step(t)
    for copy in copies:
        copy.wait()
    share_dn.hand()
    share_de.hand()
    for k in range(1, n):
        small_z(k, me.seq_peer(k)[0]).wait_recv()
    v1g[me.z] = v1[:, pl.ds(pl.multiple_of(me.z * cs, cs), cs)]
    total = v1g[0]
    for k in range(1, n):
        total = total + v1g[k]
    v2m[...] = jnp.zeros_like(v2m)
    v2m[0:8] = total
    for i in range(layer.BUG.shape[1] // cs):
        v2m[8 + i : 9 + i] = layer.BUG[:, i * cs : i * cs + cs]
    for i in range(layer.BQG.shape[1] // cs):
        v2m[12 + i : 13 + i] = layer.BQG[:, i * cs : i * cs + cs]
    for k in range(1, data):
        small_dp(k, me.d).start()
    share_u.forward()
    for k in range(1, data):
        small_dp(k, me.dp_peer(k)[0]).wait_recv()
    v2g[me.d] = v2m[...]

    def add(i, acc):
        return acc + v2g[i]

    small[...] = lax.fori_loop(1, data, add, v2g[0])
    share_q.forward()
    share_u.hand()
    share_q.hand()
    rx.total(layer.G, None, dx, layer.TMP)
    ro.finish()
    rx.finish()
    lx.finish()
    lg.finish()
    for k in range(1, n):
        tiny(k, me.z).wait_send()
        small_z(k, me.z).wait_send()
    for k in range(1, data):
        small_dp(k, me.d).wait_send()
    for red in reduces:
        red.finish()
    for share in shares:
        share.finish()
    back_u.finish()
    back_q.finish()


def rotary_constant(length):
    half = ROT_DIM // 2
    freqs = np.float32(10000.0) ** (-np.arange(half, dtype=np.float32) * np.float32(2.0 / ROT_DIM))
    angles = np.arange(length, dtype=np.float32)[:, None] * freqs.astype(np.float32)[None, :]
    cosine, sine = np.cos(angles), np.sin(angles)
    rest = HEAD_DIM - ROT_DIM
    keep, none, gap = np.ones((length, rest)), np.zeros((length, rest)), np.zeros_like(sine)
    same = np.concatenate([cosine, cosine, keep] * 2, axis=1)
    up = np.concatenate([-sine, gap, none] * 2, axis=1)
    down = np.concatenate([gap, sine, none] * 2, axis=1)
    return np.stack([same, up, down]).astype(np.float32)


def whole_layer(n, data, vectors, x, g, wq, wu, w_dense, w_down, b_qkv, b_up):
    rows, width = x.shape
    length = n * rows
    packed, hidden = wq.shape[1] // n, wu.shape[1] // n
    heads = packed // (3 * HEAD_DIM)
    depth = wq.shape[0]
    chunks = 4
    groups = data // PLANE
    vm = pl.BlockSpec(memory_space=pltpu.VMEM)
    hbm = pl.BlockSpec(memory_space=pl.ANY)
    dma = pltpu.SemaphoreType.DMA
    sds = jax.ShapeDtypeStruct
    mem = pltpu.VMEM
    named = layer_scratch(length, width, heads, hidden)
    named.update(
        X=mem((length, width), BF),
        G=mem((length, width), BF),
        WQ=mem((width, packed), BF),
        WU=mem((width, hidden), BF),
        VEC=mem((8, width), F32),
        WDE=mem(w_dense.shape, BF),
        WDN=mem(w_down.shape, BF),
        ROT=mem((3, length, 128), F32),
        OP=mem((length, width), BF),
        SUMS=mem((8, width), F32),
        BUG=mem((1, hidden), F32),
        BQG=mem((1, packed), F32),
        BQ=mem((1, packed), F32),
        BU=mem((1, hidden), F32),
        TMP=mem((rows, width), F32),
        COLS=mem((4, 8, width), F32),
    )
    scratch = list(named.values())
    scratch += [mem((n, 8, depth), F32), mem((8, depth), F32)]
    scratch += [dma((7,)), dma((n,)), dma((n,))]
    scratch += [dma((2, n, chunks)), dma((n, chunks))] * 2
    scratch += column_sems(n) + column_sems(n)
    scratch += [mem((n + 1, 2, rows // 2, width), BF)] * 2
    scratch += [dma((n, 2)), dma((n + 1, 2))] * 2
    scratch += [mem((8, width), F32), mem((n, 8, depth), F32), dma((n,)), dma((n,))]
    scratch += [mem((16, depth), F32), mem((data, 16, depth), F32), dma((data,)), dma((data,))]
    shapes = [
        (1, hidden // PLANE, width),
        (1, packed // 3 // PLANE, width),
        (n, depth // PLANE, hidden),
        (n, depth // PLANE, packed),
    ]
    for m, rp, cols in shapes:
        scratch += [mem((m, PLANE, rp, cols), BF)] + reduce_scratch(m, rp, cols, groups)
    for unused in range(4):
        scratch += share_sems()
    scratch += [dma((n,)), dma((n,)), dma] * 2
    scratch += [dma((4,))]
    outs = [
        sds((rows, width), BF),
        sds((rows, width), BF),
        sds((16, depth), F32),
        sds((PLANE, depth // PLANE, hidden * n), BF),
        sds((PLANE, depth // PLANE, packed * n), BF),
        sds((PLANE, hidden // PLANE, width), BF),
        sds((PLANE, packed // 3 // PLANE, width), BF),
    ]
    return pl.pallas_call(
        functools.partial(layer_kernel, n, data, chunks, list(named)),
        out_shape=outs,
        in_specs=[vm] * VECTORS + [hbm] * 7 + [vm] * 2,
        out_specs=[vm] * 3 + [hbm] * 4,
        scratch_shapes=scratch,
        compiler_params=pltpu.CompilerParams(
            collective_id=2, has_side_effects=True, vmem_limit_bytes=67043328
        ),
        name="layer",
    )(*vectors, x, g, wq, wu, w_dense, w_down, rotary_constant(length), b_qkv, b_up)


def fits(n, data, tokens, qkv, up):
    unused, rows, width = tokens
    length, depth = n * rows, qkv[0]
    return (
        length * (width + up[1] // n) <= 1024 * 2048
        and rows == 256
        and depth == 256
        and up[1] // n == width
        and up[1] // n % 256 == 0
        and qkv[1] // n % (6 * HEAD_DIM) == 0
    )


def per_device(
    n,
    data,
    layer_input,
    attn_gain,
    attn_shift,
    mlp_gain,
    mlp_shift,
    qkv_weight,
    qkv_bias,
    dense_weight,
    dense_bias,
    up_weight,
    up_bias,
    down_weight,
    down_bias,
    out_grad,
):
    unused, rows, width = layer_input.shape
    x = layer_input.reshape(rows, width)
    g = out_grad.reshape(rows, width)
    part = width // n
    if fits(n, data, layer_input.shape, qkv_weight.shape, up_weight.shape):
        vectors = (attn_gain, attn_shift, mlp_gain, mlp_shift, dense_bias, down_bias)
        out, dx, tiny, fu, fq, fdn, fde = whole_layer(
            n, data, vectors, x, g, qkv_weight, up_weight, dense_weight, down_weight,
            qkv_bias, up_bias,
        )
    else:
        small = jnp.stack(
            [attn_gain, attn_shift, mlp_gain, mlp_shift, dense_bias, down_bias] + [attn_gain] * 2
        ).astype(F32)
        SM, X, G, WQ, WU = gather(n, data, small, x, g, qkv_weight, up_weight)
        vectors = jnp.swapaxes(SM, 0, 1).reshape(8, width)
        bias = (vectors[4] + vectors[5])[None]
        OP, DX, sums, bu, bq, UG, QG, DnG, DeG = middle(
            X, G, WQ, WU, dense_weight, down_weight, qkv_bias, up_bias, vectors
        )
        v1 = jnp.concatenate(
            [sums, jnp.sum(g.astype(F32), axis=0)[None], jnp.zeros((3, width), F32)], axis=0
        )
        v2 = jnp.concatenate(
            [bu.reshape(4, part), bq.reshape(3, part), jnp.zeros((1, part), F32)]
        )
        out, dx, tiny, fu, fq, fdn, fde = reduce_all(
            n, data, OP, DX, v1, v2, bias, x, g, UG, QG, DnG, DeG
        )
    results = finish(part, out, dx, tiny, fu, fq, fdn, fde)
    return tuple(r.reshape(layer_input.shape) for r in results[:2]) + tuple(results[2:])


def finish_kernel(part, out, dx, tiny, fu, fq, fdn, fde, *results):
    (o_out, o_dx, ag, ash, mg, ms, gq, bq, gde, bde, gu, bu, gdn, bdn) = results
    o_out[...] = out[...]
    o_dx[...] = dx[...]
    for source, result in ((fq, gq), (fde, gde), (fu, gu), (fdn, gdn)):
        result[...] = source[...].astype(F32)

    @pl.when(pl.program_id(0) == 0)
    def _():
        for row, result in enumerate((ag, ash, mg, ms, bde)):
            result[...] = tiny[row]
        bdn[...] = tiny[4]
        for base, result in ((8, bu), (12, bq)):
            for i in range(result.shape[0] // part):
                result[i * part : i * part + part] = tiny[base + i]


def finish(part, out, dx, tiny, fu, fq, fdn, fde):
    steps = 4
    sds = jax.ShapeDtypeStruct

    def tile(rows, cols):
        return pl.BlockSpec((rows // steps, cols), lambda i: (i, 0))

    def line(size):
        return sds((size,), F32), pl.BlockSpec((size,), lambda i: (0,))

    wide = [a.reshape(-1, a.shape[-1]) for a in (fu, fq, fdn, fde)]
    gu, gq, gdn, gde = ((sds(a.shape, F32), tile(*a.shape)) for a in wide)
    tokens = (sds(out.shape, BF), tile(*out.shape))
    vector = line(part)
    shapes, specs = zip(
        tokens, tokens, vector, vector, vector, vector, gq, line(fq.shape[-1] // (fu.shape[-1] // gdn[0].shape[0])),
        gde, vector, gu, line(gdn[0].shape[0]), gdn, vector,
    )
    return pl.pallas_call(
        functools.partial(finish_kernel, part),
        grid=(steps,),
        out_shape=shapes,
        in_specs=[tile(*out.shape), tile(*out.shape), pl.BlockSpec(tiny.shape, lambda i: (0, 0))]
        + [tile(*a.shape) for a in wide],
        out_specs=specs,
        compiler_params=pltpu.CompilerParams(vmem_limit_bytes=63 << 20),
        name="finish",
    )(out, dx, tiny, *wide)


def solution(mesh):
    tokens, row, vector = P("dp", "seq", None), P("seq", None), P("seq")
    in_specs = (tokens,) + (vector,) * 4 + (row, vector) * 4 + (tokens,)
    out_specs = (tokens, tokens) + (vector,) * 4 + (row, vector) * 4
    return jax.shard_map(
        functools.partial(per_device, mesh.shape["seq"], mesh.shape["dp"]),
        mesh=mesh,
        in_specs=in_specs,
        out_specs=out_specs,
        check_vma=False,
    )
```

```python
import functools
import math

import jax
import jax.numpy as jnp
import numpy as np
from jax import lax
from jax.experimental import pallas as pl
from jax.experimental.pallas import tpu as pltpu
from jax.sharding import PartitionSpec as P

HEADS = 16
HEAD_DIM = 64
ROT_DIM = 16
PLANE = 8
CHIPS = 4
epsilon = 1e-05
mask_fill = -1e30
MESH = pl.DeviceIdType.MESH
BF = jnp.bfloat16
F32 = jnp.float32


def rows_at(ref, start, count):
    return ref.at[pl.ds(pl.multiple_of(start, count), count)]


def block_at(ref, row, rows, col, cols):
    return ref.at[
        pl.ds(pl.multiple_of(row, rows), rows), pl.ds(pl.multiple_of(col, cols), cols)
    ]


class Place:
    def __init__(self, n, data):
        self.n, self.data = n, data
        self.d = lax.axis_index("dp")
        self.z = lax.axis_index("seq")
        self.base = self.d // PLANE * PLANE
        self.r = lax.rem(self.d, PLANE)
        self.ch = self.r // 2
        self.c = lax.rem(self.r, 2)
        self.piece = self.c * CHIPS + self.ch

    def seq_peer(self, k):
        other = lax.rem(self.z + k, self.n)
        return other, (self.d, other)

    def chip_peer(self, k):
        other = lax.rem(self.ch + k, CHIPS)
        return other, (self.base + other * 2 + self.c, self.z)

    def beside(self, way):
        other = self.ch + 1 - 2 * lax.rem(self.ch, 2) if way == 0 else lax.rem(self.ch + 2, CHIPS)
        return other, (self.base + other * 2 + self.c, self.z)

    def partner(self):
        return (self.base + self.ch * 2 + 1 - self.c, self.z)

    def dp_peer(self, k):
        other = lax.rem(self.d + k, self.data)
        return other, (other, self.z)

    def barrier(self):
        self.greet()
        self.met()

    def greet(self):
        sem = pltpu.get_barrier_semaphore()
        for k in range(1, self.n):
            pl.semaphore_signal(sem, inc=1, device_id=self.seq_peer(k)[1], device_id_type=MESH)
        for k in range(1, self.data):
            pl.semaphore_signal(sem, inc=1, device_id=self.dp_peer(k)[1], device_id_type=MESH)

    def met(self):
        pl.semaphore_wait(pltpu.get_barrier_semaphore(), self.n - 1 + self.data - 1)


def send(src, dst, ssem, rsem, to):
    return pltpu.make_async_remote_copy(
        src_ref=src, dst_ref=dst, send_sem=ssem, recv_sem=rsem, device_id=to, device_id_type=MESH
    )


class LineGather:
    def __init__(self, me, shard, full, rows, chunks, ssem, rsem):
        self.me, self.shard, self.full = me, shard, full
        self.rows, self.chunks, self.ssem, self.rsem = rows, chunks, ssem, rsem

    def part(self, owner, c):
        size = self.rows // self.chunks
        return rows_at(self.full, owner * self.rows + c * size, size)

    def copy(self, src, owner, c, way):
        me = self.me
        to = jnp.minimum(me.z + 1, me.n - 1) if way == 0 else jnp.maximum(me.z - 1, 0)
        return send(
            src,
            self.part(owner, c),
            self.ssem.at[way, owner, c],
            self.rsem.at[owner, c],
            (me.d, to),
        )

    def start(self):
        me = self.me
        size = self.rows // self.chunks
        for c in range(self.chunks):
            src = rows_at(self.shard, c * size, size)

            @pl.when(me.z < me.n - 1)
            def _():
                self.copy(src, me.z, c, 0).start()

            @pl.when(me.z > 0)
            def _():
                self.copy(src, me.z, c, 1).start()

    def step(self, s, c):
        me = self.me

        @pl.when(me.z >= s)
        def _():
            owner = me.z - s
            copy = self.copy(self.part(owner, c), owner, c, 0)
            copy.wait_recv()

            @pl.when(me.z < me.n - 1)
            def _():
                copy.start()

        @pl.when(me.z + s < me.n)
        def _():
            owner = me.z + s
            copy = self.copy(self.part(owner, c), owner, c, 1)
            copy.wait_recv()

            @pl.when(me.z > 0)
            def _():
                copy.start()

    def forward(self, s):
        me = self.me
        inner = (me.z > 0) & (me.z < me.n - 1)
        for c in range(self.chunks):
            for way, valid, owner in ((0, me.z >= s, me.z - s), (1, me.z + s < me.n, me.z + s)):

                @pl.when(inner & valid)
                def _():
                    copy = self.copy(self.part(owner, c), owner, c, way)
                    copy.wait_recv()
                    copy.start()

    def arrive(self, owner):
        me = self.me

        @pl.when(((me.z == 0) | (me.z == me.n - 1)) & (owner != me.z))
        def _():
            for c in range(self.chunks):
                self.copy(self.part(owner, c), owner, c, 0).wait_recv()

    def finish(self):
        me = self.me
        for c in range(self.chunks):
            for owner in range(me.n):

                @pl.when((me.z < me.n - 1) & (owner <= me.z))
                def _():
                    self.copy(self.part(owner, c), owner, c, 0).wait_send()

                @pl.when((me.z > 0) & (owner >= me.z))
                def _():
                    self.copy(self.part(owner, c), owner, c, 1).wait_send()


class ColumnGather:
    def __init__(self, me, shard, full, sems):
        self.me, self.shard, self.full = me, shard, full
        self.depth = shard.shape[0]
        self.rp = self.depth // PLANE
        self.cols = full.shape[1]
        self.zs, self.zr, self.ps, self.pr, self.fs = sems

    def part(self, src_z, piece):
        return rows_at(self.full, (src_z * PLANE + piece) * self.rp, self.rp)

    def across(self, k):
        me = self.me
        other, to = me.seq_peer(k)
        src = block_at(self.shard, me.piece * self.rp, self.rp, other * self.cols, self.cols)
        return send(src, self.part(me.z, me.piece), self.zs.at[k], self.zr.at[me.n - k], to)

    def came(self, k):
        me = self.me
        other, to = me.seq_peer(k)
        src = block_at(self.shard, me.piece * self.rp, self.rp, other * self.cols, self.cols)
        return send(src, self.part(other, me.piece), self.zs.at[k], self.zr.at[k], to)

    def shares(self, k):
        me = self.me
        other, unused = me.seq_peer(k)
        mine = self.part(other, me.piece)
        for j in range(1, CHIPS):
            to = me.chip_peer(j)[1]
            yield send(mine, mine, self.ps.at[k, j], self.pr.at[k, CHIPS - j], to)
        yield send(mine, mine, self.ps.at[k, 0], self.fs.at[1, k, 0], me.partner())

    def handed(self, k, j):
        me = self.me
        other, unused = me.seq_peer(k)
        chip = me.chip_peer(j)[0]
        return self.part(other, me.c * CHIPS + chip), self.part(other, (1 - me.c) * CHIPS + chip)

    def start(self):
        for k in range(self.me.n - 1, 0, -1):
            self.across(k).start()

    def share(self, k):
        self.came(k).wait_recv()
        for copy in self.shares(k):
            copy.start()

    def hand(self, k):
        me = self.me
        for j in range(1, CHIPS):
            got, unused = self.handed(k, j)
            send(got, got, self.ps.at[k, j], self.pr.at[k, j], me.chip_peer(j)[1]).wait_recv()
            send(got, got, self.fs.at[0, k, j], self.fs.at[1, k, j], me.partner()).start()

    def finish(self):
        me = self.me
        for k in range(1, me.n):
            self.across(k).wait_send()
            for copy in self.shares(k):
                copy.wait_send()
            other, unused = me.seq_peer(k)
            for j in range(CHIPS):
                unused, got = self.handed(k, j)
                copy = send(got, got, self.fs.at[0, k, j], self.fs.at[1, k, j], me.partner())
                copy.wait_recv()
                if j > 0:
                    copy.wait_send()


def column_sems(n):
    dma = pltpu.SemaphoreType.DMA
    return [dma((n,)), dma((n,)), dma((n, CHIPS)), dma((n, CHIPS)), dma((2, n, CHIPS))]


def gather_kernel(n, data, chunks, sm, x, g, wq, wu, SM, X, G, WQ, WU, *sems):
    me = Place(n, data)
    rows = x.shape[0]
    lsem, ss, sr, xs, xr, gs, gr = sems[:7]
    me.barrier()
    cq, cu = ColumnGather(me, wq, WQ, sems[7:12]), ColumnGather(me, wu, WU, sems[12:17])
    lx = LineGather(me, x, X, rows, chunks, xs, xr)
    lg = LineGather(me, g, G, rows, chunks, gs, gr)
    depth = wq.shape[0]
    own = [
        pltpu.make_async_copy(sm, SM.at[me.z], lsem.at[0]),
        pltpu.make_async_copy(x, rows_at(X, me.z * rows, rows), lsem.at[1]),
        pltpu.make_async_copy(g, rows_at(G, me.z * rows, rows), lsem.at[2]),
        pltpu.make_async_copy(
            block_at(wq, 0, depth, me.z * WQ.shape[1], WQ.shape[1]),
            rows_at(WQ, me.z * depth, depth),
            lsem.at[3],
        ),
        pltpu.make_async_copy(
            block_at(wu, 0, depth, me.z * WU.shape[1], WU.shape[1]),
            rows_at(WU, me.z * depth, depth),
            lsem.at[4],
        ),
    ]
    for copy in own:
        copy.start()

    def small(k, slot):
        return send(sm, SM.at[slot], ss.at[k], sr.at[slot], me.seq_peer(k)[1])

    for k in range(1, n):
        small(k, me.z).start()
    cq.start()
    cu.start()
    lx.start()
    lg.start()
    near = sorted({1, n - 1})
    for k in near:
        cq.share(k)
        cu.share(k)
    for c in range(chunks):
        lx.step(1, c)
    for k in range(1, n):
        if k not in near:
            cq.share(k)
            cu.share(k)
    for s in range(2, n):
        for c in range(chunks):
            lx.step(s, c)
    for k in range(1, n):
        cq.hand(k)
        cu.hand(k)
    for s in range(1, n):
        for c in range(chunks):
            lg.step(s, c)
    for k in range(1, n):
        small(k, me.z).wait_send()
        small(k, me.seq_peer(k)[0]).wait_recv()
    cq.finish()
    cu.finish()
    lx.finish()
    lg.finish()
    for copy in own:
        copy.wait()


def gather(n, data, sm, x, g, wq, wu):
    rows, width = x.shape
    depth = wq.shape[0]
    chunks = 4
    vm = pl.BlockSpec(memory_space=pltpu.VMEM)
    dma = pltpu.SemaphoreType.DMA
    sds = jax.ShapeDtypeStruct
    return pl.pallas_call(
        functools.partial(gather_kernel, n, data, chunks),
        out_shape=[
            sds((n,) + sm.shape, sm.dtype),
            sds((n * rows, width), x.dtype),
            sds((n * rows, width), x.dtype),
            sds((n * depth, wq.shape[1] // n), wq.dtype),
            sds((n * depth, wu.shape[1] // n), wu.dtype),
        ],
        in_specs=[vm] * 5,
        out_specs=[vm] * 5,
        scratch_shapes=[
            dma((5,)),
            dma((n,)),
            dma((n,)),
            dma((2, n, chunks)),
            dma((n, chunks)),
            dma((2, n, chunks)),
            dma((n, chunks)),
        ]
        + column_sems(n)
        + column_sems(n),
        compiler_params=pltpu.CompilerParams(
            collective_id=0, has_side_effects=True, vmem_limit_bytes=60 << 20
        ),
        name="gather",
    )(sm, x, g, wq, wu)


class RowReduce:
    def __init__(self, me, part, got, ssem, rsem):
        self.me, self.part, self.got, self.ssem, self.rsem = me, part, got, ssem, rsem
        self.rows = got.shape[1]

    def copy(self, k, slot):
        other, to = self.me.seq_peer(k)
        return send(
            rows_at(self.part, other * self.rows, self.rows),
            self.got.at[slot],
            self.ssem.at[k],
            self.rsem.at[slot],
            to,
        )

    def start(self):
        for k in range(1, self.me.n):
            self.copy(k, self.me.z).start()

    def wait(self):
        for k in range(1, self.me.n):
            self.copy(k, self.me.seq_peer(k)[0]).wait_recv()

    def finish(self):
        for k in range(1, self.me.n):
            self.copy(k, self.me.z).wait_send()


def halves(cols):
    middle = cols // 2 // 128 * 128
    return slice(0, middle), slice(middle, cols)


class GradReduce:
    def __init__(self, me, part, half, near, far, total, groups, sems):
        self.me, self.part, self.half, self.near, self.far = me, part, half, near, far
        self.total, self.groups = total, groups
        self.hs, self.hr, self.ns, self.nr, self.fs, self.fr, self.gs, self.gr = sems
        self.cols = halves(part.shape[3])

    def swap(self):
        me = self.me
        return send(
            self.part.at[:, pl.ds((1 - me.c) * CHIPS, CHIPS)],
            self.half,
            self.hs,
            self.hr,
            me.partner(),
        )

    def piece(self, way, index, other):
        me = self.me
        a, b = me.ch // 2, lax.rem(me.ch, 2)
        if way == 0:
            chip = index * 2 + (1 - b if other else b)
        else:
            chip = (1 - a if other else a) * 2 + index
        return me.c * CHIPS + chip

    def first(self, way, index):
        return send(
            self.part.at[:, self.piece(way, index, True), :, self.cols[way]],
            self.near[way].at[index],
            self.ns.at[way, index],
            self.nr.at[way, index],
            self.me.beside(way)[1],
        )

    def second(self, way):
        a, b = self.me.ch // 2, lax.rem(self.me.ch, 2)
        other = 1 - a if way == 0 else 1 - b
        return send(
            self.part.at[:, self.piece(way, other, False), :, self.cols[way]],
            self.far[way],
            self.fs.at[way],
            self.fr.at[way],
            self.me.beside(1 - way)[1],
        )

    def start(self):
        self.swap().start()

    def chip_sums(self):
        me = self.me
        self.swap().wait_recv()

        @pl.loop(0, CHIPS)
        def _(j):
            for m in range(self.half.shape[0]):
                self.part[m, me.c * CHIPS + j] = (
                    self.part[m, me.c * CHIPS + j].astype(F32) + self.half[m, j].astype(F32)
                ).astype(BF)

        for way in range(2):
            for index in range(2):
                self.first(way, index).start()

    def pair_sums(self):
        for way in range(2):
            for index in range(2):
                self.first(way, index).wait_recv()
            cols = self.cols[way]
            for index in range(2):
                piece = self.piece(way, index, False)
                for m in range(self.half.shape[0]):
                    self.part[m, piece, :, cols] = (
                        self.part[m, piece, :, cols].astype(F32)
                        + self.near[way][index, m].astype(F32)
                    ).astype(BF)
            self.second(way).start()

    def to_group(self, k, slot):
        me = self.me
        count = me.data // PLANE
        other = lax.rem(me.d // PLANE + k, count)
        return send(
            self.total,
            self.groups.at[slot],
            self.gs.at[k],
            self.gr.at[slot],
            (other * PLANE + me.r, me.z),
        )

    def sum_up(self):
        me = self.me
        for way in range(2):
            self.second(way).wait_recv()
            cols = self.cols[way]
            for m in range(self.total.shape[0]):
                self.total[m, :, cols] = (
                    self.part[m, me.piece, :, cols].astype(F32) + self.far[way][m].astype(F32)
                ).astype(BF)
        count = me.data // PLANE
        if count > 1:
            own = me.d // PLANE
            for k in range(1, count):
                self.to_group(k, own).start()
            for k in range(1, count):
                self.to_group(k, lax.rem(own + k, count)).wait_recv()
                self.to_group(k, own).wait_send()
            self.groups[own] = self.total[...]
            total = self.groups[0].astype(F32)
            for e in range(1, count):
                total = total + self.groups[e].astype(F32)
            self.total[...] = total.astype(BF)

    def finish(self):
        self.swap().wait_send()
        for way in range(2):
            for index in range(2):
                self.first(way, index).wait_send()
            self.second(way).wait_send()


def reduce_scratch(m, rp, cols, groups):
    mem, dma = pltpu.VMEM, pltpu.SemaphoreType.DMA
    widths = [part.stop - part.start for part in halves(cols)]
    return (
        [mem((m, CHIPS, rp, cols), BF)]
        + [mem((2, m, rp, width), BF) for width in widths]
        + [mem((m, rp, width), BF) for width in widths]
        + [
            mem((m, rp, cols), BF),
            mem((groups, m, rp, cols) if groups > 1 else (1, 1, 16, 128), BF),
            dma,
            dma,
            dma((2, 2)),
            dma((2, 2)),
            dma((2,)),
            dma((2,)),
            dma((groups,)),
            dma((groups,)),
        ]
    )


def take_reduce(me, part, take):
    half, near0, near1, far0, far1, total, groups = take(7)
    return GradReduce(me, part, half, (near0, near1), (far0, far1), total, groups, take(8))


class GradShare:
    def __init__(self, me, final, sems):
        self.me, self.final = me, final
        self.ss, self.sr, self.fs, self.fr, self.hs, self.hr = sems
        self.cols = halves(final.shape[2])

    def own(self, way, source=None):
        mine = self.final.at[self.me.piece]
        return send(
            mine if source is None else source,
            mine,
            self.ss.at[way],
            self.sr.at[way],
            self.me.beside(way)[1],
        )

    def to_partner(self, index, chip, core, source=None):
        got = self.final.at[core * CHIPS + chip]
        return send(
            got if source is None else source,
            got,
            self.hs.at[index],
            self.hr.at[index],
            self.me.partner(),
        )

    def onward(self, way, chip):
        got = self.final.at[self.me.c * CHIPS + chip, :, self.cols[way]]
        return send(got, got, self.fs.at[way], self.fr.at[way], self.me.beside(1 - way)[1])

    def across(self):
        return CHIPS - 1 - self.me.ch

    def start(self, source=None):
        for way in range(2):
            self.own(way, source).start()
        self.to_partner(0, self.me.ch, self.me.c, source).start()

    def forward(self):
        me = self.me
        for way in range(2):
            chip = me.beside(way)[0]
            got = self.final.at[me.c * CHIPS + chip]
            send(got, got, self.ss.at[way], self.sr.at[way], me.beside(way)[1]).wait_recv()
            self.onward(way, chip).start()
            self.to_partner(1 + way, chip, me.c).start()

    def hand(self):
        for way in range(2):
            self.onward(way, self.across()).wait_recv()
        self.to_partner(3, self.across(), self.me.c).start()

    def finish(self):
        me = self.me
        chips = [me.ch, me.beside(0)[0], me.beside(1)[0], self.across()]
        for way in range(2):
            self.own(way).wait_send()
            self.onward(way, chips[1 + way]).wait_send()
        for index, chip in enumerate(chips):
            self.to_partner(index, chip, me.c).wait_send()
            self.to_partner(index, chip, 1 - me.c).wait_recv()


def share_sems():
    dma = pltpu.SemaphoreType.DMA
    return [dma((2,))] * 4 + [dma((4,))] * 2


class RowsBack:
    def __init__(self, me, total, final, ssem, rsem, lsem):
        self.me, self.total, self.final = me, total, final
        self.ssem, self.rsem, self.lsem = ssem, rsem, lsem

    def place(self, src_z):
        cols = self.total.shape[2]
        return self.final.at[
            self.me.piece, :, pl.ds(pl.multiple_of(src_z * cols, cols), cols)
        ]

    def copy(self, k, slot):
        other, to = self.me.seq_peer(k)
        return send(
            self.total.at[other], self.place(slot), self.ssem.at[k], self.rsem.at[slot], to
        )

    def own(self):
        me = self.me
        return pltpu.make_async_copy(self.total.at[me.z], self.place(me.z), self.lsem)

    def start(self):
        for k in range(1, self.me.n):
            self.copy(k, self.me.z).start()
        self.own().start()

    def wait(self):
        me = self.me
        for k in range(1, me.n):
            self.copy(k, me.seq_peer(k)[0]).wait_recv()
        self.own().wait()

    def finish(self):
        for k in range(1, self.me.n):
            self.copy(k, self.me.z).wait_send()


def reduce_kernel(n, data, *refs):
    (OP, DX, v1, v2, bias, x, g, UG, QG, DnG, DeG) = refs[:11]
    out, dx, small, fu, fq, fdn, fde = refs[11:18]
    scratch = list(refs[18:])
    me = Place(n, data)

    def take(count):
        got = scratch[:count]
        del scratch[:count]
        return got

    og, xg, zs, zr, v1g, v1s, v1r, v2m, v2g, v2s, v2r = take(11)
    reduces = []
    for part in (DnG, DeG, UG, QG):
        reduces.append(take_reduce(me, part, take))
    red_dn, red_de, red_u, red_q = reduces
    shares = [GradShare(me, final, take(6)) for final in (fdn, fde, fu, fq)]
    back_u = RowsBack(me, red_u.total, fu, *take(3))
    back_q = RowsBack(me, red_q.total, fq, *take(3))
    (dsem,) = take(1)
    assert not scratch
    ro = RowReduce(me, OP, og, zs.at[0], zr.at[0])
    rx = RowReduce(me, DX, xg, zs.at[1], zr.at[1])
    me.barrier()
    cs = v1g.shape[2]

    def small_z(k, slot):
        other, to = me.seq_peer(k)
        return send(
            v1.at[:, pl.ds(pl.multiple_of(other * cs, cs), cs)],
            v1g.at[slot],
            v1s.at[k],
            v1r.at[slot],
            to,
        )

    def small_dp(k, slot):
        return send(v2m, v2g.at[slot], v2s.at[k], v2r.at[slot], me.dp_peer(k)[1])

    for k in range(1, n):
        small_z(k, me.z).start()
    for red in reduces:
        red.start()
    ro.start()
    rx.start()
    for red in reduces:
        red.chip_sums()
    for red in reduces:
        red.pair_sums()
    for k in range(1, n):
        small_z(k, me.seq_peer(k)[0]).wait_recv()
    v1g[me.z] = v1[:, pl.ds(pl.multiple_of(me.z * cs, cs), cs)]
    total = v1g[0]
    for k in range(1, n):
        total = total + v1g[k]
    v2m[0:8] = total
    v2m[8:16] = v2[...]
    for k in range(1, data):
        small_dp(k, me.d).start()
    own = []
    for i, (red, final) in enumerate(((red_dn, fdn), (red_de, fde))):
        red.sum_up()
        copy = pltpu.make_async_copy(red.total.at[0], final.at[me.piece], dsem.at[i])
        copy.start()
        own.append(copy)
    red_u.sum_up()
    back_u.start()
    red_q.sum_up()
    back_q.start()
    for copy in own:
        copy.wait()
    shares[0].start()
    shares[1].start()
    back_u.wait()
    shares[2].start()
    back_q.wait()
    shares[3].start()
    for share in shares:
        share.forward()
    for share in shares:
        share.hand()
    for k in range(1, data):
        small_dp(k, me.dp_peer(k)[0]).wait_recv()
    v2g[me.d] = v2m[...]

    def add(i, acc):
        return acc + v2g[i]

    small[...] = lax.fori_loop(1, data, add, v2g[0])
    rows = x.shape[0]
    for red, base, result, extra in ((ro, x, out, bias), (rx, g, dx, None)):
        red.wait()
        step = rows // 4

        @pl.loop(0, 4)
        def _(i):
            at = pl.ds(pl.multiple_of(i * step, step), step)
            mine = pl.ds(pl.multiple_of(me.z * rows + i * step, step), step)
            acc = base[at].astype(F32) + red.part[mine].astype(F32)
            for k in range(1, n):
                acc = acc + red.got[me.seq_peer(k)[0], at].astype(F32)
            if extra is not None:
                acc = acc + extra[...]
            result[at] = acc.astype(BF)

        red.finish()
    for k in range(1, n):
        small_z(k, me.z).wait_send()
    for k in range(1, data):
        small_dp(k, me.d).wait_send()
    for red in reduces:
        red.finish()
    for share in shares:
        share.finish()
    back_u.finish()
    back_q.finish()


def reduce_all(n, data, OP, DX, v1, v2, bias, x, g, UG, QG, DnG, DeG):
    vm = pl.BlockSpec(memory_space=pltpu.VMEM)
    dma = pltpu.SemaphoreType.DMA
    sds = jax.ShapeDtypeStruct
    rows, width = x.shape
    groups = data // PLANE
    parts = []
    for whole in (DnG, DeG):
        lead, cols = whole.shape
        parts.append(whole.reshape(1, PLANE, lead // PLANE, cols))
    for whole in (UG, QG):
        lead, cols = whole.shape
        parts.append(whole.reshape(n, PLANE, lead // n // PLANE, cols))
    dn, de, u, q = parts
    scratch = [
        pltpu.VMEM((n, rows, width), BF),
        pltpu.VMEM((n, rows, width), BF),
        dma((2, n)),
        dma((2, n)),
        pltpu.VMEM((n, 8, width // n), F32),
        dma((n,)),
        dma((n,)),
        pltpu.VMEM((16, width // n), F32),
        pltpu.VMEM((data, 16, width // n), F32),
        dma((data,)),
        dma((data,)),
    ]
    for part in (dn, de, u, q):
        m, unused, rp, cols = part.shape
        scratch += reduce_scratch(m, rp, cols, groups)
    for unused in range(4):
        scratch += share_sems()
    scratch += [dma((n,)), dma((n,)), dma] * 2
    scratch += [dma((2,))]
    outs = [
        sds((rows, width), BF),
        sds((rows, width), BF),
        sds((16, width // n), F32),
        sds((PLANE, u.shape[2], u.shape[3] * n), BF),
        sds((PLANE, q.shape[2], q.shape[3] * n), BF),
        sds((PLANE,) + dn.shape[2:], BF),
        sds((PLANE,) + de.shape[2:], BF),
    ]
    return pl.pallas_call(
        functools.partial(reduce_kernel, n, data),
        out_shape=outs,
        in_specs=[vm] * 11,
        out_specs=[vm] * 7,
        scratch_shapes=scratch,
        compiler_params=pltpu.CompilerParams(
            collective_id=1, has_side_effects=True, vmem_limit_bytes=63 << 20
        ),
        name="reduce",
    )(OP, DX, v1, v2, bias, x, g, u, q, dn, de)


def layer_norm_parts(token_rows):
    average = jnp.mean(token_rows, axis=-1, keepdims=True)
    centered = token_rows - average
    variance = jnp.mean(centered * centered, axis=-1, keepdims=True)
    inverse = lax.rsqrt(variance + epsilon)
    return centered * inverse, inverse


def rotate(packed, positions, sign):
    half = ROT_DIM // 2
    freqs = 10000.0 ** (-jnp.arange(half, dtype=F32) * 2.0 / ROT_DIM)
    angles = positions.astype(F32)[:, None] * freqs[None, :]
    cosine = jnp.cos(angles)[:, None, None, :]
    sine = jnp.sin(angles)[:, None, None, :] * sign
    first = packed[..., :half]
    second = packed[..., half:ROT_DIM]
    turned = jnp.concatenate(
        [first * cosine - second * sine, second * cosine + first * sine, packed[..., ROT_DIM:]],
        axis=-1,
    )
    select = (jnp.arange(3) < 2)[:, None]
    return jnp.where(select, turned, packed)


def middle(X, G, WQ, WU, w_dense, w_down, b_qkv, b_up, vectors):
    length, width = X.shape
    heads = WQ.shape[1] // (3 * HEAD_DIM)
    scale = HEAD_DIM ** (-0.5)
    gain_one, shift_one, gain_two, shift_two = (vectors[i] for i in range(4))
    xhat, inverse = layer_norm_parts(X.astype(F32))
    norm_one = (xhat * gain_one + shift_one).astype(BF)
    norm_two = (xhat * gain_two + shift_two).astype(BF)
    packed = jnp.dot(norm_one, WQ, preferred_element_type=F32) + b_qkv.astype(F32)
    positions = jnp.arange(length, dtype=jnp.int32)
    packed = rotate(packed.reshape(length, heads, 3, HEAD_DIM), positions, 1.0).astype(BF)
    query, keys, values = packed[:, :, 0], packed[:, :, 1], packed[:, :, 2]
    scores = jnp.einsum("qhd,khd->hqk", query, keys, preferred_element_type=F32) * scale
    allowed = positions[:, None] >= positions[None, :]
    probs = jax.nn.softmax(jnp.where(allowed, scores, mask_fill), axis=-1)
    low = probs.astype(BF)
    context = jnp.einsum("hqk,khd->qhd", low, values, preferred_element_type=F32)
    context = context.astype(BF).reshape(length, heads * HEAD_DIM)
    hidden = jnp.dot(norm_two, WU, preferred_element_type=F32) + b_up.astype(F32)
    active = jax.nn.gelu(hidden, approximate=False).astype(BF)
    out = jnp.dot(context, w_dense, preferred_element_type=F32) + jnp.dot(
        active, w_down, preferred_element_type=F32
    )
    down_grad = jnp.einsum("tf,to->fo", active, G, preferred_element_type=F32)
    dense_grad = jnp.einsum("ti,to->io", context, G, preferred_element_type=F32)
    active_grad = jnp.einsum("to,fo->tf", G, w_down, preferred_element_type=F32)
    unused, pull = jax.vjp(lambda v: jax.nn.gelu(v, approximate=False), hidden)
    hidden_grad = pull(active_grad)[0].astype(BF)
    up_bias_grad = jnp.sum(hidden_grad.astype(F32), axis=0)
    up_grad = jnp.einsum("ti,tf->if", norm_two, hidden_grad, preferred_element_type=F32)
    norm_two_grad = jnp.einsum("tf,if->ti", hidden_grad, WU, preferred_element_type=F32)
    context_grad = jnp.einsum("to,io->ti", G, w_dense, preferred_element_type=F32).astype(BF)
    context_grad = context_grad.reshape(length, heads, HEAD_DIM)
    prob_grad = jnp.einsum("qhd,khd->hqk", context_grad, values, preferred_element_type=F32)
    weighted = jnp.sum(probs * prob_grad, axis=-1, keepdims=True)
    score_grad = (probs * (prob_grad - weighted)).astype(BF)
    query_grad = jnp.einsum("hqk,khd->qhd", score_grad, keys, preferred_element_type=F32) * scale
    key_grad = jnp.einsum("hqk,qhd->khd", score_grad, query, preferred_element_type=F32) * scale
    value_grad = jnp.einsum("hqk,qhd->khd", low, context_grad, preferred_element_type=F32)
    rotated_grad = jnp.stack([query_grad, key_grad, value_grad], axis=2).astype(BF).astype(F32)
    packed_grad = rotate(rotated_grad, positions, -1.0).reshape(length, -1).astype(BF)
    qkv_bias_grad = jnp.sum(packed_grad.astype(F32), axis=0)
    qkv_grad = jnp.einsum("ti,tj->ij", norm_one, packed_grad, preferred_element_type=F32)
    norm_one_grad = jnp.einsum("tj,ij->ti", packed_grad, WQ, preferred_element_type=F32)
    u = norm_one_grad * gain_one + norm_two_grad * gain_two
    mean_u = jnp.mean(u, axis=-1, keepdims=True)
    mean_ux = jnp.mean(u * xhat, axis=-1, keepdims=True)
    dx = inverse * (u - mean_u - xhat * mean_ux)
    sums = jnp.stack(
        [
            jnp.sum(norm_one_grad * xhat, axis=0),
            jnp.sum(norm_one_grad, axis=0),
            jnp.sum(norm_two_grad * xhat, axis=0),
            jnp.sum(norm_two_grad, axis=0),
        ]
    )
    return (
        out.astype(BF),
        dx.astype(BF),
        sums,
        up_bias_grad,
        qkv_bias_grad,
        up_grad.astype(BF),
        qkv_grad.astype(BF),
        down_grad.astype(BF),
        dense_grad.astype(BF),
    )


NN = (((1,), (0,)), ((), ()))
NT = (((1,), (1,)), ((), ()))
TN = (((0,), (0,)), ((), ()))
ROOT_HALF = 0.7071067811865476
PDF_SCALE = 0.3989422804014327


def dot(left, right, dims=NN):
    return lax.dot_general(left, right, dims, preferred_element_type=F32)


def rotary_tables(length):
    half = ROT_DIM // 2
    freqs = 10000.0 ** (-jnp.arange(half, dtype=F32) * 2.0 / ROT_DIM)
    angles = jnp.arange(length, dtype=jnp.int32).astype(F32)[:, None] * freqs[None, :]
    cosine, sine = jnp.cos(angles), jnp.sin(angles)
    rest = HEAD_DIM - ROT_DIM
    keep, none, gap = jnp.ones((length, rest)), jnp.zeros((length, rest)), jnp.zeros_like(sine)
    same = jnp.concatenate([cosine, cosine, keep] * 2, axis=1)
    up = jnp.concatenate([-sine, gap, none] * 2, axis=1)
    down = jnp.concatenate([gap, sine, none] * 2, axis=1)
    return jnp.stack([same, up, down]).astype(F32)


class Layer:
    def __init__(self, rows, refs):
        self.rows = rows
        for name, ref in refs.items():
            setattr(self, name, ref)
        self.length, self.width = self.X.shape
        self.heads = self.Q.shape[0]
        self.block = min(256, self.length)

    def at(self, j, rows=None, part=0):
        rows = rows or self.rows
        return pl.ds(pl.multiple_of(j * self.rows + part * rows, rows), rows)

    def norm(self, j):
        step = 64

        @pl.loop(0, self.rows // step)
        def _(i):
            at = self.at(j, step, i)
            x = self.X[at].astype(F32)
            average = jnp.mean(x, axis=-1, keepdims=True)
            centered = x - average
            variance = jnp.mean(centered * centered, axis=-1, keepdims=True)
            inverse = lax.rsqrt(variance + epsilon)
            xhat = centered * inverse
            self.STAT[at, 0:1] = average
            self.STAT[at, 1:2] = inverse
            self.N1[at] = (xhat * self.VEC[0:1] + self.VEC[1:2]).astype(BF)
            self.N2[at] = (xhat * self.VEC[2:3] + self.VEC[3:4]).astype(BF)

    def turn(self, values, at, kind, sign):
        lanes = lax.broadcasted_iota(jnp.int32, values.shape, 1)
        turned = values * self.ROT[0, at] + sign * (
            pltpu.roll(values, 128 - ROT_DIM // 2, 1) * self.ROT[1, at]
            + pltpu.roll(values, ROT_DIM // 2, 1) * self.ROT[2, at]
        )
        if kind == 0:
            return turned
        return jnp.where((lanes >= HEAD_DIM) if kind == 1 else (lanes < HEAD_DIM), turned, values)

    def qkv(self, j):
        at = self.at(j)
        scale = HEAD_DIM ** (-0.5)
        packed = dot(self.N1[at], self.WQ[...])
        bias = self.BQ[...]
        places = [(self.Q, scale, None), (self.K, None, self.KT), (self.V, None, self.VT)]
        for t in range(packed.shape[1] // 128):
            cols = slice(t * 128, t * 128 + 128)
            low = self.turn(packed[:, cols] + bias[:, cols], at, t % 3, 1.0).astype(BF)
            across = low.T
            for side in range(2):
                index = 2 * t + side
                ref, factor, turned = places[index % 3]
                half = slice(side * HEAD_DIM, side * HEAD_DIM + HEAD_DIM)
                value = low[:, half]
                ref[index // 3, at] = value if factor is None else value * jnp.asarray(factor, BF)
                if turned is not None:
                    turned[index // 3, :, at] = across[half]

    def up(self, j):
        at = self.at(j)
        tile = 256

        for i in range(self.WU.shape[1] // tile):
            cols = slice(i * tile, i * tile + tile)
            hidden = dot(self.N2[at], self.WU[:, cols]) + self.BU[:, cols]
            cdf = 0.5 + 0.5 * lax.erf(hidden * ROOT_HALF)
            self.ACT[at, cols] = (hidden * cdf).astype(BF)
            pdf = PDF_SCALE * jnp.exp(-0.5 * hidden * hidden)
            self.DG[at, cols] = cdf + hidden * pdf

    def down(self, j):
        at = self.at(j)
        self.ACC[at] = dot(self.ACT[at], self.WDN[...])

    def masked(self, scores):
        rows = lax.broadcasted_iota(jnp.int32, scores.shape, 0)
        cols = lax.broadcasted_iota(jnp.int32, scores.shape, 1)
        return jnp.where(rows <= cols, scores, mask_fill)

    def attend_block(self, m, qb):
        size = self.block
        mine, before = slice(qb * size, qb * size + size), slice(0, qb * size)
        sides = []
        for side in range(2):
            h = 2 * m + side
            q = self.Q[h, mine]
            near = self.masked(dot(self.K[h, mine], q, NT))
            top = jnp.max(near, axis=0, keepdims=True)
            if qb:
                far = dot(self.K[h, before], q, NT)
                top = jnp.maximum(top, jnp.max(far, axis=0, keepdims=True))
            near = jnp.exp(near - top)
            total = jnp.sum(near, axis=0, keepdims=True)
            if qb:
                far = jnp.exp(far - top)
                total = total + jnp.sum(far, axis=0, keepdims=True)
            inverse = 1.0 / total
            self.LSE[h, :, mine] = top + jnp.log(total)
            context = dot(self.VT[h, :, mine], (near * inverse).astype(BF))
            if qb:
                context = context + dot(self.VT[h, :, before], (far * inverse).astype(BF))
            sides.append(context.astype(BF))
        self.CTX[m, mine] = jnp.concatenate(sides, axis=0).T

    def attend_part(self, qb):
        @pl.loop(0, self.heads // 2)
        def _(m):
            self.attend_block(m, qb)

    def out(self, j):
        at = self.at(j)
        total = self.ACC[at]
        for m in range(self.heads // 2):
            total = total + dot(self.CTX[m, at], self.WDE[m * 128 : m * 128 + 128])
        self.OP[at] = total.astype(BF)

    def mlp_back(self, j):
        at = self.at(j)
        tile = 256

        for i in range(self.WU.shape[1] // tile):
            cols = slice(i * tile, i * tile + tile)
            active_grad = dot(self.G[at], self.WDN[cols], NT)
            self.HG[at, cols] = (active_grad * self.DG[at, cols]).astype(BF)

        self.ACC[at] = dot(self.HG[at], self.WU[...], NT)

    def context_grad(self, j):
        at = self.at(j)
        for m in range(self.heads // 2):
            self.DO[m, at] = dot(self.G[at], self.WDE[m * 128 : m * 128 + 128], NT).astype(BF)

    def back_block(self, m, qb):
        size = self.block
        mine, before = slice(qb * size, qb * size + size), slice(0, qb * size)
        scale = HEAD_DIM ** (-0.5)
        upstream = self.DO[m, mine]
        values, keys, queries, values_before, keys_before = [], [], [], [], []
        for side in range(2):
            h = 2 * m + side
            q = self.Q[h, mine]
            do = upstream[:, side * HEAD_DIM : side * HEAD_DIM + HEAD_DIM]
            lse = self.LSE[h, :, mine]
            near = jnp.exp(self.masked(dot(self.K[h, mine], q, NT)) - lse)
            near_grad = dot(self.V[h, mine], do, NT)
            weighted = jnp.sum(near * near_grad, axis=0, keepdims=True)
            if qb:
                far = jnp.exp(dot(self.K[h, before], q, NT) - lse)
                far_grad = dot(self.V[h, before], do, NT)
                weighted = weighted + jnp.sum(far * far_grad, axis=0, keepdims=True)
            values.append(dot(near.astype(BF), do))
            score = (near * (near_grad - weighted)).astype(BF)
            keys.append(dot(score, q))
            query = dot(self.KT[h, :, mine], score)
            if qb:
                values_before.append(dot(far.astype(BF), do))
                score = (far * (far_grad - weighted)).astype(BF)
                keys_before.append(dot(score, q))
                query = query + dot(self.KT[h, :, before], score)
            queries.append((query * scale).astype(BF))
        self.DV[m, mine] += jnp.concatenate(values, axis=1)
        self.DK[m, mine] += jnp.concatenate(keys, axis=1)
        self.DQ[m, mine] = jnp.concatenate(queries, axis=0).T
        if qb:
            self.DV[m, before] += jnp.concatenate(values_before, axis=1)
            self.DK[m, before] += jnp.concatenate(keys_before, axis=1)

    def attend_back(self, j, m):
        for qb in range(self.length // self.block):

            @pl.when(j == qb)
            def _():
                self.back_block(m, qb)

    def unturn(self, j):
        at = self.at(j)
        for m in range(self.heads // 2):
            q = self.DQ[m, at].astype(F32)
            k = pltpu.roll(self.DK[m, at], HEAD_DIM, 1).astype(BF).astype(F32)
            v = self.DV[m, at].astype(BF).astype(F32)
            left = lax.broadcasted_iota(jnp.int32, q.shape, 1) < HEAD_DIM
            for kind, pair in enumerate(((q, k), (v, q), (k, v))):
                both = jnp.where(left, *pair)
                cols = slice((3 * m + kind) * 128, (3 * m + kind) * 128 + 128)
                self.PG[at, cols] = self.turn(both, at, kind, -1.0).astype(BF)

    def zero_sums(self):
        self.SUMS[...] = jnp.zeros_like(self.SUMS)
        self.COLS[...] = jnp.zeros_like(self.COLS)
        self.DK[...] = jnp.zeros_like(self.DK)
        self.DV[...] = jnp.zeros_like(self.DV)
        self.BUG[...] = jnp.zeros_like(self.BUG)
        self.BQG[...] = jnp.zeros_like(self.BQG)

    def input_back(self, j):
        self.TMP[...] = dot(self.PG[self.at(j)], self.WQ[...], NT)
        ones = jnp.ones((8, self.rows), BF)
        self.BQG[...] += dot(ones, self.PG[self.at(j)])[0:1]
        self.BUG[...] += dot(ones, self.HG[self.at(j)])[0:1]
        step = 32

        @pl.loop(0, self.rows // step)
        def _(i):
            at = self.at(j, step, i)
            here = pl.ds(pl.multiple_of(i * step, step), step)
            inverse = self.STAT[at, 1:2]
            xhat = (self.X[at].astype(F32) - self.STAT[at, 0:1]) * inverse
            one, two = self.TMP[here], self.ACC[at]
            u = one * self.VEC[0:1] + two * self.VEC[2:3]
            mean_u = jnp.mean(u, axis=-1, keepdims=True)
            mean_ux = jnp.mean(u * xhat, axis=-1, keepdims=True)
            self.DX[at] = (inverse * (u - mean_u - xhat * mean_ux)).astype(BF)
            for row, value in enumerate((one * xhat, one, two * xhat, two)):
                folded = value[0:8]
                for r in range(8, step, 8):
                    folded = folded + value[r : r + 8]
                self.COLS[row] += folded

    def fold_sums(self):
        for row in range(4):
            self.SUMS[row : row + 1] = jnp.sum(self.COLS[row], axis=0, keepdims=True)

    def weight_grad(self, left, right, put, at):
        tile = 256

        @pl.loop(0, left.shape[1] // tile)
        def _(i):
            cols = pl.ds(pl.multiple_of(i * tile, tile), tile)
            put(i, dot(left[at, cols], right[at], TN))

    def down_grad(self, put, at, core, half_done):
        tile = 256
        count = self.ACT.shape[1] // tile

        @pl.loop(0, count)
        def _(k):
            i = lax.rem(k + (1 - core) * (count // 2), count)
            cols = pl.ds(pl.multiple_of(i * tile, tile), tile)
            put(i, dot(self.ACT[at, cols], self.G[at], TN))

            @pl.when(k == count // 2 - 1)
            def _():
                half_done()

    def up_grad(self, put, at):
        self.weight_grad(self.N2, self.HG, put, at)

    def qkv_grad(self, put):
        self.weight_grad(self.N1, self.PG, put, slice(0, self.length))

    def dense_grad(self, put, at):
        for m in range(self.heads // 2):
            put(m, dot(self.CTX[m, at], self.G[at], TN))


def layer_scratch(length, width, heads, hidden):
    vm = pltpu.VMEM
    pairs, packed = heads // 2, heads * 3 * HEAD_DIM
    return dict(
        STAT=vm((length, 2), F32),
        N1=vm((length, width), BF),
        N2=vm((length, width), BF),
        Q=vm((heads, length, HEAD_DIM), BF),
        K=vm((heads, length, HEAD_DIM), BF),
        V=vm((heads, length, HEAD_DIM), BF),
        ACT=vm((length, hidden), BF),
        DG=vm((length, hidden), F32),
        ACC=vm((length, width), F32),
        LSE=vm((heads, 1, length), F32),
        KT=vm((heads, HEAD_DIM, length), BF),
        VT=vm((heads, HEAD_DIM, length), BF),
        CTX=vm((pairs, length, 2 * HEAD_DIM), BF),
        DO=vm((pairs, length, 2 * HEAD_DIM), BF),
        HG=vm((length, hidden), BF),
        DQ=vm((pairs, length, 2 * HEAD_DIM), BF),
        DK=vm((pairs, length, 2 * HEAD_DIM), F32),
        DV=vm((pairs, length, 2 * HEAD_DIM), F32),
        PG=vm((length, packed), BF),
    )


class LineReduce:
    def __init__(self, me, part, got, ssem, rsem):
        self.me, self.part, self.got, self.ssem, self.rsem = me, part, got, ssem, rsem
        self.parts, self.rows = got.shape[1:3]

    def copy(self, j, p, way):
        me = self.me
        to = jnp.minimum(me.z + 1, me.n - 1) if way == 0 else jnp.maximum(me.z - 1, 0)
        slot = j if way == 0 else jnp.where(j == to, me.n, j)
        return send(
            rows_at(self.part, (j * self.parts + p) * self.rows, self.rows),
            self.got.at[slot, p],
            self.ssem.at[j, p],
            self.rsem.at[slot, p],
            (me.d, to),
        )

    def came(self, slot, p):
        me = self.me
        got = self.got.at[slot, p]
        return send(got, got, self.ssem.at[0, p], self.rsem.at[slot, p], (me.d, me.z))

    def start(self, j, which=None):
        me = self.me
        for p in range(self.parts) if which is None else which:

            @pl.when((me.z == 0) & (j > 0))
            def _():
                self.copy(j, p, 0).start()

            @pl.when((me.z == me.n - 1) & (j < me.n - 1))
            def _():
                self.copy(j, p, 1).start()

    def add(self, j, p):
        step = 64

        @pl.loop(0, self.rows // step)
        def _(i):
            mine = pl.ds(pl.multiple_of((j * self.parts + p) * self.rows + i * step, step), step)
            here = pl.ds(pl.multiple_of(i * step, step), step)
            self.part[mine] = (
                self.part[mine].astype(F32) + self.got[j, p, here].astype(F32)
            ).astype(BF)

    def step(self, t, which=None):
        me = self.me
        n = me.n
        for p in range(self.parts) if which is None else which:
            for way, e in ((0, t - me.z), (1, t - (n - 1 - me.z))):
                j = n - 1 - e if way == 0 else e
                valid = (me.z > 0) & (me.z < n - 1) & (e >= 0)
                valid = valid & ((j > me.z) if way == 0 else (j < me.z))

                @pl.when(valid)
                def _():
                    self.came(j, p).wait_recv()
                    self.add(j, p)
                    self.copy(j, p, way).start()

    def total(self, base, extra, result, tmp):
        me = self.me
        step = 64
        for p in range(self.parts):

            @pl.when(me.z > 0)
            def _():
                self.came(me.z, p).wait_recv()

            @pl.when(me.z < me.n - 1)
            def _():
                self.came(me.n, p).wait_recv()

            @pl.loop(0, self.rows // step)
            def _(i):
                at = p * self.rows + i * step
                here = pl.ds(pl.multiple_of(i * step, step), step)
                there = pl.ds(pl.multiple_of(at, step), step)
                mine = pl.ds(pl.multiple_of(me.z * self.parts * self.rows + at, step), step)
                tmp[here] = base[mine].astype(F32) + self.part[mine].astype(F32)
                if extra is not None:
                    tmp[here] += extra

                @pl.when(me.z > 0)
                def _():
                    tmp[here] += self.got[me.z, p, here].astype(F32)

                @pl.when(me.z < me.n - 1)
                def _():
                    tmp[here] += self.got[me.n, p, here].astype(F32)

                result[there] = tmp[here].astype(BF)

    def finish(self):
        me = self.me
        for j in range(me.n):
            for p in range(self.parts):

                @pl.when((j > me.z) & (me.z < me.n - 1))
                def _():
                    self.copy(j, p, 0).wait_send()

                @pl.when((j < me.z) & (me.z > 0))
                def _():
                    self.copy(j, p, 1).wait_send()


def nearest(n):
    return [sorted(range(n), key=lambda j: abs(j - z)) for z in range(n)]


def pick(table, z, k):
    value = jnp.int32(0)
    for at, row in enumerate(table):
        for index, entry in enumerate(row):
            if entry:
                value = jnp.where((z == at) & (k == index), entry, value)
    return value


VECTORS = 6


def layer_kernel(n, data, chunks, names, *refs):
    refs = list(refs)

    def take(count):
        got = refs[:count]
        del refs[:count]
        return got

    vectors = take(VECTORS)
    x, g, wq, wu, wde, wdn, rot, bq, bu = take(9)
    out, dx, small, fu, fq, fdn, fde = take(7)
    ins = dict(zip(names, take(len(names))))
    rows = out.shape[0]
    layer = Layer(rows, ins)
    me = Place(n, data)
    SM, sm = take(2)
    layer.DX = layer.ACT
    lsem, ss, sr, xs, xr, gs, gr = take(7)
    cq, cu = ColumnGather(me, wq, layer.WQ, take(5)), ColumnGather(me, wu, layer.WU, take(5))
    og, xg, os, orr, ds, dr = take(6)
    v1, v1g, v1s, v1r, v2m, v2g, v2s, v2r = take(8)
    reduces = []
    for unused in range(4):
        reduces.append(take_reduce(me, take(1)[0], take))
    red_dn, red_de, red_u, red_q = reduces
    shares = [GradShare(me, final, take(6)) for final in (fdn, fde, fu, fq)]
    share_dn, share_de, share_u, share_q = shares
    back_u = RowsBack(me, red_u.total, fu, *take(3))
    back_q = RowsBack(me, red_q.total, fq, *take(3))
    (dsem,) = take(1)
    assert not refs
    lx = LineGather(me, x, layer.X, rows, chunks, xs, xr)
    lg = LineGather(me, g, layer.G, rows, chunks, gs, gr)
    ro = LineReduce(me, layer.OP, og, os, orr)
    rx = LineReduce(me, layer.ACT, xg, ds, dr)
    near = nearest(n)
    far = [list(range(n - 1, -1, -1)) if 2 * z < n else list(range(n)) for z in range(n)]
    depth = wq.shape[0]
    part = depth

    own = [
        pltpu.make_async_copy(x, rows_at(layer.X, me.z * rows, rows), lsem.at[0]),
        pltpu.make_async_copy(g, rows_at(layer.G, me.z * rows, rows), lsem.at[1]),
        pltpu.make_async_copy(
            block_at(wq, 0, depth, me.z * layer.WQ.shape[1], layer.WQ.shape[1]),
            rows_at(layer.WQ, me.z * depth, depth),
            lsem.at[2],
        ),
        pltpu.make_async_copy(
            block_at(wu, 0, depth, me.z * layer.WU.shape[1], layer.WU.shape[1]),
            rows_at(layer.WU, me.z * depth, depth),
            lsem.at[3],
        ),
    ]
    own += [
        pltpu.make_async_copy(source, place, lsem.at[4 + i])
        for i, (source, place) in enumerate(
            ((wde, layer.WDE), (wdn, layer.WDN), (rot, layer.ROT))
        )
    ]
    me.greet()
    for copy in own:
        copy.start()
    sm[...] = jnp.zeros_like(sm)
    for i, vector in enumerate(vectors):
        sm[i] = vector[...].astype(F32)
    layer.BQ[0] = bq[...].astype(F32)
    layer.BU[0] = bu[...].astype(F32)
    me.met()

    def tiny(k, slot):
        return send(sm, SM.at[slot], ss.at[k], sr.at[slot], me.seq_peer(k)[1])

    for k in range(1, n):
        tiny(k, me.z).start()
    cq.start()
    cu.start()
    lx.start()
    SM[me.z] = sm[...]
    layer.zero_sums()
    for k in range(1, n):
        tiny(k, me.seq_peer(k)[0]).wait_recv()
    for i in range(n):
        layer.VEC[:, i * part : i * part + part] = SM[i]
    near_k = sorted({1, n - 1})
    for k in near_k:
        cq.share(k)
        cu.share(k)
    lx.forward(1)
    for k in range(1, n):
        if k not in near_k:
            cq.share(k)
            cu.share(k)
    for s in range(2, n - 1):
        lx.forward(s)
    lg.start()
    own[0].wait()
    layer.norm(me.z)
    for k in range(1, n):
        cq.hand(k)
        cu.hand(k)
    for i in (2, 3, 4, 5, 6):
        own[i].wait()
    cq.finish()
    cu.finish()

    @pl.loop(0, n)
    def _(k):
        j = pick(near, me.z, k)

        @pl.when(k > 0)
        def _():
            lx.arrive(j)
            layer.norm(j)

        layer.qkv(j)
        layer.up(j)
        layer.down(j)

    lg.forward(1)
    blocks = layer.length // layer.block
    for qb in range(blocks):
        layer.attend_part(qb)

    @pl.loop(0, n)
    def _(k):
        j = pick(far, me.z, k)
        layer.out(j)
        ro.start(j)

    for s in range(2, n - 1):
        lg.forward(s)

    own[1].wait()
    layer.SUMS[4:5] = jnp.sum(layer.G[layer.at(me.z)].astype(F32), axis=0, keepdims=True)

    def put(red):
        def store(i, value):
            parts, unused, rp, cols = red.part.shape
            pieces = value.shape[0] // rp
            value = value.reshape(pieces, rp, cols)
            at = (0, pl.ds(i * pieces, pieces)) if parts == 1 else (i,)
            red.part[at] = value.astype(BF)

        return store

    pairs = layer.heads // 2
    every = slice(0, layer.length)

    @pl.loop(0, n)
    def _(k):
        j = pick(near, me.z, k)
        lg.arrive(j)

        @pl.when(k == n - 1)
        def _():
            layer.down_grad(put(red_dn), every, me.c, red_dn.start)
            layer.dense_grad(put(red_de), every)
            red_de.start()
            red_dn.chip_sums()

        layer.mlp_back(j)
        layer.context_grad(j)

        @pl.when(k == n - 1)
        def _():
            red_de.chip_sums()
            layer.up_grad(put(red_u), every)
            red_u.start()

        @pl.loop(0, pairs)
        def _(m):
            layer.attend_back(j, m)

            @pl.when((k == n - 1) & (m == 0))
            def _():
                red_u.chip_sums()
                red_dn.pair_sums()

        @pl.when(k == n - 2)
        def _():
            ro.step(1)

    for t in range(2, 2 * n - 5):
        ro.step(t)
    red_de.pair_sums()
    copies = [
        pltpu.make_async_copy(red.total.at[0], final.at[me.piece], dsem.at[i])
        for i, (red, final) in enumerate(((red_dn, fdn), (red_de, fde)))
    ]

    @pl.loop(0, n)
    def _(j):
        layer.unturn(j)

    layer.qkv_grad(put(red_q))
    red_q.start()

    @pl.loop(0, n)
    def _(k):
        j = pick(far, me.z, k)
        layer.input_back(j)

        @pl.when(k == 0)
        def _():
            rx.start(j)
            red_u.pair_sums()
            red_q.chip_sums()
            red_dn.sum_up()
            red_de.sum_up()
            for copy in copies:
                copy.start()
            share_dn.start(red_dn.total.at[0])
            share_de.start(red_de.total.at[0])

        @pl.when(k == 1)
        def _():
            red_u.sum_up()
            back_u.start()
            rx.start(j, (0,))

        @pl.when(k == n - 2)
        def _():
            red_q.pair_sums()

    rx.start(pick(far, me.z, 1), (1,))
    layer.fold_sums()
    cs = part
    v1[...] = layer.SUMS[...]

    def small_z(k, slot):
        other, to = me.seq_peer(k)
        return send(
            v1.at[:, pl.ds(pl.multiple_of(other * cs, cs), cs)],
            v1g.at[slot],
            v1s.at[k],
            v1r.at[slot],
            to,
        )

    def small_dp(k, slot):
        return send(v2m, v2g.at[slot], v2s.at[k], v2r.at[slot], me.dp_peer(k)[1])

    for k in range(1, n):
        small_z(k, me.z).start()
    rx.step(1, (0,))
    back_u.wait()
    share_u.start()
    rx.step(1, (1,))
    share_dn.forward()
    share_de.forward()
    red_q.sum_up()
    back_q.start()
    for k in range(2, n - 1):
        rx.start(pick(far, me.z, k))
    ro.total(layer.X, layer.VEC[4:5] + layer.VEC[5:6], out, layer.TMP)
    back_q.wait()
    share_q.start()
    for t in range(2, 2 * n - 5):
        rx.step(t)
    for copy in copies:
        copy.wait()
    share_dn.hand()
    share_de.hand()
    for k in range(1, n):
        small_z(k, me.seq_peer(k)[0]).wait_recv()
    v1g[me.z] = v1[:, pl.ds(pl.multiple_of(me.z * cs, cs), cs)]
    total = v1g[0]
    for k in range(1, n):
        total = total + v1g[k]
    v2m[...] = jnp.zeros_like(v2m)
    v2m[0:8] = total
    for i in range(layer.BUG.shape[1] // cs):
        v2m[8 + i : 9 + i] = layer.BUG[:, i * cs : i * cs + cs]
    for i in range(layer.BQG.shape[1] // cs):
        v2m[12 + i : 13 + i] = layer.BQG[:, i * cs : i * cs + cs]
    for k in range(1, data):
        small_dp(k, me.d).start()
    share_u.forward()
    for k in range(1, data):
        small_dp(k, me.dp_peer(k)[0]).wait_recv()
    v2g[me.d] = v2m[...]

    def add(i, acc):
        return acc + v2g[i]

    small[...] = lax.fori_loop(1, data, add, v2g[0])
    share_q.forward()
    share_u.hand()
    share_q.hand()
    rx.total(layer.G, None, dx, layer.TMP)
    ro.finish()
    rx.finish()
    lx.finish()
    lg.finish()
    for k in range(1, n):
        tiny(k, me.z).wait_send()
        small_z(k, me.z).wait_send()
    for k in range(1, data):
        small_dp(k, me.d).wait_send()
    for red in reduces:
        red.finish()
    for share in shares:
        share.finish()
    back_u.finish()
    back_q.finish()


def rotary_constant(length):
    half = ROT_DIM // 2
    freqs = np.float32(10000.0) ** (-np.arange(half, dtype=np.float32) * np.float32(2.0 / ROT_DIM))
    angles = np.arange(length, dtype=np.float32)[:, None] * freqs.astype(np.float32)[None, :]
    cosine, sine = np.cos(angles), np.sin(angles)
    rest = HEAD_DIM - ROT_DIM
    keep, none, gap = np.ones((length, rest)), np.zeros((length, rest)), np.zeros_like(sine)
    same = np.concatenate([cosine, cosine, keep] * 2, axis=1)
    up = np.concatenate([-sine, gap, none] * 2, axis=1)
    down = np.concatenate([gap, sine, none] * 2, axis=1)
    return np.stack([same, up, down]).astype(np.float32)


def whole_layer(n, data, vectors, x, g, wq, wu, w_dense, w_down, b_qkv, b_up):
    rows, width = x.shape
    length = n * rows
    packed, hidden = wq.shape[1] // n, wu.shape[1] // n
    heads = packed // (3 * HEAD_DIM)
    depth = wq.shape[0]
    chunks = 4
    groups = data // PLANE
    vm = pl.BlockSpec(memory_space=pltpu.VMEM)
    hbm = pl.BlockSpec(memory_space=pl.ANY)
    dma = pltpu.SemaphoreType.DMA
    sds = jax.ShapeDtypeStruct
    mem = pltpu.VMEM
    named = layer_scratch(length, width, heads, hidden)
    named.update(
        X=mem((length, width), BF),
        G=mem((length, width), BF),
        WQ=mem((width, packed), BF),
        WU=mem((width, hidden), BF),
        VEC=mem((8, width), F32),
        WDE=mem(w_dense.shape, BF),
        WDN=mem(w_down.shape, BF),
        ROT=mem((3, length, 128), F32),
        OP=mem((length, width), BF),
        SUMS=mem((8, width), F32),
        BUG=mem((1, hidden), F32),
        BQG=mem((1, packed), F32),
        BQ=mem((1, packed), F32),
        BU=mem((1, hidden), F32),
        TMP=mem((rows, width), F32),
        COLS=mem((4, 8, width), F32),
    )
    scratch = list(named.values())
    scratch += [mem((n, 8, depth), F32), mem((8, depth), F32)]
    scratch += [dma((7,)), dma((n,)), dma((n,))]
    scratch += [dma((2, n, chunks)), dma((n, chunks))] * 2
    scratch += column_sems(n) + column_sems(n)
    scratch += [mem((n + 1, 2, rows // 2, width), BF)] * 2
    scratch += [dma((n, 2)), dma((n + 1, 2))] * 2
    scratch += [mem((8, width), F32), mem((n, 8, depth), F32), dma((n,)), dma((n,))]
    scratch += [mem((16, depth), F32), mem((data, 16, depth), F32), dma((data,)), dma((data,))]
    shapes = [
        (1, hidden // PLANE, width),
        (1, packed // 3 // PLANE, width),
        (n, depth // PLANE, hidden),
        (n, depth // PLANE, packed),
    ]
    for m, rp, cols in shapes:
        scratch += [mem((m, PLANE, rp, cols), BF)] + reduce_scratch(m, rp, cols, groups)
    for unused in range(4):
        scratch += share_sems()
    scratch += [dma((n,)), dma((n,)), dma] * 2
    scratch += [dma((4,))]
    outs = [
        sds((rows, width), BF),
        sds((rows, width), BF),
        sds((16, depth), F32),
        sds((PLANE, depth // PLANE, hidden * n), BF),
        sds((PLANE, depth // PLANE, packed * n), BF),
        sds((PLANE, hidden // PLANE, width), BF),
        sds((PLANE, packed // 3 // PLANE, width), BF),
    ]
    return pl.pallas_call(
        functools.partial(layer_kernel, n, data, chunks, list(named)),
        out_shape=outs,
        in_specs=[vm] * VECTORS + [hbm] * 7 + [vm] * 2,
        out_specs=[vm] * 3 + [hbm] * 4,
        scratch_shapes=scratch,
        compiler_params=pltpu.CompilerParams(
            collective_id=2, has_side_effects=True, vmem_limit_bytes=67043328
        ),
        name="layer",
    )(*vectors, x, g, wq, wu, w_dense, w_down, rotary_constant(length), b_qkv, b_up)


def fits(n, data, tokens, qkv, up):
    unused, rows, width = tokens
    length, depth = n * rows, qkv[0]
    return (
        length * (width + up[1] // n) <= 1024 * 2048
        and rows == 256
        and depth == 256
        and up[1] // n == width
        and up[1] // n % 256 == 0
        and qkv[1] // n % (6 * HEAD_DIM) == 0
    )


def per_device(
    n,
    data,
    layer_input,
    attn_gain,
    attn_shift,
    mlp_gain,
    mlp_shift,
    qkv_weight,
    qkv_bias,
    dense_weight,
    dense_bias,
    up_weight,
    up_bias,
    down_weight,
    down_bias,
    out_grad,
):
    unused, rows, width = layer_input.shape
    x = layer_input.reshape(rows, width)
    g = out_grad.reshape(rows, width)
    part = width // n
    if fits(n, data, layer_input.shape, qkv_weight.shape, up_weight.shape):
        vectors = (attn_gain, attn_shift, mlp_gain, mlp_shift, dense_bias, down_bias)
        out, dx, tiny, fu, fq, fdn, fde = whole_layer(
            n, data, vectors, x, g, qkv_weight, up_weight, dense_weight, down_weight,
            qkv_bias, up_bias,
        )
    else:
        small = jnp.stack(
            [attn_gain, attn_shift, mlp_gain, mlp_shift, dense_bias, down_bias] + [attn_gain] * 2
        ).astype(F32)
        SM, X, G, WQ, WU = gather(n, data, small, x, g, qkv_weight, up_weight)
        vectors = jnp.swapaxes(SM, 0, 1).reshape(8, width)
        bias = (vectors[4] + vectors[5])[None]
        OP, DX, sums, bu, bq, UG, QG, DnG, DeG = middle(
            X, G, WQ, WU, dense_weight, down_weight, qkv_bias, up_bias, vectors
        )
        v1 = jnp.concatenate(
            [sums, jnp.sum(g.astype(F32), axis=0)[None], jnp.zeros((3, width), F32)], axis=0
        )
        v2 = jnp.concatenate(
            [bu.reshape(4, part), bq.reshape(3, part), jnp.zeros((1, part), F32)]
        )
        out, dx, tiny, fu, fq, fdn, fde = reduce_all(
            n, data, OP, DX, v1, v2, bias, x, g, UG, QG, DnG, DeG
        )
    results = finish(part, out, dx, tiny, fu, fq, fdn, fde)
    return tuple(r.reshape(layer_input.shape) for r in results[:2]) + tuple(results[2:])


def finish_kernel(part, out, dx, tiny, fu, fq, fdn, fde, *results):
    (o_out, o_dx, ag, ash, mg, ms, gq, bq, gde, bde, gu, bu, gdn, bdn) = results
    o_out[...] = out[...]
    o_dx[...] = dx[...]
    for source, result in ((fq, gq), (fde, gde), (fu, gu), (fdn, gdn)):
        result[...] = source[...].astype(F32)

    @pl.when(pl.program_id(0) == 0)
    def _():
        for row, result in enumerate((ag, ash, mg, ms, bde)):
            result[...] = tiny[row]
        bdn[...] = tiny[4]
        for base, result in ((8, bu), (12, bq)):
            for i in range(result.shape[0] // part):
                result[i * part : i * part + part] = tiny[base + i]


def finish(part, out, dx, tiny, fu, fq, fdn, fde):
    steps = 4
    sds = jax.ShapeDtypeStruct

    def tile(rows, cols):
        return pl.BlockSpec((rows // steps, cols), lambda i: (i, 0))

    def line(size):
        return sds((size,), F32), pl.BlockSpec((size,), lambda i: (0,))

    wide = [a.reshape(-1, a.shape[-1]) for a in (fu, fq, fdn, fde)]
    gu, gq, gdn, gde = ((sds(a.shape, F32), tile(*a.shape)) for a in wide)
    tokens = (sds(out.shape, BF), tile(*out.shape))
    vector = line(part)
    shapes, specs = zip(
        tokens, tokens, vector, vector, vector, vector, gq, line(fq.shape[-1] // (fu.shape[-1] // gdn[0].shape[0])),
        gde, vector, gu, line(gdn[0].shape[0]), gdn, vector,
    )
    return pl.pallas_call(
        functools.partial(finish_kernel, part),
        grid=(steps,),
        out_shape=shapes,
        in_specs=[tile(*out.shape), tile(*out.shape), pl.BlockSpec(tiny.shape, lambda i: (0, 0))]
        + [tile(*a.shape) for a in wide],
        out_specs=specs,
        compiler_params=pltpu.CompilerParams(vmem_limit_bytes=63 << 20),
        name="finish",
    )(out, dx, tiny, *wide)


def solution(mesh):
    tokens, row, vector = P("dp", "seq", None), P("seq", None), P("seq")
    in_specs = (tokens,) + (vector,) * 4 + (row, vector) * 4 + (tokens,)
    out_specs = (tokens, tokens) + (vector,) * 4 + (row, vector) * 4
    return jax.shard_map(
        functools.partial(per_device, mesh.shape["seq"], mesh.shape["dp"]),
        mesh=mesh,
        in_specs=in_specs,
        out_specs=out_specs,
        check_vma=False,
    )
```

```python
import functools
import math

import jax
import jax.numpy as jnp
import numpy as np
from jax import lax
from jax.experimental import pallas as pl
from jax.experimental.pallas import tpu as pltpu
from jax.sharding import PartitionSpec as P

HEADS = 16
HEAD_DIM = 64
ROT_DIM = 16
PLANE = 8
CHIPS = 4
epsilon = 1e-05
mask_fill = -1e30
MESH = pl.DeviceIdType.MESH
BF = jnp.bfloat16
F32 = jnp.float32


def rows_at(ref, start, count):
    return ref.at[pl.ds(pl.multiple_of(start, count), count)]


def block_at(ref, row, rows, col, cols):
    return ref.at[
        pl.ds(pl.multiple_of(row, rows), rows), pl.ds(pl.multiple_of(col, cols), cols)
    ]


class Place:
    def __init__(self, n, data):
        self.n, self.data = n, data
        self.d = lax.axis_index("dp")
        self.z = lax.axis_index("seq")
        self.base = self.d // PLANE * PLANE
        self.r = lax.rem(self.d, PLANE)
        self.ch = self.r // 2
        self.c = lax.rem(self.r, 2)
        self.piece = self.c * CHIPS + self.ch

    def seq_peer(self, k):
        other = lax.rem(self.z + k, self.n)
        return other, (self.d, other)

    def chip_peer(self, k):
        other = lax.rem(self.ch + k, CHIPS)
        return other, (self.base + other * 2 + self.c, self.z)

    def beside(self, way):
        other = self.ch + 1 - 2 * lax.rem(self.ch, 2) if way == 0 else lax.rem(self.ch + 2, CHIPS)
        return other, (self.base + other * 2 + self.c, self.z)

    def partner(self):
        return (self.base + self.ch * 2 + 1 - self.c, self.z)

    def dp_peer(self, k):
        other = lax.rem(self.d + k, self.data)
        return other, (other, self.z)

    def barrier(self):
        self.greet()
        self.met()

    def greet(self):
        sem = pltpu.get_barrier_semaphore()
        for k in range(1, self.n):
            pl.semaphore_signal(sem, inc=1, device_id=self.seq_peer(k)[1], device_id_type=MESH)
        for k in range(1, self.data):
            pl.semaphore_signal(sem, inc=1, device_id=self.dp_peer(k)[1], device_id_type=MESH)

    def met(self):
        pl.semaphore_wait(pltpu.get_barrier_semaphore(), self.n - 1 + self.data - 1)


def send(src, dst, ssem, rsem, to):
    return pltpu.make_async_remote_copy(
        src_ref=src, dst_ref=dst, send_sem=ssem, recv_sem=rsem, device_id=to, device_id_type=MESH
    )


class LineGather:
    def __init__(self, me, shard, full, rows, chunks, ssem, rsem):
        self.me, self.shard, self.full = me, shard, full
        self.rows, self.chunks, self.ssem, self.rsem = rows, chunks, ssem, rsem

    def part(self, owner, c):
        size = self.rows // self.chunks
        return rows_at(self.full, owner * self.rows + c * size, size)

    def copy(self, src, owner, c, way):
        me = self.me
        to = jnp.minimum(me.z + 1, me.n - 1) if way == 0 else jnp.maximum(me.z - 1, 0)
        return send(
            src,
            self.part(owner, c),
            self.ssem.at[way, owner, c],
            self.rsem.at[owner, c],
            (me.d, to),
        )

    def start(self):
        me = self.me
        size = self.rows // self.chunks
        for c in range(self.chunks):
            src = rows_at(self.shard, c * size, size)

            @pl.when(me.z < me.n - 1)
            def _():
                self.copy(src, me.z, c, 0).start()

            @pl.when(me.z > 0)
            def _():
                self.copy(src, me.z, c, 1).start()

    def step(self, s, c):
        me = self.me

        @pl.when(me.z >= s)
        def _():
            owner = me.z - s
            copy = self.copy(self.part(owner, c), owner, c, 0)
            copy.wait_recv()

            @pl.when(me.z < me.n - 1)
            def _():
                copy.start()

        @pl.when(me.z + s < me.n)
        def _():
            owner = me.z + s
            copy = self.copy(self.part(owner, c), owner, c, 1)
            copy.wait_recv()

            @pl.when(me.z > 0)
            def _():
                copy.start()

    def forward(self, s):
        me = self.me
        inner = (me.z > 0) & (me.z < me.n - 1)
        for c in range(self.chunks):
            for way, valid, owner in ((0, me.z >= s, me.z - s), (1, me.z + s < me.n, me.z + s)):

                @pl.when(inner & valid)
                def _():
                    copy = self.copy(self.part(owner, c), owner, c, way)
                    copy.wait_recv()
                    copy.start()

    def arrive(self, owner):
        me = self.me

        @pl.when(((me.z == 0) | (me.z == me.n - 1)) & (owner != me.z))
        def _():
            for c in range(self.chunks):
                self.copy(self.part(owner, c), owner, c, 0).wait_recv()

    def finish(self):
        me = self.me
        for c in range(self.chunks):
            for owner in range(me.n):

                @pl.when((me.z < me.n - 1) & (owner <= me.z))
                def _():
                    self.copy(self.part(owner, c), owner, c, 0).wait_send()

                @pl.when((me.z > 0) & (owner >= me.z))
                def _():
                    self.copy(self.part(owner, c), owner, c, 1).wait_send()


class ColumnGather:
    def __init__(self, me, shard, full, sems):
        self.me, self.shard, self.full = me, shard, full
        self.depth = shard.shape[0]
        self.rp = self.depth // PLANE
        self.cols = full.shape[1]
        self.zs, self.zr, self.ps, self.pr, self.fs = sems

    def part(self, src_z, piece):
        return rows_at(self.full, (src_z * PLANE + piece) * self.rp, self.rp)

    def across(self, k):
        me = self.me
        other, to = me.seq_peer(k)
        src = block_at(self.shard, me.piece * self.rp, self.rp, other * self.cols, self.cols)
        return send(src, self.part(me.z, me.piece), self.zs.at[k], self.zr.at[me.n - k], to)

    def came(self, k):
        me = self.me
        other, to = me.seq_peer(k)
        src = block_at(self.shard, me.piece * self.rp, self.rp, other * self.cols, self.cols)
        return send(src, self.part(other, me.piece), self.zs.at[k], self.zr.at[k], to)

    def shares(self, k):
        me = self.me
        other, unused = me.seq_peer(k)
        mine = self.part(other, me.piece)
        for j in range(1, CHIPS):
            to = me.chip_peer(j)[1]
            yield send(mine, mine, self.ps.at[k, j], self.pr.at[k, CHIPS - j], to)
        yield send(mine, mine, self.ps.at[k, 0], self.fs.at[1, k, 0], me.partner())

    def handed(self, k, j):
        me = self.me
        other, unused = me.seq_peer(k)
        chip = me.chip_peer(j)[0]
        return self.part(other, me.c * CHIPS + chip), self.part(other, (1 - me.c) * CHIPS + chip)

    def start(self):
        for k in range(self.me.n - 1, 0, -1):
            self.across(k).start()

    def share(self, k):
        self.came(k).wait_recv()
        for copy in self.shares(k):
            copy.start()

    def hand(self, k):
        me = self.me
        for j in range(1, CHIPS):
            got, unused = self.handed(k, j)
            send(got, got, self.ps.at[k, j], self.pr.at[k, j], me.chip_peer(j)[1]).wait_recv()
            send(got, got, self.fs.at[0, k, j], self.fs.at[1, k, j], me.partner()).start()

    def finish(self):
        me = self.me
        for k in range(1, me.n):
            self.across(k).wait_send()
            for copy in self.shares(k):
                copy.wait_send()
            other, unused = me.seq_peer(k)
            for j in range(CHIPS):
                unused, got = self.handed(k, j)
                copy = send(got, got, self.fs.at[0, k, j], self.fs.at[1, k, j], me.partner())
                copy.wait_recv()
                if j > 0:
                    copy.wait_send()


def column_sems(n):
    dma = pltpu.SemaphoreType.DMA
    return [dma((n,)), dma((n,)), dma((n, CHIPS)), dma((n, CHIPS)), dma((2, n, CHIPS))]


def gather_kernel(n, data, chunks, sm, x, g, wq, wu, SM, X, G, WQ, WU, *sems):
    me = Place(n, data)
    rows = x.shape[0]
    lsem, ss, sr, xs, xr, gs, gr = sems[:7]
    me.barrier()
    cq, cu = ColumnGather(me, wq, WQ, sems[7:12]), ColumnGather(me, wu, WU, sems[12:17])
    lx = LineGather(me, x, X, rows, chunks, xs, xr)
    lg = LineGather(me, g, G, rows, chunks, gs, gr)
    depth = wq.shape[0]
    own = [
        pltpu.make_async_copy(sm, SM.at[me.z], lsem.at[0]),
        pltpu.make_async_copy(x, rows_at(X, me.z * rows, rows), lsem.at[1]),
        pltpu.make_async_copy(g, rows_at(G, me.z * rows, rows), lsem.at[2]),
        pltpu.make_async_copy(
            block_at(wq, 0, depth, me.z * WQ.shape[1], WQ.shape[1]),
            rows_at(WQ, me.z * depth, depth),
            lsem.at[3],
        ),
        pltpu.make_async_copy(
            block_at(wu, 0, depth, me.z * WU.shape[1], WU.shape[1]),
            rows_at(WU, me.z * depth, depth),
            lsem.at[4],
        ),
    ]
    for copy in own:
        copy.start()

    def small(k, slot):
        return send(sm, SM.at[slot], ss.at[k], sr.at[slot], me.seq_peer(k)[1])

    for k in range(1, n):
        small(k, me.z).start()
    cq.start()
    cu.start()
    lx.start()
    lg.start()
    near = sorted({1, n - 1})
    for k in near:
        cq.share(k)
        cu.share(k)
    for c in range(chunks):
        lx.step(1, c)
    for k in range(1, n):
        if k not in near:
            cq.share(k)
            cu.share(k)
    for s in range(2, n):
        for c in range(chunks):
            lx.step(s, c)
    for k in range(1, n):
        cq.hand(k)
        cu.hand(k)
    for s in range(1, n):
        for c in range(chunks):
            lg.step(s, c)
    for k in range(1, n):
        small(k, me.z).wait_send()
        small(k, me.seq_peer(k)[0]).wait_recv()
    cq.finish()
    cu.finish()
    lx.finish()
    lg.finish()
    for copy in own:
        copy.wait()


def gather(n, data, sm, x, g, wq, wu):
    rows, width = x.shape
    depth = wq.shape[0]
    chunks = 4
    vm = pl.BlockSpec(memory_space=pltpu.VMEM)
    dma = pltpu.SemaphoreType.DMA
    sds = jax.ShapeDtypeStruct
    return pl.pallas_call(
        functools.partial(gather_kernel, n, data, chunks),
        out_shape=[
            sds((n,) + sm.shape, sm.dtype),
            sds((n * rows, width), x.dtype),
            sds((n * rows, width), x.dtype),
            sds((n * depth, wq.shape[1] // n), wq.dtype),
            sds((n * depth, wu.shape[1] // n), wu.dtype),
        ],
        in_specs=[vm] * 5,
        out_specs=[vm] * 5,
        scratch_shapes=[
            dma((5,)),
            dma((n,)),
            dma((n,)),
            dma((2, n, chunks)),
            dma((n, chunks)),
            dma((2, n, chunks)),
            dma((n, chunks)),
        ]
        + column_sems(n)
        + column_sems(n),
        compiler_params=pltpu.CompilerParams(
            collective_id=0, has_side_effects=True, vmem_limit_bytes=60 << 20
        ),
        name="gather",
    )(sm, x, g, wq, wu)


class RowReduce:
    def __init__(self, me, part, got, ssem, rsem):
        self.me, self.part, self.got, self.ssem, self.rsem = me, part, got, ssem, rsem
        self.rows = got.shape[1]

    def copy(self, k, slot):
        other, to = self.me.seq_peer(k)
        return send(
            rows_at(self.part, other * self.rows, self.rows),
            self.got.at[slot],
            self.ssem.at[k],
            self.rsem.at[slot],
            to,
        )

    def start(self):
        for k in range(1, self.me.n):
            self.copy(k, self.me.z).start()

    def wait(self):
        for k in range(1, self.me.n):
            self.copy(k, self.me.seq_peer(k)[0]).wait_recv()

    def finish(self):
        for k in range(1, self.me.n):
            self.copy(k, self.me.z).wait_send()


def halves(cols):
    middle = cols // 2 // 128 * 128
    return slice(0, middle), slice(middle, cols)


class GradReduce:
    def __init__(self, me, part, half, near, far, total, groups, sems):
        self.me, self.part, self.half, self.near, self.far = me, part, half, near, far
        self.total, self.groups = total, groups
        self.hs, self.hr, self.ns, self.nr, self.fs, self.fr, self.gs, self.gr = sems
        self.cols = halves(part.shape[3])

    def swap(self):
        me = self.me
        return send(
            self.part.at[:, pl.ds((1 - me.c) * CHIPS, CHIPS)],
            self.half,
            self.hs,
            self.hr,
            me.partner(),
        )

    def piece(self, way, index, other):
        me = self.me
        a, b = me.ch // 2, lax.rem(me.ch, 2)
        if way == 0:
            chip = index * 2 + (1 - b if other else b)
        else:
            chip = (1 - a if other else a) * 2 + index
        return me.c * CHIPS + chip

    def first(self, way, index):
        return send(
            self.part.at[:, self.piece(way, index, True), :, self.cols[way]],
            self.near[way].at[index],
            self.ns.at[way, index],
            self.nr.at[way, index],
            self.me.beside(way)[1],
        )

    def second(self, way):
        a, b = self.me.ch // 2, lax.rem(self.me.ch, 2)
        other = 1 - a if way == 0 else 1 - b
        return send(
            self.part.at[:, self.piece(way, other, False), :, self.cols[way]],
            self.far[way],
            self.fs.at[way],
            self.fr.at[way],
            self.me.beside(1 - way)[1],
        )

    def start(self):
        self.swap().start()

    def chip_sums(self):
        me = self.me
        self.swap().wait_recv()

        @pl.loop(0, CHIPS)
        def _(j):
            for m in range(self.half.shape[0]):
                self.part[m, me.c * CHIPS + j] = (
                    self.part[m, me.c * CHIPS + j].astype(F32) + self.half[m, j].astype(F32)
                ).astype(BF)

        for way in range(2):
            for index in range(2):
                self.first(way, index).start()

    def pair_sums(self):
        for way in range(2):
            for index in range(2):
                self.first(way, index).wait_recv()
            cols = self.cols[way]
            for index in range(2):
                piece = self.piece(way, index, False)
                for m in range(self.half.shape[0]):
                    self.part[m, piece, :, cols] = (
                        self.part[m, piece, :, cols].astype(F32)
                        + self.near[way][index, m].astype(F32)
                    ).astype(BF)
            self.second(way).start()

    def to_group(self, k, slot):
        me = self.me
        count = me.data // PLANE
        other = lax.rem(me.d // PLANE + k, count)
        return send(
            self.total,
            self.groups.at[slot],
            self.gs.at[k],
            self.gr.at[slot],
            (other * PLANE + me.r, me.z),
        )

    def sum_up(self):
        me = self.me
        for way in range(2):
            self.second(way).wait_recv()
            cols = self.cols[way]
            for m in range(self.total.shape[0]):
                self.total[m, :, cols] = (
                    self.part[m, me.piece, :, cols].astype(F32) + self.far[way][m].astype(F32)
                ).astype(BF)
        count = me.data // PLANE
        if count > 1:
            own = me.d // PLANE
            for k in range(1, count):
                self.to_group(k, own).start()
            for k in range(1, count):
                self.to_group(k, lax.rem(own + k, count)).wait_recv()
                self.to_group(k, own).wait_send()
            self.groups[own] = self.total[...]
            total = self.groups[0].astype(F32)
            for e in range(1, count):
                total = total + self.groups[e].astype(F32)
            self.total[...] = total.astype(BF)

    def finish(self):
        self.swap().wait_send()
        for way in range(2):
            for index in range(2):
                self.first(way, index).wait_send()
            self.second(way).wait_send()


def reduce_scratch(m, rp, cols, groups):
    mem, dma = pltpu.VMEM, pltpu.SemaphoreType.DMA
    widths = [part.stop - part.start for part in halves(cols)]
    return (
        [mem((m, CHIPS, rp, cols), BF)]
        + [mem((2, m, rp, width), BF) for width in widths]
        + [mem((m, rp, width), BF) for width in widths]
        + [
            mem((m, rp, cols), BF),
            mem((groups, m, rp, cols) if groups > 1 else (1, 1, 16, 128), BF),
            dma,
            dma,
            dma((2, 2)),
            dma((2, 2)),
            dma((2,)),
            dma((2,)),
            dma((groups,)),
            dma((groups,)),
        ]
    )


def take_reduce(me, part, take):
    half, near0, near1, far0, far1, total, groups = take(7)
    return GradReduce(me, part, half, (near0, near1), (far0, far1), total, groups, take(8))


class GradShare:
    def __init__(self, me, final, sems):
        self.me, self.final = me, final
        self.ss, self.sr, self.fs, self.fr, self.hs, self.hr = sems
        self.cols = halves(final.shape[2])

    def own(self, way, source=None):
        mine = self.final.at[self.me.piece]
        return send(
            mine if source is None else source,
            mine,
            self.ss.at[way],
            self.sr.at[way],
            self.me.beside(way)[1],
        )

    def to_partner(self, index, chip, core, source=None):
        got = self.final.at[core * CHIPS + chip]
        return send(
            got if source is None else source,
            got,
            self.hs.at[index],
            self.hr.at[index],
            self.me.partner(),
        )

    def onward(self, way, chip):
        got = self.final.at[self.me.c * CHIPS + chip, :, self.cols[way]]
        return send(got, got, self.fs.at[way], self.fr.at[way], self.me.beside(1 - way)[1])

    def across(self):
        return CHIPS - 1 - self.me.ch

    def start(self, source=None):
        for way in range(2):
            self.own(way, source).start()
        self.to_partner(0, self.me.ch, self.me.c, source).start()

    def forward(self):
        me = self.me
        for way in range(2):
            chip = me.beside(way)[0]
            got = self.final.at[me.c * CHIPS + chip]
            send(got, got, self.ss.at[way], self.sr.at[way], me.beside(way)[1]).wait_recv()
            self.onward(way, chip).start()
            self.to_partner(1 + way, chip, me.c).start()

    def hand(self):
        for way in range(2):
            self.onward(way, self.across()).wait_recv()
        self.to_partner(3, self.across(), self.me.c).start()

    def finish(self):
        me = self.me
        chips = [me.ch, me.beside(0)[0], me.beside(1)[0], self.across()]
        for way in range(2):
            self.own(way).wait_send()
            self.onward(way, chips[1 + way]).wait_send()
        for index, chip in enumerate(chips):
            self.to_partner(index, chip, me.c).wait_send()
            self.to_partner(index, chip, 1 - me.c).wait_recv()


def share_sems():
    dma = pltpu.SemaphoreType.DMA
    return [dma((2,))] * 4 + [dma((4,))] * 2


class RowsBack:
    def __init__(self, me, total, final, ssem, rsem, lsem):
        self.me, self.total, self.final = me, total, final
        self.ssem, self.rsem, self.lsem = ssem, rsem, lsem

    def place(self, src_z):
        cols = self.total.shape[2]
        return self.final.at[
            self.me.piece, :, pl.ds(pl.multiple_of(src_z * cols, cols), cols)
        ]

    def copy(self, k, slot):
        other, to = self.me.seq_peer(k)
        return send(
            self.total.at[other], self.place(slot), self.ssem.at[k], self.rsem.at[slot], to
        )

    def own(self):
        me = self.me
        return pltpu.make_async_copy(self.total.at[me.z], self.place(me.z), self.lsem)

    def start(self):
        for k in range(1, self.me.n):
            self.copy(k, self.me.z).start()
        self.own().start()

    def wait(self):
        me = self.me
        for k in range(1, me.n):
            self.copy(k, me.seq_peer(k)[0]).wait_recv()
        self.own().wait()

    def finish(self):
        for k in range(1, self.me.n):
            self.copy(k, self.me.z).wait_send()


def reduce_kernel(n, data, *refs):
    (OP, DX, v1, v2, bias, x, g, UG, QG, DnG, DeG) = refs[:11]
    out, dx, small, fu, fq, fdn, fde = refs[11:18]
    scratch = list(refs[18:])
    me = Place(n, data)

    def take(count):
        got = scratch[:count]
        del scratch[:count]
        return got

    og, xg, zs, zr, v1g, v1s, v1r, v2m, v2g, v2s, v2r = take(11)
    reduces = []
    for part in (DnG, DeG, UG, QG):
        reduces.append(take_reduce(me, part, take))
    red_dn, red_de, red_u, red_q = reduces
    shares = [GradShare(me, final, take(6)) for final in (fdn, fde, fu, fq)]
    back_u = RowsBack(me, red_u.total, fu, *take(3))
    back_q = RowsBack(me, red_q.total, fq, *take(3))
    (dsem,) = take(1)
    assert not scratch
    ro = RowReduce(me, OP, og, zs.at[0], zr.at[0])
    rx = RowReduce(me, DX, xg, zs.at[1], zr.at[1])
    me.barrier()
    cs = v1g.shape[2]

    def small_z(k, slot):
        other, to = me.seq_peer(k)
        return send(
            v1.at[:, pl.ds(pl.multiple_of(other * cs, cs), cs)],
            v1g.at[slot],
            v1s.at[k],
            v1r.at[slot],
            to,
        )

    def small_dp(k, slot):
        return send(v2m, v2g.at[slot], v2s.at[k], v2r.at[slot], me.dp_peer(k)[1])

    for k in range(1, n):
        small_z(k, me.z).start()
    for red in reduces:
        red.start()
    ro.start()
    rx.start()
    for red in reduces:
        red.chip_sums()
    for red in reduces:
        red.pair_sums()
    for k in range(1, n):
        small_z(k, me.seq_peer(k)[0]).wait_recv()
    v1g[me.z] = v1[:, pl.ds(pl.multiple_of(me.z * cs, cs), cs)]
    total = v1g[0]
    for k in range(1, n):
        total = total + v1g[k]
    v2m[0:8] = total
    v2m[8:16] = v2[...]
    for k in range(1, data):
        small_dp(k, me.d).start()
    own = []
    for i, (red, final) in enumerate(((red_dn, fdn), (red_de, fde))):
        red.sum_up()
        copy = pltpu.make_async_copy(red.total.at[0], final.at[me.piece], dsem.at[i])
        copy.start()
        own.append(copy)
    red_u.sum_up()
    back_u.start()
    red_q.sum_up()
    back_q.start()
    for copy in own:
        copy.wait()
    shares[0].start()
    shares[1].start()
    back_u.wait()
    shares[2].start()
    back_q.wait()
    shares[3].start()
    for share in shares:
        share.forward()
    for share in shares:
        share.hand()
    for k in range(1, data):
        small_dp(k, me.dp_peer(k)[0]).wait_recv()
    v2g[me.d] = v2m[...]

    def add(i, acc):
        return acc + v2g[i]

    small[...] = lax.fori_loop(1, data, add, v2g[0])
    rows = x.shape[0]
    for red, base, result, extra in ((ro, x, out, bias), (rx, g, dx, None)):
        red.wait()
        step = rows // 4

        @pl.loop(0, 4)
        def _(i):
            at = pl.ds(pl.multiple_of(i * step, step), step)
            mine = pl.ds(pl.multiple_of(me.z * rows + i * step, step), step)
            acc = base[at].astype(F32) + red.part[mine].astype(F32)
            for k in range(1, n):
                acc = acc + red.got[me.seq_peer(k)[0], at].astype(F32)
            if extra is not None:
                acc = acc + extra[...]
            result[at] = acc.astype(BF)

        red.finish()
    for k in range(1, n):
        small_z(k, me.z).wait_send()
    for k in range(1, data):
        small_dp(k, me.d).wait_send()
    for red in reduces:
        red.finish()
    for share in shares:
        share.finish()
    back_u.finish()
    back_q.finish()


def reduce_all(n, data, OP, DX, v1, v2, bias, x, g, UG, QG, DnG, DeG):
    vm = pl.BlockSpec(memory_space=pltpu.VMEM)
    dma = pltpu.SemaphoreType.DMA
    sds = jax.ShapeDtypeStruct
    rows, width = x.shape
    groups = data // PLANE
    parts = []
    for whole in (DnG, DeG):
        lead, cols = whole.shape
        parts.append(whole.reshape(1, PLANE, lead // PLANE, cols))
    for whole in (UG, QG):
        lead, cols = whole.shape
        parts.append(whole.reshape(n, PLANE, lead // n // PLANE, cols))
    dn, de, u, q = parts
    scratch = [
        pltpu.VMEM((n, rows, width), BF),
        pltpu.VMEM((n, rows, width), BF),
        dma((2, n)),
        dma((2, n)),
        pltpu.VMEM((n, 8, width // n), F32),
        dma((n,)),
        dma((n,)),
        pltpu.VMEM((16, width // n), F32),
        pltpu.VMEM((data, 16, width // n), F32),
        dma((data,)),
        dma((data,)),
    ]
    for part in (dn, de, u, q):
        m, unused, rp, cols = part.shape
        scratch += reduce_scratch(m, rp, cols, groups)
    for unused in range(4):
        scratch += share_sems()
    scratch += [dma((n,)), dma((n,)), dma] * 2
    scratch += [dma((2,))]
    outs = [
        sds((rows, width), BF),
        sds((rows, width), BF),
        sds((16, width // n), F32),
        sds((PLANE, u.shape[2], u.shape[3] * n), BF),
        sds((PLANE, q.shape[2], q.shape[3] * n), BF),
        sds((PLANE,) + dn.shape[2:], BF),
        sds((PLANE,) + de.shape[2:], BF),
    ]
    return pl.pallas_call(
        functools.partial(reduce_kernel, n, data),
        out_shape=outs,
        in_specs=[vm] * 11,
        out_specs=[vm] * 7,
        scratch_shapes=scratch,
        compiler_params=pltpu.CompilerParams(
            collective_id=1, has_side_effects=True, vmem_limit_bytes=63 << 20
        ),
        name="reduce",
    )(OP, DX, v1, v2, bias, x, g, u, q, dn, de)


def layer_norm_parts(token_rows):
    average = jnp.mean(token_rows, axis=-1, keepdims=True)
    centered = token_rows - average
    variance = jnp.mean(centered * centered, axis=-1, keepdims=True)
    inverse = lax.rsqrt(variance + epsilon)
    return centered * inverse, inverse


def rotate(packed, positions, sign):
    half = ROT_DIM // 2
    freqs = 10000.0 ** (-jnp.arange(half, dtype=F32) * 2.0 / ROT_DIM)
    angles = positions.astype(F32)[:, None] * freqs[None, :]
    cosine = jnp.cos(angles)[:, None, None, :]
    sine = jnp.sin(angles)[:, None, None, :] * sign
    first = packed[..., :half]
    second = packed[..., half:ROT_DIM]
    turned = jnp.concatenate(
        [first * cosine - second * sine, second * cosine + first * sine, packed[..., ROT_DIM:]],
        axis=-1,
    )
    select = (jnp.arange(3) < 2)[:, None]
    return jnp.where(select, turned, packed)


def middle(X, G, WQ, WU, w_dense, w_down, b_qkv, b_up, vectors):
    length, width = X.shape
    heads = WQ.shape[1] // (3 * HEAD_DIM)
    scale = HEAD_DIM ** (-0.5)
    gain_one, shift_one, gain_two, shift_two = (vectors[i] for i in range(4))
    xhat, inverse = layer_norm_parts(X.astype(F32))
    norm_one = (xhat * gain_one + shift_one).astype(BF)
    norm_two = (xhat * gain_two + shift_two).astype(BF)
    packed = jnp.dot(norm_one, WQ, preferred_element_type=F32) + b_qkv.astype(F32)
    positions = jnp.arange(length, dtype=jnp.int32)
    packed = rotate(packed.reshape(length, heads, 3, HEAD_DIM), positions, 1.0).astype(BF)
    query, keys, values = packed[:, :, 0], packed[:, :, 1], packed[:, :, 2]
    scores = jnp.einsum("qhd,khd->hqk", query, keys, preferred_element_type=F32) * scale
    allowed = positions[:, None] >= positions[None, :]
    probs = jax.nn.softmax(jnp.where(allowed, scores, mask_fill), axis=-1)
    low = probs.astype(BF)
    context = jnp.einsum("hqk,khd->qhd", low, values, preferred_element_type=F32)
    context = context.astype(BF).reshape(length, heads * HEAD_DIM)
    hidden = jnp.dot(norm_two, WU, preferred_element_type=F32) + b_up.astype(F32)
    active = jax.nn.gelu(hidden, approximate=False).astype(BF)
    out = jnp.dot(context, w_dense, preferred_element_type=F32) + jnp.dot(
        active, w_down, preferred_element_type=F32
    )
    down_grad = jnp.einsum("tf,to->fo", active, G, preferred_element_type=F32)
    dense_grad = jnp.einsum("ti,to->io", context, G, preferred_element_type=F32)
    active_grad = jnp.einsum("to,fo->tf", G, w_down, preferred_element_type=F32)
    unused, pull = jax.vjp(lambda v: jax.nn.gelu(v, approximate=False), hidden)
    hidden_grad = pull(active_grad)[0].astype(BF)
    up_bias_grad = jnp.sum(hidden_grad.astype(F32), axis=0)
    up_grad = jnp.einsum("ti,tf->if", norm_two, hidden_grad, preferred_element_type=F32)
    norm_two_grad = jnp.einsum("tf,if->ti", hidden_grad, WU, preferred_element_type=F32)
    context_grad = jnp.einsum("to,io->ti", G, w_dense, preferred_element_type=F32).astype(BF)
    context_grad = context_grad.reshape(length, heads, HEAD_DIM)
    prob_grad = jnp.einsum("qhd,khd->hqk", context_grad, values, preferred_element_type=F32)
    weighted = jnp.sum(probs * prob_grad, axis=-1, keepdims=True)
    score_grad = (probs * (prob_grad - weighted)).astype(BF)
    query_grad = jnp.einsum("hqk,khd->qhd", score_grad, keys, preferred_element_type=F32) * scale
    key_grad = jnp.einsum("hqk,qhd->khd", score_grad, query, preferred_element_type=F32) * scale
    value_grad = jnp.einsum("hqk,qhd->khd", low, context_grad, preferred_element_type=F32)
    rotated_grad = jnp.stack([query_grad, key_grad, value_grad], axis=2).astype(BF).astype(F32)
    packed_grad = rotate(rotated_grad, positions, -1.0).reshape(length, -1).astype(BF)
    qkv_bias_grad = jnp.sum(packed_grad.astype(F32), axis=0)
    qkv_grad = jnp.einsum("ti,tj->ij", norm_one, packed_grad, preferred_element_type=F32)
    norm_one_grad = jnp.einsum("tj,ij->ti", packed_grad, WQ, preferred_element_type=F32)
    u = norm_one_grad * gain_one + norm_two_grad * gain_two
    mean_u = jnp.mean(u, axis=-1, keepdims=True)
    mean_ux = jnp.mean(u * xhat, axis=-1, keepdims=True)
    dx = inverse * (u - mean_u - xhat * mean_ux)
    sums = jnp.stack(
        [
            jnp.sum(norm_one_grad * xhat, axis=0),
            jnp.sum(norm_one_grad, axis=0),
            jnp.sum(norm_two_grad * xhat, axis=0),
            jnp.sum(norm_two_grad, axis=0),
        ]
    )
    return (
        out.astype(BF),
        dx.astype(BF),
        sums,
        up_bias_grad,
        qkv_bias_grad,
        up_grad.astype(BF),
        qkv_grad.astype(BF),
        down_grad.astype(BF),
        dense_grad.astype(BF),
    )


NN = (((1,), (0,)), ((), ()))
NT = (((1,), (1,)), ((), ()))
TN = (((0,), (0,)), ((), ()))
ROOT_HALF = 0.7071067811865476
PDF_SCALE = 0.3989422804014327


def dot(left, right, dims=NN):
    return lax.dot_general(left, right, dims, preferred_element_type=F32)


def rotary_tables(length):
    half = ROT_DIM // 2
    freqs = 10000.0 ** (-jnp.arange(half, dtype=F32) * 2.0 / ROT_DIM)
    angles = jnp.arange(length, dtype=jnp.int32).astype(F32)[:, None] * freqs[None, :]
    cosine, sine = jnp.cos(angles), jnp.sin(angles)
    rest = HEAD_DIM - ROT_DIM
    keep, none, gap = jnp.ones((length, rest)), jnp.zeros((length, rest)), jnp.zeros_like(sine)
    same = jnp.concatenate([cosine, cosine, keep] * 2, axis=1)
    up = jnp.concatenate([-sine, gap, none] * 2, axis=1)
    down = jnp.concatenate([gap, sine, none] * 2, axis=1)
    return jnp.stack([same, up, down]).astype(F32)


class Layer:
    def __init__(self, rows, refs):
        self.rows = rows
        for name, ref in refs.items():
            setattr(self, name, ref)
        self.length, self.width = self.X.shape
        self.heads = self.Q.shape[0]
        self.block = min(256, self.length)

    def at(self, j, rows=None, part=0):
        rows = rows or self.rows
        return pl.ds(pl.multiple_of(j * self.rows + part * rows, rows), rows)

    def norm(self, j):
        step = 64

        @pl.loop(0, self.rows // step)
        def _(i):
            at = self.at(j, step, i)
            x = self.X[at].astype(F32)
            average = jnp.mean(x, axis=-1, keepdims=True)
            centered = x - average
            variance = jnp.mean(centered * centered, axis=-1, keepdims=True)
            inverse = lax.rsqrt(variance + epsilon)
            xhat = centered * inverse
            self.STAT[at, 0:1] = average
            self.STAT[at, 1:2] = inverse
            self.N1[at] = (xhat * self.VEC[0:1] + self.VEC[1:2]).astype(BF)
            self.N2[at] = (xhat * self.VEC[2:3] + self.VEC[3:4]).astype(BF)

    def turn(self, values, at, kind, sign):
        lanes = lax.broadcasted_iota(jnp.int32, values.shape, 1)
        turned = values * self.ROT[0, at] + sign * (
            pltpu.roll(values, 128 - ROT_DIM // 2, 1) * self.ROT[1, at]
            + pltpu.roll(values, ROT_DIM // 2, 1) * self.ROT[2, at]
        )
        if kind == 0:
            return turned
        return jnp.where((lanes >= HEAD_DIM) if kind == 1 else (lanes < HEAD_DIM), turned, values)

    def qkv(self, j):
        at = self.at(j)
        scale = HEAD_DIM ** (-0.5)
        packed = dot(self.N1[at], self.WQ[...])
        bias = self.BQ[...]
        places = [(self.Q, scale, None), (self.K, None, self.KT), (self.V, None, self.VT)]
        for t in range(packed.shape[1] // 128):
            cols = slice(t * 128, t * 128 + 128)
            low = self.turn(packed[:, cols] + bias[:, cols], at, t % 3, 1.0).astype(BF)
            across = low.T
            for side in range(2):
                index = 2 * t + side
                ref, factor, turned = places[index % 3]
                half = slice(side * HEAD_DIM, side * HEAD_DIM + HEAD_DIM)
                value = low[:, half]
                ref[index // 3, at] = value if factor is None else value * jnp.asarray(factor, BF)
                if turned is not None:
                    turned[index // 3, :, at] = across[half]

    def up(self, j):
        at = self.at(j)
        tile = 256

        for i in range(self.WU.shape[1] // tile):
            cols = slice(i * tile, i * tile + tile)
            hidden = dot(self.N2[at], self.WU[:, cols]) + self.BU[:, cols]
            cdf = 0.5 + 0.5 * lax.erf(hidden * ROOT_HALF)
            self.ACT[at, cols] = (hidden * cdf).astype(BF)
            pdf = PDF_SCALE * jnp.exp(-0.5 * hidden * hidden)
            self.DG[at, cols] = cdf + hidden * pdf

    def down(self, j):
        at = self.at(j)
        self.ACC[at] = dot(self.ACT[at], self.WDN[...])

    def masked(self, scores):
        rows = lax.broadcasted_iota(jnp.int32, scores.shape, 0)
        cols = lax.broadcasted_iota(jnp.int32, scores.shape, 1)
        return jnp.where(rows <= cols, scores, mask_fill)

    def attend_block(self, m, qb):
        size = self.block
        mine, before = slice(qb * size, qb * size + size), slice(0, qb * size)
        sides = []
        for side in range(2):
            h = 2 * m + side
            q = self.Q[h, mine]
            near = self.masked(dot(self.K[h, mine], q, NT))
            top = jnp.max(near, axis=0, keepdims=True)
            if qb:
                far = dot(self.K[h, before], q, NT)
                top = jnp.maximum(top, jnp.max(far, axis=0, keepdims=True))
            near = jnp.exp(near - top)
            total = jnp.sum(near, axis=0, keepdims=True)
            if qb:
                far = jnp.exp(far - top)
                total = total + jnp.sum(far, axis=0, keepdims=True)
            inverse = 1.0 / total
            self.LSE[h, :, mine] = top + jnp.log(total)
            context = dot(self.VT[h, :, mine], (near * inverse).astype(BF))
            if qb:
                context = context + dot(self.VT[h, :, before], (far * inverse).astype(BF))
            sides.append(context.astype(BF))
        self.CTX[m, mine] = jnp.concatenate(sides, axis=0).T

    def attend_part(self, qb):
        @pl.loop(0, self.heads // 2)
        def _(m):
            self.attend_block(m, qb)

    def out(self, j):
        at = self.at(j)
        total = self.ACC[at]
        for m in range(self.heads // 2):
            total = total + dot(self.CTX[m, at], self.WDE[m * 128 : m * 128 + 128])
        self.OP[at] = total.astype(BF)

    def mlp_back(self, j):
        at = self.at(j)
        tile = 256

        for i in range(self.WU.shape[1] // tile):
            cols = slice(i * tile, i * tile + tile)
            active_grad = dot(self.G[at], self.WDN[cols], NT)
            self.HG[at, cols] = (active_grad * self.DG[at, cols]).astype(BF)

        self.ACC[at] = dot(self.HG[at], self.WU[...], NT)

    def context_grad(self, j):
        at = self.at(j)
        for m in range(self.heads // 2):
            self.DO[m, at] = dot(self.G[at], self.WDE[m * 128 : m * 128 + 128], NT).astype(BF)

    def back_block(self, m, qb):
        size = self.block
        mine, before = slice(qb * size, qb * size + size), slice(0, qb * size)
        scale = HEAD_DIM ** (-0.5)
        upstream = self.DO[m, mine]
        values, keys, queries, values_before, keys_before = [], [], [], [], []
        for side in range(2):
            h = 2 * m + side
            q = self.Q[h, mine]
            do = upstream[:, side * HEAD_DIM : side * HEAD_DIM + HEAD_DIM]
            lse = self.LSE[h, :, mine]
            near = jnp.exp(self.masked(dot(self.K[h, mine], q, NT)) - lse)
            near_grad = dot(self.V[h, mine], do, NT)
            weighted = jnp.sum(near * near_grad, axis=0, keepdims=True)
            if qb:
                far = jnp.exp(dot(self.K[h, before], q, NT) - lse)
                far_grad = dot(self.V[h, before], do, NT)
                weighted = weighted + jnp.sum(far * far_grad, axis=0, keepdims=True)
            values.append(dot(near.astype(BF), do))
            score = (near * (near_grad - weighted)).astype(BF)
            keys.append(dot(score, q))
            query = dot(self.KT[h, :, mine], score)
            if qb:
                values_before.append(dot(far.astype(BF), do))
                score = (far * (far_grad - weighted)).astype(BF)
                keys_before.append(dot(score, q))
                query = query + dot(self.KT[h, :, before], score)
            queries.append((query * scale).astype(BF))
        self.DV[m, mine] += jnp.concatenate(values, axis=1)
        self.DK[m, mine] += jnp.concatenate(keys, axis=1)
        self.DQ[m, mine] = jnp.concatenate(queries, axis=0).T
        if qb:
            self.DV[m, before] += jnp.concatenate(values_before, axis=1)
            self.DK[m, before] += jnp.concatenate(keys_before, axis=1)

    def attend_back(self, j, m):
        for qb in range(self.length // self.block):

            @pl.when(j == qb)
            def _():
                self.back_block(m, qb)

    def unturn(self, j):
        at = self.at(j)
        for m in range(self.heads // 2):
            q = self.DQ[m, at].astype(F32)
            k = pltpu.roll(self.DK[m, at], HEAD_DIM, 1).astype(BF).astype(F32)
            v = self.DV[m, at].astype(BF).astype(F32)
            left = lax.broadcasted_iota(jnp.int32, q.shape, 1) < HEAD_DIM
            for kind, pair in enumerate(((q, k), (v, q), (k, v))):
                both = jnp.where(left, *pair)
                cols = slice((3 * m + kind) * 128, (3 * m + kind) * 128 + 128)
                self.PG[at, cols] = self.turn(both, at, kind, -1.0).astype(BF)

    def zero_sums(self):
        self.SUMS[...] = jnp.zeros_like(self.SUMS)
        self.COLS[...] = jnp.zeros_like(self.COLS)
        self.DK[...] = jnp.zeros_like(self.DK)
        self.DV[...] = jnp.zeros_like(self.DV)
        self.BUG[...] = jnp.zeros_like(self.BUG)
        self.BQG[...] = jnp.zeros_like(self.BQG)

    def input_back(self, j):
        self.TMP[...] = dot(self.PG[self.at(j)], self.WQ[...], NT)
        ones = jnp.ones((8, self.rows), BF)
        self.BQG[...] += dot(ones, self.PG[self.at(j)])[0:1]
        self.BUG[...] += dot(ones, self.HG[self.at(j)])[0:1]
        step = 32

        @pl.loop(0, self.rows // step)
        def _(i):
            at = self.at(j, step, i)
            here = pl.ds(pl.multiple_of(i * step, step), step)
            inverse = self.STAT[at, 1:2]
            xhat = (self.X[at].astype(F32) - self.STAT[at, 0:1]) * inverse
            one, two = self.TMP[here], self.ACC[at]
            u = one * self.VEC[0:1] + two * self.VEC[2:3]
            mean_u = jnp.mean(u, axis=-1, keepdims=True)
            mean_ux = jnp.mean(u * xhat, axis=-1, keepdims=True)
            self.DX[at] = (inverse * (u - mean_u - xhat * mean_ux)).astype(BF)
            for row, value in enumerate((one * xhat, one, two * xhat, two)):
                folded = value[0:8]
                for r in range(8, step, 8):
                    folded = folded + value[r : r + 8]
                self.COLS[row] += folded

    def fold_sums(self):
        for row in range(4):
            self.SUMS[row : row + 1] = jnp.sum(self.COLS[row], axis=0, keepdims=True)

    def weight_grad(self, left, right, put, at):
        tile = 256

        @pl.loop(0, left.shape[1] // tile)
        def _(i):
            cols = pl.ds(pl.multiple_of(i * tile, tile), tile)
            put(i, dot(left[at, cols], right[at], TN))

    def down_grad(self, put, at, core, half_done):
        tile = 256
        count = self.ACT.shape[1] // tile

        @pl.loop(0, count)
        def _(k):
            i = lax.rem(k + (1 - core) * (count // 2), count)
            cols = pl.ds(pl.multiple_of(i * tile, tile), tile)
            put(i, dot(self.ACT[at, cols], self.G[at], TN))

            @pl.when(k == count // 2 - 1)
            def _():
                half_done()

    def up_grad(self, put, at):
        self.weight_grad(self.N2, self.HG, put, at)

    def qkv_grad(self, put):
        self.weight_grad(self.N1, self.PG, put, slice(0, self.length))

    def dense_grad(self, put, at):
        for m in range(self.heads // 2):
            put(m, dot(self.CTX[m, at], self.G[at], TN))


def layer_scratch(length, width, heads, hidden):
    vm = pltpu.VMEM
    pairs, packed = heads // 2, heads * 3 * HEAD_DIM
    return dict(
        STAT=vm((length, 2), F32),
        N1=vm((length, width), BF),
        N2=vm((length, width), BF),
        Q=vm((heads, length, HEAD_DIM), BF),
        K=vm((heads, length, HEAD_DIM), BF),
        V=vm((heads, length, HEAD_DIM), BF),
        ACT=vm((length, hidden), BF),
        DG=vm((length, hidden), F32),
        ACC=vm((length, width), F32),
        LSE=vm((heads, 1, length), F32),
        KT=vm((heads, HEAD_DIM, length), BF),
        VT=vm((heads, HEAD_DIM, length), BF),
        CTX=vm((pairs, length, 2 * HEAD_DIM), BF),
        DO=vm((pairs, length, 2 * HEAD_DIM), BF),
        HG=vm((length, hidden), BF),
        DQ=vm((pairs, length, 2 * HEAD_DIM), BF),
        DK=vm((pairs, length, 2 * HEAD_DIM), F32),
        DV=vm((pairs, length, 2 * HEAD_DIM), F32),
        PG=vm((length, packed), BF),
    )


class LineReduce:
    def __init__(self, me, part, got, ssem, rsem):
        self.me, self.part, self.got, self.ssem, self.rsem = me, part, got, ssem, rsem
        self.parts, self.rows = got.shape[1:3]

    def copy(self, j, p, way):
        me = self.me
        to = jnp.minimum(me.z + 1, me.n - 1) if way == 0 else jnp.maximum(me.z - 1, 0)
        slot = j if way == 0 else jnp.where(j == to, me.n, j)
        return send(
            rows_at(self.part, (j * self.parts + p) * self.rows, self.rows),
            self.got.at[slot, p],
            self.ssem.at[j, p],
            self.rsem.at[slot, p],
            (me.d, to),
        )

    def came(self, slot, p):
        me = self.me
        got = self.got.at[slot, p]
        return send(got, got, self.ssem.at[0, p], self.rsem.at[slot, p], (me.d, me.z))

    def start(self, j, which=None):
        me = self.me
        for p in range(self.parts) if which is None else which:

            @pl.when((me.z == 0) & (j > 0))
            def _():
                self.copy(j, p, 0).start()

            @pl.when((me.z == me.n - 1) & (j < me.n - 1))
            def _():
                self.copy(j, p, 1).start()

    def add(self, j, p):
        step = 64

        @pl.loop(0, self.rows // step)
        def _(i):
            mine = pl.ds(pl.multiple_of((j * self.parts + p) * self.rows + i * step, step), step)
            here = pl.ds(pl.multiple_of(i * step, step), step)
            self.part[mine] = (
                self.part[mine].astype(F32) + self.got[j, p, here].astype(F32)
            ).astype(BF)

    def step(self, t, which=None):
        me = self.me
        n = me.n
        for p in range(self.parts) if which is None else which:
            for way, e in ((0, t - me.z), (1, t - (n - 1 - me.z))):
                j = n - 1 - e if way == 0 else e
                valid = (me.z > 0) & (me.z < n - 1) & (e >= 0)
                valid = valid & ((j > me.z) if way == 0 else (j < me.z))

                @pl.when(valid)
                def _():
                    self.came(j, p).wait_recv()
                    self.add(j, p)
                    self.copy(j, p, way).start()

    def total(self, base, extra, result, tmp):
        me = self.me
        step = 64
        for p in range(self.parts):

            @pl.when(me.z > 0)
            def _():
                self.came(me.z, p).wait_recv()

            @pl.when(me.z < me.n - 1)
            def _():
                self.came(me.n, p).wait_recv()

            @pl.loop(0, self.rows // step)
            def _(i):
                at = p * self.rows + i * step
                here = pl.ds(pl.multiple_of(i * step, step), step)
                there = pl.ds(pl.multiple_of(at, step), step)
                mine = pl.ds(pl.multiple_of(me.z * self.parts * self.rows + at, step), step)
                tmp[here] = base[mine].astype(F32) + self.part[mine].astype(F32)
                if extra is not None:
                    tmp[here] += extra

                @pl.when(me.z > 0)
                def _():
                    tmp[here] += self.got[me.z, p, here].astype(F32)

                @pl.when(me.z < me.n - 1)
                def _():
                    tmp[here] += self.got[me.n, p, here].astype(F32)

                result[there] = tmp[here].astype(BF)

    def finish(self):
        me = self.me
        for j in range(me.n):
            for p in range(self.parts):

                @pl.when((j > me.z) & (me.z < me.n - 1))
                def _():
                    self.copy(j, p, 0).wait_send()

                @pl.when((j < me.z) & (me.z > 0))
                def _():
                    self.copy(j, p, 1).wait_send()


def nearest(n):
    return [sorted(range(n), key=lambda j: abs(j - z)) for z in range(n)]


def pick(table, z, k):
    value = jnp.int32(0)
    for at, row in enumerate(table):
        for index, entry in enumerate(row):
            if entry:
                value = jnp.where((z == at) & (k == index), entry, value)
    return value


VECTORS = 6


def layer_kernel(n, data, chunks, names, *refs):
    refs = list(refs)

    def take(count):
        got = refs[:count]
        del refs[:count]
        return got

    vectors = take(VECTORS)
    x, g, wq, wu, wde, wdn, rot, bq, bu = take(9)
    out, dx, small, fu, fq, fdn, fde = take(7)
    ins = dict(zip(names, take(len(names))))
    rows = out.shape[0]
    layer = Layer(rows, ins)
    me = Place(n, data)
    SM, sm = take(2)
    layer.DX = layer.ACT
    lsem, ss, sr, xs, xr, gs, gr = take(7)
    cq, cu = ColumnGather(me, wq, layer.WQ, take(5)), ColumnGather(me, wu, layer.WU, take(5))
    og, xg, os, orr, ds, dr = take(6)
    v1, v1g, v1s, v1r, v2m, v2g, v2s, v2r = take(8)
    reduces = []
    for unused in range(4):
        reduces.append(take_reduce(me, take(1)[0], take))
    red_dn, red_de, red_u, red_q = reduces
    shares = [GradShare(me, final, take(6)) for final in (fdn, fde, fu, fq)]
    share_dn, share_de, share_u, share_q = shares
    back_u = RowsBack(me, red_u.total, fu, *take(3))
    back_q = RowsBack(me, red_q.total, fq, *take(3))
    (dsem,) = take(1)
    assert not refs
    lx = LineGather(me, x, layer.X, rows, chunks, xs, xr)
    lg = LineGather(me, g, layer.G, rows, chunks, gs, gr)
    ro = LineReduce(me, layer.OP, og, os, orr)
    rx = LineReduce(me, layer.ACT, xg, ds, dr)
    near = nearest(n)
    far = [list(range(n - 1, -1, -1)) if 2 * z < n else list(range(n)) for z in range(n)]
    depth = wq.shape[0]
    part = depth

    own = [
        pltpu.make_async_copy(x, rows_at(layer.X, me.z * rows, rows), lsem.at[0]),
        pltpu.make_async_copy(g, rows_at(layer.G, me.z * rows, rows), lsem.at[1]),
        pltpu.make_async_copy(
            block_at(wq, 0, depth, me.z * layer.WQ.shape[1], layer.WQ.shape[1]),
            rows_at(layer.WQ, me.z * depth, depth),
            lsem.at[2],
        ),
        pltpu.make_async_copy(
            block_at(wu, 0, depth, me.z * layer.WU.shape[1], layer.WU.shape[1]),
            rows_at(layer.WU, me.z * depth, depth),
            lsem.at[3],
        ),
    ]
    own += [
        pltpu.make_async_copy(source, place, lsem.at[4 + i])
        for i, (source, place) in enumerate(
            ((wde, layer.WDE), (wdn, layer.WDN), (rot, layer.ROT))
        )
    ]
    me.greet()
    for copy in own:
        copy.start()
    sm[...] = jnp.zeros_like(sm)
    for i, vector in enumerate(vectors):
        sm[i] = vector[...].astype(F32)
    layer.BQ[0] = bq[...].astype(F32)
    layer.BU[0] = bu[...].astype(F32)
    me.met()

    def tiny(k, slot):
        return send(sm, SM.at[slot], ss.at[k], sr.at[slot], me.seq_peer(k)[1])

    for k in range(1, n):
        tiny(k, me.z).start()
    cq.start()
    cu.start()
    lx.start()
    SM[me.z] = sm[...]
    layer.zero_sums()
    for k in range(1, n):
        tiny(k, me.seq_peer(k)[0]).wait_recv()
    for i in range(n):
        layer.VEC[:, i * part : i * part + part] = SM[i]
    near_k = sorted({1, n - 1})
    for k in near_k:
        cq.share(k)
        cu.share(k)
    lx.forward(1)
    for k in range(1, n):
        if k not in near_k:
            cq.share(k)
            cu.share(k)
    for s in range(2, n - 1):
        lx.forward(s)
    lg.start()
    own[0].wait()
    layer.norm(me.z)
    for k in range(1, n):
        cq.hand(k)
        cu.hand(k)
    for i in (2, 3, 4, 5, 6):
        own[i].wait()
    cq.finish()
    cu.finish()

    @pl.loop(0, n)
    def _(k):
        j = pick(near, me.z, k)

        @pl.when(k > 0)
        def _():
            lx.arrive(j)
            layer.norm(j)

        layer.qkv(j)
        layer.up(j)
        layer.down(j)

    lg.forward(1)
    blocks = layer.length // layer.block
    for qb in range(blocks):
        layer.attend_part(qb)

    @pl.loop(0, n)
    def _(k):
        j = pick(far, me.z, k)
        layer.out(j)
        ro.start(j)

    for s in range(2, n - 1):
        lg.forward(s)

    own[1].wait()
    layer.SUMS[4:5] = jnp.sum(layer.G[layer.at(me.z)].astype(F32), axis=0, keepdims=True)

    def put(red):
        def store(i, value):
            parts, unused, rp, cols = red.part.shape
            pieces = value.shape[0] // rp
            value = value.reshape(pieces, rp, cols)
            at = (0, pl.ds(i * pieces, pieces)) if parts == 1 else (i,)
            red.part[at] = value.astype(BF)

        return store

    pairs = layer.heads // 2
    every = slice(0, layer.length)

    @pl.loop(0, n)
    def _(k):
        j = pick(near, me.z, k)
        lg.arrive(j)

        @pl.when(k == n - 1)
        def _():
            layer.down_grad(put(red_dn), every, me.c, red_dn.start)
            layer.dense_grad(put(red_de), every)
            red_de.start()
            red_dn.chip_sums()

        layer.mlp_back(j)
        layer.context_grad(j)

        @pl.when(k == n - 1)
        def _():
            red_de.chip_sums()
            layer.up_grad(put(red_u), every)
            red_u.start()

        @pl.loop(0, pairs)
        def _(m):
            layer.attend_back(j, m)

            @pl.when((k == n - 1) & (m == 0))
            def _():
                red_u.chip_sums()
                red_dn.pair_sums()

        @pl.when(k == n - 2)
        def _():
            ro.step(1)

    for t in range(2, 2 * n - 5):
        ro.step(t)
    red_de.pair_sums()
    copies = [
        pltpu.make_async_copy(red.total.at[0], final.at[me.piece], dsem.at[i])
        for i, (red, final) in enumerate(((red_dn, fdn), (red_de, fde)))
    ]

    @pl.loop(0, n)
    def _(j):
        layer.unturn(j)

    layer.qkv_grad(put(red_q))
    red_q.start()

    @pl.loop(0, n)
    def _(k):
        j = pick(far, me.z, k)
        layer.input_back(j)

        @pl.when(k == 0)
        def _():
            rx.start(j)
            red_u.pair_sums()
            red_q.chip_sums()
            red_dn.sum_up()
            red_de.sum_up()
            for copy in copies:
                copy.start()

        @pl.when(k == 1)
        def _():
            red_u.sum_up()
            back_u.start()
            rx.start(j, (0,))

        @pl.when(k == n - 2)
        def _():
            red_q.pair_sums()
            share_dn.start(red_dn.total.at[0])
            share_de.start(red_de.total.at[0])

    rx.start(pick(far, me.z, 1), (1,))
    layer.fold_sums()
    cs = part
    v1[...] = layer.SUMS[...]

    def small_z(k, slot):
        other, to = me.seq_peer(k)
        return send(
            v1.at[:, pl.ds(pl.multiple_of(other * cs, cs), cs)],
            v1g.at[slot],
            v1s.at[k],
            v1r.at[slot],
            to,
        )

    def small_dp(k, slot):
        return send(v2m, v2g.at[slot], v2s.at[k], v2r.at[slot], me.dp_peer(k)[1])

    for k in range(1, n):
        small_z(k, me.z).start()
    rx.step(1, (0,))
    back_u.wait()
    share_u.start()
    rx.step(1, (1,))
    red_q.sum_up()
    back_q.start()
    share_dn.forward()
    share_de.forward()
    for k in range(2, n - 1):
        rx.start(pick(far, me.z, k))
    ro.total(layer.X, layer.VEC[4:5] + layer.VEC[5:6], out, layer.TMP)
    back_q.wait()
    share_q.start()
    for t in range(2, 2 * n - 5):
        rx.step(t)
    for copy in copies:
        copy.wait()
    share_dn.hand()
    share_de.hand()
    for k in range(1, n):
        small_z(k, me.seq_peer(k)[0]).wait_recv()
    v1g[me.z] = v1[:, pl.ds(pl.multiple_of(me.z * cs, cs), cs)]
    total = v1g[0]
    for k in range(1, n):
        total = total + v1g[k]
    v2m[...] = jnp.zeros_like(v2m)
    v2m[0:8] = total
    for i in range(layer.BUG.shape[1] // cs):
        v2m[8 + i : 9 + i] = layer.BUG[:, i * cs : i * cs + cs]
    for i in range(layer.BQG.shape[1] // cs):
        v2m[12 + i : 13 + i] = layer.BQG[:, i * cs : i * cs + cs]
    for k in range(1, data):
        small_dp(k, me.d).start()
    share_u.forward()
    for k in range(1, data):
        small_dp(k, me.dp_peer(k)[0]).wait_recv()
    v2g[me.d] = v2m[...]

    def add(i, acc):
        return acc + v2g[i]

    small[...] = lax.fori_loop(1, data, add, v2g[0])
    share_q.forward()
    share_u.hand()
    share_q.hand()
    rx.total(layer.G, None, dx, layer.TMP)
    ro.finish()
    rx.finish()
    lx.finish()
    lg.finish()
    for k in range(1, n):
        tiny(k, me.z).wait_send()
        small_z(k, me.z).wait_send()
    for k in range(1, data):
        small_dp(k, me.d).wait_send()
    for red in reduces:
        red.finish()
    for share in shares:
        share.finish()
    back_u.finish()
    back_q.finish()


def rotary_constant(length):
    half = ROT_DIM // 2
    freqs = np.float32(10000.0) ** (-np.arange(half, dtype=np.float32) * np.float32(2.0 / ROT_DIM))
    angles = np.arange(length, dtype=np.float32)[:, None] * freqs.astype(np.float32)[None, :]
    cosine, sine = np.cos(angles), np.sin(angles)
    rest = HEAD_DIM - ROT_DIM
    keep, none, gap = np.ones((length, rest)), np.zeros((length, rest)), np.zeros_like(sine)
    same = np.concatenate([cosine, cosine, keep] * 2, axis=1)
    up = np.concatenate([-sine, gap, none] * 2, axis=1)
    down = np.concatenate([gap, sine, none] * 2, axis=1)
    return np.stack([same, up, down]).astype(np.float32)


def whole_layer(n, data, vectors, x, g, wq, wu, w_dense, w_down, b_qkv, b_up):
    rows, width = x.shape
    length = n * rows
    packed, hidden = wq.shape[1] // n, wu.shape[1] // n
    heads = packed // (3 * HEAD_DIM)
    depth = wq.shape[0]
    chunks = 4
    groups = data // PLANE
    vm = pl.BlockSpec(memory_space=pltpu.VMEM)
    hbm = pl.BlockSpec(memory_space=pl.ANY)
    dma = pltpu.SemaphoreType.DMA
    sds = jax.ShapeDtypeStruct
    mem = pltpu.VMEM
    named = layer_scratch(length, width, heads, hidden)
    named.update(
        X=mem((length, width), BF),
        G=mem((length, width), BF),
        WQ=mem((width, packed), BF),
        WU=mem((width, hidden), BF),
        VEC=mem((8, width), F32),
        WDE=mem(w_dense.shape, BF),
        WDN=mem(w_down.shape, BF),
        ROT=mem((3, length, 128), F32),
        OP=mem((length, width), BF),
        SUMS=mem((8, width), F32),
        BUG=mem((1, hidden), F32),
        BQG=mem((1, packed), F32),
        BQ=mem((1, packed), F32),
        BU=mem((1, hidden), F32),
        TMP=mem((rows, width), F32),
        COLS=mem((4, 8, width), F32),
    )
    scratch = list(named.values())
    scratch += [mem((n, 8, depth), F32), mem((8, depth), F32)]
    scratch += [dma((7,)), dma((n,)), dma((n,))]
    scratch += [dma((2, n, chunks)), dma((n, chunks))] * 2
    scratch += column_sems(n) + column_sems(n)
    scratch += [mem((n + 1, 2, rows // 2, width), BF)] * 2
    scratch += [dma((n, 2)), dma((n + 1, 2))] * 2
    scratch += [mem((8, width), F32), mem((n, 8, depth), F32), dma((n,)), dma((n,))]
    scratch += [mem((16, depth), F32), mem((data, 16, depth), F32), dma((data,)), dma((data,))]
    shapes = [
        (1, hidden // PLANE, width),
        (1, packed // 3 // PLANE, width),
        (n, depth // PLANE, hidden),
        (n, depth // PLANE, packed),
    ]
    for m, rp, cols in shapes:
        scratch += [mem((m, PLANE, rp, cols), BF)] + reduce_scratch(m, rp, cols, groups)
    for unused in range(4):
        scratch += share_sems()
    scratch += [dma((n,)), dma((n,)), dma] * 2
    scratch += [dma((4,))]
    outs = [
        sds((rows, width), BF),
        sds((rows, width), BF),
        sds((16, depth), F32),
        sds((PLANE, depth // PLANE, hidden * n), BF),
        sds((PLANE, depth // PLANE, packed * n), BF),
        sds((PLANE, hidden // PLANE, width), BF),
        sds((PLANE, packed // 3 // PLANE, width), BF),
    ]
    return pl.pallas_call(
        functools.partial(layer_kernel, n, data, chunks, list(named)),
        out_shape=outs,
        in_specs=[vm] * VECTORS + [hbm] * 7 + [vm] * 2,
        out_specs=[vm] * 3 + [hbm] * 4,
        scratch_shapes=scratch,
        compiler_params=pltpu.CompilerParams(
            collective_id=2, has_side_effects=True, vmem_limit_bytes=67043328
        ),
        name="layer",
    )(*vectors, x, g, wq, wu, w_dense, w_down, rotary_constant(length), b_qkv, b_up)


def fits(n, data, tokens, qkv, up):
    unused, rows, width = tokens
    length, depth = n * rows, qkv[0]
    return (
        length * (width + up[1] // n) <= 1024 * 2048
        and rows == 256
        and depth == 256
        and up[1] // n == width
        and up[1] // n % 256 == 0
        and qkv[1] // n % (6 * HEAD_DIM) == 0
    )


def per_device(
    n,
    data,
    layer_input,
    attn_gain,
    attn_shift,
    mlp_gain,
    mlp_shift,
    qkv_weight,
    qkv_bias,
    dense_weight,
    dense_bias,
    up_weight,
    up_bias,
    down_weight,
    down_bias,
    out_grad,
):
    unused, rows, width = layer_input.shape
    x = layer_input.reshape(rows, width)
    g = out_grad.reshape(rows, width)
    part = width // n
    if fits(n, data, layer_input.shape, qkv_weight.shape, up_weight.shape):
        vectors = (attn_gain, attn_shift, mlp_gain, mlp_shift, dense_bias, down_bias)
        out, dx, tiny, fu, fq, fdn, fde = whole_layer(
            n, data, vectors, x, g, qkv_weight, up_weight, dense_weight, down_weight,
            qkv_bias, up_bias,
        )
    else:
        small = jnp.stack(
            [attn_gain, attn_shift, mlp_gain, mlp_shift, dense_bias, down_bias] + [attn_gain] * 2
        ).astype(F32)
        SM, X, G, WQ, WU = gather(n, data, small, x, g, qkv_weight, up_weight)
        vectors = jnp.swapaxes(SM, 0, 1).reshape(8, width)
        bias = (vectors[4] + vectors[5])[None]
        OP, DX, sums, bu, bq, UG, QG, DnG, DeG = middle(
            X, G, WQ, WU, dense_weight, down_weight, qkv_bias, up_bias, vectors
        )
        v1 = jnp.concatenate(
            [sums, jnp.sum(g.astype(F32), axis=0)[None], jnp.zeros((3, width), F32)], axis=0
        )
        v2 = jnp.concatenate(
            [bu.reshape(4, part), bq.reshape(3, part), jnp.zeros((1, part), F32)]
        )
        out, dx, tiny, fu, fq, fdn, fde = reduce_all(
            n, data, OP, DX, v1, v2, bias, x, g, UG, QG, DnG, DeG
        )
    results = finish(part, out, dx, tiny, fu, fq, fdn, fde)
    return tuple(r.reshape(layer_input.shape) for r in results[:2]) + tuple(results[2:])


def finish_kernel(part, out, dx, tiny, fu, fq, fdn, fde, *results):
    (o_out, o_dx, ag, ash, mg, ms, gq, bq, gde, bde, gu, bu, gdn, bdn) = results
    o_out[...] = out[...]
    o_dx[...] = dx[...]
    for source, result in ((fq, gq), (fde, gde), (fu, gu), (fdn, gdn)):
        result[...] = source[...].astype(F32)

    @pl.when(pl.program_id(0) == 0)
    def _():
        for row, result in enumerate((ag, ash, mg, ms, bde)):
            result[...] = tiny[row]
        bdn[...] = tiny[4]
        for base, result in ((8, bu), (12, bq)):
            for i in range(result.shape[0] // part):
                result[i * part : i * part + part] = tiny[base + i]


def finish(part, out, dx, tiny, fu, fq, fdn, fde):
    steps = 4
    sds = jax.ShapeDtypeStruct

    def tile(rows, cols):
        return pl.BlockSpec((rows // steps, cols), lambda i: (i, 0))

    def line(size):
        return sds((size,), F32), pl.BlockSpec((size,), lambda i: (0,))

    wide = [a.reshape(-1, a.shape[-1]) for a in (fu, fq, fdn, fde)]
    gu, gq, gdn, gde = ((sds(a.shape, F32), tile(*a.shape)) for a in wide)
    tokens = (sds(out.shape, BF), tile(*out.shape))
    vector = line(part)
    shapes, specs = zip(
        tokens, tokens, vector, vector, vector, vector, gq, line(fq.shape[-1] // (fu.shape[-1] // gdn[0].shape[0])),
        gde, vector, gu, line(gdn[0].shape[0]), gdn, vector,
    )
    return pl.pallas_call(
        functools.partial(finish_kernel, part),
        grid=(steps,),
        out_shape=shapes,
        in_specs=[tile(*out.shape), tile(*out.shape), pl.BlockSpec(tiny.shape, lambda i: (0, 0))]
        + [tile(*a.shape) for a in wide],
        out_specs=specs,
        compiler_params=pltpu.CompilerParams(vmem_limit_bytes=63 << 20),
        name="finish",
    )(out, dx, tiny, *wide)


def solution(mesh):
    tokens, row, vector = P("dp", "seq", None), P("seq", None), P("seq")
    in_specs = (tokens,) + (vector,) * 4 + (row, vector) * 4 + (tokens,)
    out_specs = (tokens, tokens) + (vector,) * 4 + (row, vector) * 4
    return jax.shard_map(
        functools.partial(per_device, mesh.shape["seq"], mesh.shape["dp"]),
        mesh=mesh,
        in_specs=in_specs,
        out_specs=out_specs,
        check_vma=False,
    )
```
